32 devices in a mesh: section: 2 (over x), dp: 16 (over z, y, core).
Axes of the slice: x: 2, y: 2, z: 4, core: 2. Of those that a mesh axis runs over, the one named last changes fastest.
Arguments:
- inputs_long: bfloat16 [2, 16, 640, 768], P('section', 'dp'), may hold values from -6 to 6
- inputs_short: bfloat16 [2, 16, 256, 768], P('section', 'dp'), may hold values from -6 to 6
- cotangent_long: bfloat16 [2, 16, 640, 768], P('section', 'dp'), may hold values from -6 to 6
- cotangent_short: bfloat16 [2, 16, 256, 768], P('section', 'dp'), may hold values from -6 to 6
- lengths_long: int32 [2, 16], P(None, 'dp'), may hold values from 1 to 640, 7680 in all within a row
- lengths_short: int32 [2, 16], P(None, 'dp'), may hold values from 1 to 256, 3072 in all within a row
- self_in_weight: bfloat16 [2, 768, 2304], P('section'), may hold values from -0.3125 to 0.3125
- self_out_weight: bfloat16 [2, 768, 768], P('section'), may hold values from -0.625 to 0.625
- expand_weight: bfloat16 [2, 768, 3072], P('section'), may hold values from -0.21875 to 0.21875
- contract_weight: bfloat16 [2, 3072, 768], P('section'), may hold values from -0.109375 to 0.109375
- expand_bias: float32 [2, 3072], P('section'), may hold values from -1.75 to 1.75
- layer_biases: float32 [2, 6, 768], P('section'), may hold values from -1.75 to 1.75
- layer_gains: float32 [2, 2, 768], P('section'), may hold values from 0.25 to 1.75
- cross_weight: bfloat16 [768, 3072], replicated, may hold values from -0.3125 to 0.3125
- cross_biases: float32 [4, 768], replicated, may hold values from -1.75 to 1.75
- cross_gain: float32 [768], replicated, may hold values from 0.25 to 1.75
Outputs:
- outputs_long: bfloat16 [2, 16, 640, 768], P('section', 'dp')
- outputs_short: bfloat16 [2, 16, 256, 768], P('section', 'dp')
- input_grad_long: float32 [2, 16, 640, 768], P('section', 'dp')
- input_grad_short: float32 [2, 16, 256, 768], P('section', 'dp')
- self_in_grad: float32 [2, 768, 2304], P('section', 'dp')
- self_out_grad: float32 [2, 768, 768], P('section', 'dp')
- expand_grad: float32 [2, 768, 3072], P('section', 'dp')
- contract_grad: float32 [2, 3072, 768], P('section', 'dp')
- expand_bias_grad: float32 [2, 3072], P('section', 'dp')
- bias_grad: float32 [2, 6, 768], P('section', None, 'dp')
- gain_grad: float32 [2, 2, 768], P('section', None, 'dp')
- cross_grad: float32 [768, 3072], P(None, ('section', 'dp'))
- cross_bias_grad: float32 [4, 768], replicated
- cross_gain_grad: float32 [768], replicated
The draws below stay inside these ranges and needn't reach their ends.
Inputs may be any that keep to these rules, and one draw needn't show every extreme that they name: In each row of lengths_long the lengths sum to 7680 and the largest is 640. In each row of lengths_short the lengths sum to 3072 and the largest is 256.
All inputs are finite; a program needn't handle non-finite values. No bound on the sum of `lengths_long` or of `lengths_short` on one device may be relied on, other than what follows from the above.
Results may differ from the reference program's by a relative error of at most 0.02.
Values may be sent and summed in bfloat16 or wider, within the bound.
A program may use at most 320 MiB of HBM per device.

```python
import math
import jax
import jax.numpy as jnp
import numpy as np
from jax import lax

D = 768
HEAD_DIM = 64
FF = 3072
LONG_LEN = 640
SHORT_LEN = 256
LONG_ROWS = 16
SHORT_ROWS = 16


def shard_levels(rng, dims, split, least, top_value):
    level = 1.0
    for axis_at, blocks in split:
        draws = jax.random.uniform(jax.random.fold_in(jax.random.fold_in(rng, 6), axis_at), (blocks,), jnp.float32, least / len(split), top_value / len(split))
        level = level * jnp.repeat(jnp.exp(draws), dims[axis_at] // blocks).reshape((-1,) + (1,) * (len(dims) - 1 - axis_at))
    return level


def split_up(number_of, total, reach, lean):
    portions = [(1 << 20) // math.isqrt(rank ** lean) + 1 for rank in range(2, number_of + 1)]
    rest, counts = total - reach - (number_of - 1), [1] * (number_of - 1)
    while rest > 0:
        free = [i for i in range(number_of - 1) if counts[i] < reach]
        mass, budget = sum([portions[i] for i in free]), rest
        for i in free:
            more = min(reach - counts[i], max(1, budget * portions[i] // mass), rest)
            counts[i] = counts[i] + more
            rest = rest - more
    return np.array([reach] + counts)


def uneven(own_key, number_of, total, most, slope):
    if number_of == 2:
        one = jax.random.randint(own_key, (), max(1, total - most), min(most, total - 1) + 1)
        return jnp.stack([one, total - one])
    sizes = jnp.asarray(split_up(number_of, total, most, slope), jnp.int32)
    twos = (number_of - 1) // 2
    source_of, receiver = sizes[1:1 + 2 * twos:2], sizes[2:2 + 2 * twos:2]
    slack = jnp.minimum(source_of - 1, most - receiver)
    shifted = jax.random.randint(jax.random.fold_in(own_key, 1), (twos,), 0, 1 << 20) % (slack + 1)
    sizes = sizes.at[1:1 + 2 * twos:2].set(source_of - shifted).at[2:2 + 2 * twos:2].set(receiver + shifted)
    return sizes[jax.random.permutation(jax.random.fold_in(own_key, 2), number_of)]


def normal_values(stream_key, dims, deviation, bound, split=(), held_as=jnp.bfloat16):
    loudness = shard_levels(stream_key, dims, split, -0.22, 0.18) if split else 1.0
    array = jax.random.normal(stream_key, dims, jnp.float32) * deviation * loudness
    return jnp.minimum(jnp.maximum(array, -bound), bound).astype(held_as)


def setup_inputs(seed: int = 0) -> dict:
    key_of = jax.random.split(jax.random.key(seed), 17)
    inputs_long = normal_values(key_of[0], (2, LONG_ROWS, LONG_LEN, D), 1.0, 6.0, ((0, 2), (1, 16)))
    inputs_short = normal_values(key_of[1], (2, SHORT_ROWS, SHORT_LEN, D), 1.0, 6.0, ((0, 2), (1, 16)))
    cotangent_long = normal_values(key_of[2], (2, LONG_ROWS, LONG_LEN, D), 1.0, 6.0, ((0, 2), (1, 16)))
    cotangent_short = normal_values(key_of[3], (2, SHORT_ROWS, SHORT_LEN, D), 1.0, 6.0, ((0, 2), (1, 16)))
    lengths_long = jax.vmap(lambda own: uneven(own, LONG_ROWS, LONG_ROWS * LONG_LEN * 3 // 4, LONG_LEN, 1))(jax.random.split(key_of[4], 2)).reshape((2, LONG_ROWS)).astype(jnp.int32)
    lengths_short = jax.vmap(lambda own: uneven(own, SHORT_ROWS, SHORT_ROWS * SHORT_LEN * 3 // 4, SHORT_LEN, 1))(jax.random.split(key_of[5], 2)).reshape((2, SHORT_ROWS)).astype(jnp.int32)
    self_in_weight = normal_values(key_of[6], (2, D, 3 * D), (D // 2) ** -0.5, 0.3125, ((0, 2),))
    self_out_weight = normal_values(key_of[7], (2, D, D), (D // 8) ** -0.5, 0.625, ((0, 2),))
    expand_weight = normal_values(key_of[8], (2, D, FF), D ** -0.5, 0.21875, ((0, 2),))
    contract_weight = normal_values(key_of[9], (2, FF, D), FF ** -0.5, 0.109375, ((0, 2),))
    expand_bias = normal_values(key_of[10], (2, FF), 0.3, 1.75, ((0, 2),), jnp.float32)
    layer_biases = normal_values(key_of[11], (2, 6, D), 0.3, 1.75, ((0, 2),), jnp.float32)
    layer_gains = jnp.clip(1.0 + 0.15 * jax.random.normal(key_of[12], (2, 2, D), jnp.float32), 0.25, 1.75)
    cross_weight = normal_values(key_of[13], (D, 4 * D), (D // 2) ** -0.5, 0.3125)
    cross_biases = normal_values(key_of[14], (4, D), 0.3, 1.75, (), jnp.float32)
    cross_gain = jnp.clip(1.0 + 0.15 * jax.random.normal(key_of[15], (D,), jnp.float32), 0.25, 1.75)
    return {"inputs_long": inputs_long, "inputs_short": inputs_short, "cotangent_long": cotangent_long, "cotangent_short": cotangent_short, "lengths_long": lengths_long, "lengths_short": lengths_short, "self_in_weight": self_in_weight, "self_out_weight": self_out_weight, "expand_weight": expand_weight, "contract_weight": contract_weight, "expand_bias": expand_bias, "layer_biases": layer_biases, "layer_gains": layer_gains, "cross_weight": cross_weight, "cross_biases": cross_biases, "cross_gain": cross_gain}


HIGHEST = lax.Precision.HIGHEST
EPSILON = 1e-05
MASKED = -1e+30

@jax.custom_vjp
def low(v):
    return lax.optimization_barrier(v.astype(jnp.bfloat16)).astype(jnp.float32)

@jax.custom_vjp
def low_back(v):
    return v

def low_keep(v):
    return (low(v), None)

def low_pass(kept, grad):
    return (grad,)

def back_keep(v):
    return (v, None)

def back_low(kept, grad):
    return (low(grad),)
low.defvjp(low_keep, low_pass)
low_back.defvjp(back_keep, back_low)

def project(operand, factor):
    return jnp.dot(operand, factor, precision=HIGHEST)

def layer_norm(hidden, gain, shift):
    centred = hidden - lax.optimization_barrier(jnp.mean(hidden, axis=-1, keepdims=True))
    spread = lax.optimization_barrier(jnp.mean(centred * centred, axis=-1, keepdims=True))
    return centred * lax.rsqrt(spread + EPSILON) * gain + shift

def attend_rows(queries, key_rows, value_rows, key_lengths, causal):
    row_count, seq_length, model_width = queries.shape
    head_count = model_width // HEAD_DIM
    scale = HEAD_DIM ** (-0.5)

    def one_row(packet):
        query_row, key_row, value_row, key_length = packet
        split_query = query_row.reshape(seq_length, head_count, HEAD_DIM)
        split_key = key_row.reshape(-1, head_count, HEAD_DIM)
        split_value = value_row.reshape(-1, head_count, HEAD_DIM)
        scores = low_back(jnp.einsum('qhe,khe->hqk', split_query, split_key, precision=HIGHEST) * scale)
        key_place = jnp.arange(split_key.shape[0])
        query_place = jnp.arange(seq_length)
        allowed = key_place[None, :] < key_length
        if causal:
            allowed = allowed & (key_place[None, :] <= query_place[:, None])
        scores = jnp.where(allowed[None], scores, MASKED)
        highest = lax.optimization_barrier(jnp.max(scores, axis=-1, keepdims=True))
        weights = jnp.exp(scores - highest)
        probability = low(weights / lax.optimization_barrier(jnp.sum(weights, axis=-1, keepdims=True)))
        mixed = jnp.einsum('hqk,khe->qhe', probability, split_value, precision=HIGHEST)
        return mixed.reshape(seq_length, model_width)
    return lax.map(jax.checkpoint(one_row), (queries, key_rows, value_rows, key_lengths))

def reference(inputs_long, inputs_short, cotangent_long, cotangent_short, lengths_long, lengths_short, self_in_weight, self_out_weight, expand_weight, contract_weight, expand_bias, layer_biases, layer_gains, cross_weight, cross_biases, cross_gain):
    model_width = inputs_long.shape[-1]
    long_shape = inputs_long.shape[1:]
    short_shape = inputs_short.shape[1:]
    long_count = long_shape[0] * long_shape[1]
    source_lengths = (lengths_long[0], lengths_short[0])
    target_lengths = (lengths_long[1], lengths_short[1])

    def flatten(long_part, short_part):
        return jnp.concatenate([long_part.reshape(-1, model_width), short_part.reshape(-1, model_width)], 0)

    def attend_buckets(queries, key_rows, value_rows, key_lengths, causal):
        long_out = attend_rows(queries[:long_count].reshape(long_shape), key_rows[:long_count].reshape(long_shape), value_rows[:long_count].reshape(long_shape), key_lengths[0], causal)
        short_out = attend_rows(queries[long_count:].reshape(short_shape), key_rows[long_count:].reshape(short_shape), value_rows[long_count:].reshape(short_shape), key_lengths[1], causal)
        return flatten(long_out, short_out)
    params = tuple((member.astype(jnp.float32) for member in (self_in_weight, self_out_weight, expand_weight, contract_weight, expand_bias, layer_biases, layer_gains, cross_weight, cross_biases, cross_gain)))

    def forward(weights, long_in, short_in):
        self_in, self_out, expand, contract, expand_shift, bias_rows, gain_rows, cross_all, cross_shift, cross_scale = weights

        def self_sub(tokens, half, lengths, causal):
            joint = project(tokens, self_in[half])
            queries = low(low_back(joint[:, :model_width] + bias_rows[half, 0]))
            key_rows = low(low_back(joint[:, model_width:2 * model_width]))
            value_rows = low(low_back(joint[:, 2 * model_width:] + bias_rows[half, 1]))
            mixed = low(low_back(attend_buckets(queries, key_rows, value_rows, lengths, causal)))
            branch = low_back(project(mixed, self_out[half]) + bias_rows[half, 2])
            return layer_norm(tokens + branch, gain_rows[half, 0], bias_rows[half, 3])

        def expand_sub(normed, half):
            inner = low_back(project(low(normed), expand[half]) + expand_shift[half])
            active = low(jax.nn.gelu(inner, approximate=False))
            branch = low_back(project(active, contract[half]) + bias_rows[half, 4])
            return layer_norm(normed + branch, gain_rows[half, 1], bias_rows[half, 5])

        def cross_sub(normed, memory):
            queries = low(low_back(project(low(normed), cross_all[:, :model_width]) + cross_shift[0]))
            key_rows = low(low_back(project(memory, cross_all[:, model_width:2 * model_width])))
            value_rows = low(low_back(project(memory, cross_all[:, 2 * model_width:3 * model_width]) + cross_shift[1]))
            mixed = low(low_back(attend_buckets(queries, key_rows, value_rows, source_lengths, False)))
            branch = low_back(project(mixed, cross_all[:, 3 * model_width:]) + cross_shift[2])
            return layer_norm(normed + branch, cross_scale, cross_shift[3])
        encoder_in = flatten(long_in[0], short_in[0])
        decoder_in = flatten(long_in[1], short_in[1])
        encoded = expand_sub(self_sub(encoder_in, 0, source_lengths, False), 0)
        memory = low(low_back(encoded))
        decoded = expand_sub(cross_sub(self_sub(decoder_in, 1, target_lengths, True), memory), 1)
        return (encoded, decoded)

    def masked(cotangent, lengths):
        keep = (jnp.arange(cotangent.shape[1])[None, :] < lengths[:, None]).astype(jnp.float32)
        return cotangent.astype(jnp.float32) * keep[:, :, None]
    encoder_cot = flatten(masked(cotangent_long[0], source_lengths[0]), masked(cotangent_short[0], source_lengths[1]))
    decoder_cot = flatten(masked(cotangent_long[1], target_lengths[0]), masked(cotangent_short[1], target_lengths[1]))
    results, pullback = jax.vjp(forward, params, inputs_long.astype(jnp.float32), inputs_short.astype(jnp.float32))
    grad_params, grad_long, grad_short = pullback((encoder_cot, decoder_cot))
    outputs_long = jnp.stack([results[0][:long_count].reshape(long_shape), results[1][:long_count].reshape(long_shape)]).astype(jnp.bfloat16)
    outputs_short = jnp.stack([results[0][long_count:].reshape(short_shape), results[1][long_count:].reshape(short_shape)]).astype(jnp.bfloat16)
    return (outputs_long, outputs_short, grad_long, grad_short, grad_params[0], grad_params[1], grad_params[2], grad_params[3], grad_params[4], grad_params[5], grad_params[6], grad_params[7], grad_params[8], grad_params[9])
```

```python
import functools
import jax
import jax.numpy as jnp
from jax import lax
from jax.experimental import pallas as pl
from jax.experimental.pallas import tpu as pltpu
from jax.sharding import PartitionSpec as P

BF, F32 = jnp.bfloat16, jnp.float32
NEG = -1e30
NT = (((1,), (1,)), ((), ()))
TN = (((0,), (0,)), ((), ()))

def dot(a, b):
    return jnp.dot(a, b, preferred_element_type=F32)
def dot_nt(a, b):
    return lax.dot_general(a, b, NT, preferred_element_type=F32)
def dot_tn(a, b):
    return lax.dot_general(a, b, TN, preferred_element_type=F32)

def lanes(rows):
    return lax.broadcasted_iota(jnp.int32, (rows, 128), 1)

def split3(v):
    hi = v.astype(BF)
    rest = v - hi.astype(F32)
    mid = rest.astype(BF)
    low = (rest - mid.astype(F32)).astype(BF)
    return hi, mid, low

def norm_forward(u, gain, shift):
    mean = jnp.mean(u, axis=-1, keepdims=True)
    c = u - mean
    r = lax.rsqrt(jnp.mean(c * c, axis=-1, keepdims=True) + 1e-5)
    xhat = c * r
    return xhat, r, xhat * gain + shift

def attn_fwd_kernel(causal, same, len_ref, xq_ref, xkv_ref, res_ref, wqkv_ref, wo_ref, bias_ref, gain_ref,
                    qkv_ref, o_ref, lse_ref, xhat_ref, r_ref, n_ref):
    s, d = xq_ref.shape
    if not same:
        wo_ref = wqkv_ref.at[:, 3 * d :]
    xq = xq_ref[...].astype(BF)
    xkv = xq if same else xkv_ref[...]
    qkv_ref[:, :d] = (dot(xq, wqkv_ref[:, :d]) + bias_ref[0:1, :]).astype(BF)
    qkv_ref[:, d:2*d] = dot(xkv, wqkv_ref[:, d:2*d]).astype(BF)
    qkv_ref[:, 2*d:] = (dot(xkv, wqkv_ref[:, 2*d:3*d]) + bias_ref[1:2, :]).astype(BF)
    length = len_ref[0, 0]
    lane = lanes(s)
    row = lax.broadcasted_iota(jnp.int32, (s, 128), 0)
    key_bias = jnp.where(row < length, 0.0, NEG).astype(BF)
    if causal:
        tri = lax.broadcasted_iota(jnp.int32, (s, s), 1) <= lax.broadcasted_iota(jnp.int32, (s, s), 0)
    one = jnp.ones((s, 128), BF)
    zero = jnp.zeros((s, 128), BF)

    def pair(p, _):
        at = pl.multiple_of(p * 128, 128)
        q = qkv_ref[:, pl.ds(at, 128)] * jnp.asarray(0.125, BF)
        k = qkv_ref[:, pl.ds(d + at, 128)]
        v = qkv_ref[:, pl.ds(2 * d + at, 128)]
        outs, lses = [], []
        for h in range(2):
            mine = (lane < 64) if h == 0 else (lane >= 64)
            other = 64 if h == 0 else 0
            qh = jnp.where(mine, q, jnp.where(lane == other, one, zero))
            kh = jnp.where(mine, k, jnp.where(lane == other, key_bias, zero))
            sc = dot_nt(qh, kh)
            if causal:
                sc = jnp.where(tri, sc, NEG)
            m = jnp.max(sc, axis=-1, keepdims=True)
            e = jnp.exp(sc - m)
            l = jnp.sum(e, axis=-1, keepdims=True)
            outs.append(dot(e.astype(BF), v) * (1.0 / l))
            lses.append(m + jnp.log(l))
        o_ref[:, pl.ds(at, 128)] = jnp.where(lane < 64, outs[0], outs[1]).astype(BF)
        lse_ref[:, pl.ds(at, 128)] = jnp.where(lane < 64, lses[1], lses[0])
        return 0
    lax.fori_loop(0, d // 128, pair, 0)
    u = res_ref[...].astype(F32) + dot(o_ref[...], wo_ref[...]) + bias_ref[2:3, :]
    xhat, r, n = norm_forward(u, gain_ref[0:1, :], bias_ref[3:4, :])
    xhat_ref[...] = xhat
    r_ref[...] = jnp.broadcast_to(r, r_ref.shape)
    n_ref[...] = n

def attn_fwd(xq, xkv, res, wqkv, wo, bias, gain, length, causal):
    s, d = xq.shape
    same = xkv is None
    if same:
        xkv = xq
    else:
        wo = gain
    vm = pl.BlockSpec(memory_space=pltpu.VMEM)
    sm = pl.BlockSpec(memory_space=pltpu.SMEM)
    return pl.pallas_call(
        functools.partial(attn_fwd_kernel, causal, same),
        out_shape=(jax.ShapeDtypeStruct((s, 3 * d), BF), jax.ShapeDtypeStruct((s, d), BF), jax.ShapeDtypeStruct((s, d), F32),
                   jax.ShapeDtypeStruct((s, d), F32), jax.ShapeDtypeStruct((s, 128), F32), jax.ShapeDtypeStruct((s, d), F32)),
        in_specs=[sm] + [vm] * 7, out_specs=(vm,) * 6,
        compiler_params=pltpu.CompilerParams(vmem_limit_bytes=60 << 20),
    )(length.reshape(1, 1), xq, xkv, res, wqkv, wo, bias, gain)

def norm_backward(dn, xhat, r, gain):
    h = dn * gain
    return r * (h - jnp.mean(h, axis=-1, keepdims=True) - xhat * jnp.mean(h * xhat, axis=-1, keepdims=True))

def attn_bwd_kernel(causal, same, len_ref, dn_ref, qkv_ref, o_ref, lse_ref, xhat_ref, r_ref, wqkv_ref, wo_ref, gain_ref,
                    dres_ref, dqkv_ref, dt_ref, dkvx_ref, sums_ref, do_ref, dq_ref):
    s, d = dn_ref.shape
    if not same:
        wo_ref = wqkv_ref.at[:, 3 * d :]
    dn = dn_ref[...]
    xhat = xhat_ref[...]
    du = norm_backward(dn, xhat, r_ref[:, :1], gain_ref[0:1, :])
    dt = du.astype(BF)
    dt_ref[...] = dt
    sums_ref[2:3, :] = jnp.sum(dt.astype(F32), axis=0, keepdims=True)
    sums_ref[3:4, :] = jnp.sum(dn, axis=0, keepdims=True)
    sums_ref[4:5, :] = jnp.sum(dn * xhat, axis=0, keepdims=True)
    do_ref[...] = dot_nt(dt, wo_ref[...]).astype(BF)
    length = len_ref[0, 0]
    lane = lanes(s)
    row = lax.broadcasted_iota(jnp.int32, (s, 128), 0)
    key_bias = jnp.where(row < length, 0.0, NEG).astype(BF)
    if causal:
        tri = lax.broadcasted_iota(jnp.int32, (s, s), 0) <= lax.broadcasted_iota(jnp.int32, (s, s), 1)
    one = jnp.ones((s, 128), BF)
    zero = jnp.zeros((s, 128), BF)

    def place(base, mine, other, extra):
        out = zero
        for j, val in enumerate(extra):
            out = jnp.where(lane == other + j, val, out)
        return jnp.where(mine, base, out)

    def pair(p, _):
        at = pl.multiple_of(p * 128, 128)
        q = qkv_ref[:, pl.ds(at, 128)] * jnp.asarray(0.125, BF)
        k = qkv_ref[:, pl.ds(d + at, 128)]
        v = qkv_ref[:, pl.ds(2 * d + at, 128)]
        do = do_ref[:, pl.ds(at, 128)]
        lse3 = split3(-lse_ref[:, pl.ds(at, 128)])
        prod = do.astype(F32) * o_ref[:, pl.ds(at, 128)].astype(F32)
        dq, dk, dv = [], [], []
        for h in range(2):
            mine = (lane < 64) if h == 0 else (lane >= 64)
            other = 64 if h == 0 else 0
            inner = jnp.broadcast_to(jnp.sum(jnp.where(mine, prod, 0.0), axis=-1, keepdims=True), (s, 128))
            qh = place(q, mine, other, (*lse3, one))
            kh = place(k, mine, other, (one, one, one, key_bias))
            doh = place(do, mine, other, split3(-inner))
            vh = place(v, mine, other, (one, one, one))
            st = dot_nt(kh, qh)
            if causal:
                st = jnp.where(tri, st, NEG)
            pt = jnp.exp(st)
            dst = (pt * dot_nt(vh, doh)).astype(BF)
            dv.append(dot(pt.astype(BF), do))
            dk.append(dot(dst, q))
            dq.append(dot_tn(k, dst))
        m1 = lane < 64
        dq_ref[...] = jnp.where(lax.broadcasted_iota(jnp.int32, (128, s), 0) < 64, dq[0], dq[1])
        dqkv_ref[:, pl.ds(at, 128)] = (dq_ref[...].T * 0.125).astype(BF)
        dqkv_ref[:, pl.ds(d + at, 128)] = jnp.where(m1, dk[0], dk[1]).astype(BF)
        dqkv_ref[:, pl.ds(2 * d + at, 128)] = jnp.where(m1, dv[0], dv[1]).astype(BF)
        return 0
    lax.fori_loop(0, d // 128, pair, 0)
    if same:
        dres_ref[...] = du + dot_nt(dqkv_ref[...], wqkv_ref[...])
    else:
        dres_ref[...] = du + dot_nt(dqkv_ref[:, :d], wqkv_ref[:, :d])
        dkvx_ref[...] = dot_nt(dqkv_ref[:, d:], wqkv_ref[:, d:3*d]).astype(BF)
    sums_ref[0:1, :] = jnp.sum(dqkv_ref[:, :d].astype(F32), axis=0, keepdims=True)
    sums_ref[1:2, :] = jnp.sum(dqkv_ref[:, 2*d:].astype(F32), axis=0, keepdims=True)
    sums_ref[5:8, :] = jnp.zeros((3, d), F32)

def attn_bwd(dn, saved, wqkv, wo, gain, length, causal, same):
    qkv, o, lse, xhat, r = saved
    s, d = dn.shape
    if not same:
        wo = gain
    vm = pl.BlockSpec(memory_space=pltpu.VMEM)
    sm = pl.BlockSpec(memory_space=pltpu.SMEM)
    return pl.pallas_call(
        functools.partial(attn_bwd_kernel, causal, same),
        out_shape=(jax.ShapeDtypeStruct((s, d), F32), jax.ShapeDtypeStruct((s, 3 * d), BF), jax.ShapeDtypeStruct((s, d), BF),
                   jax.ShapeDtypeStruct((8, 128) if same else (s, d), BF), jax.ShapeDtypeStruct((8, d), F32)),
        in_specs=[sm] + [vm] * 9, out_specs=(vm,) * 5,
        scratch_shapes=[pltpu.VMEM((s, d), BF), pltpu.VMEM((128, s), F32)],
        compiler_params=pltpu.CompilerParams(vmem_limit_bytes=60 << 20),
    )(length.reshape(1, 1), dn, qkv, o, lse, xhat, r, wqkv, wo, gain)

def gelu_parts(a):
    e = jnp.exp(-0.5 * a * a)
    t = 1.0 / (1.0 + 0.23164188624 * jnp.abs(a))
    tail = t * (0.127414796 + t * (-0.142248368 + t * (0.7107068705 + t * (-0.7265760135 + t * 0.5307027145)))) * e
    phi_cap = jnp.where(a < 0.0, tail, 1.0 - tail)
    return phi_cap, e * 0.3989422804014327

def ffn_fwd_kernel(chunk, n_ref, we_ref, wc_ref, be_ref, bias_ref, gain_ref,
                   y_ref, g_ref, gp_ref, xhat_ref, r_ref, acc_ref):
    s, d = n_ref.shape
    ff = we_ref.shape[1]
    low = n_ref[...].astype(BF)
    acc_ref[...] = n_ref[...] + bias_ref[4:5, :]

    def step(c, _):
        at = pl.multiple_of(c * chunk, chunk)
        a = dot(low, we_ref[:, pl.ds(at, chunk)]) + be_ref[:, pl.ds(at, chunk)]
        cap, dens = gelu_parts(a)
        g = (a * cap).astype(BF)
        g_ref[:, pl.ds(at, chunk)] = g
        gp_ref[:, pl.ds(at, chunk)] = (cap + a * dens).astype(BF)
        acc_ref[...] += dot(g, wc_ref[pl.ds(at, chunk), :])
        return 0
    lax.fori_loop(0, ff // chunk, step, 0)
    xhat, r, y = norm_forward(acc_ref[...], gain_ref[1:2, :], bias_ref[5:6, :])
    xhat_ref[...] = xhat
    r_ref[...] = jnp.broadcast_to(r, r_ref.shape)
    y_ref[...] = y.astype(BF)

def ffn_fwd(n, we, wc, be, bias, gain, chunk=512):
    s, d = n.shape
    ff = we.shape[1]
    vm = pl.BlockSpec(memory_space=pltpu.VMEM)
    return pl.pallas_call(
        functools.partial(ffn_fwd_kernel, chunk),
        out_shape=(jax.ShapeDtypeStruct((s, d), BF), jax.ShapeDtypeStruct((s, ff), BF), jax.ShapeDtypeStruct((s, ff), BF),
                   jax.ShapeDtypeStruct((s, d), F32), jax.ShapeDtypeStruct((s, 128), F32)),
        in_specs=[vm] * 6, out_specs=(vm,) * 5,
        scratch_shapes=[pltpu.VMEM((s, d), F32)],
        compiler_params=pltpu.CompilerParams(vmem_limit_bytes=60 << 20),
    )(n, we, wc, be.reshape(1, ff), bias, gain)

def ffn_bwd_kernel(chunk, extra, len_ref, cot_ref, dm_ref, gp_ref, xhat_ref, r_ref, we_ref, wc_ref, gain_ref,
                   dn_ref, da_ref, dt_ref, sums_ref, sume_ref):
    s, d = cot_ref.shape
    ff = we_ref.shape[1]
    row = lax.broadcasted_iota(jnp.int32, (s, 1), 0)
    dy = jnp.where(row < len_ref[0, 0], cot_ref[...].astype(F32), 0.0)
    if extra:
        dy = dy + dm_ref[...].astype(F32)
    xhat = xhat_ref[...]
    du = norm_backward(dy, xhat, r_ref[:, :1], gain_ref[1:2, :])
    dt = du.astype(BF)
    dt_ref[...] = dt
    sums_ref[0:1, :] = jnp.sum(dt.astype(F32), axis=0, keepdims=True)
    sums_ref[1:2, :] = jnp.sum(dy, axis=0, keepdims=True)
    sums_ref[2:3, :] = jnp.sum(dy * xhat, axis=0, keepdims=True)
    sums_ref[3:8, :] = jnp.zeros((5, d), F32)
    dn_ref[...] = du

    def step(c, _):
        at = pl.multiple_of(c * chunk, chunk)
        dg = dot_nt(dt_ref[...], wc_ref[pl.ds(at, chunk), :])
        da = (dg * gp_ref[:, pl.ds(at, chunk)].astype(F32)).astype(BF)
        da_ref[:, pl.ds(at, chunk)] = da
        sume_ref[:, pl.ds(at, chunk)] = jnp.sum(da.astype(F32), axis=0, keepdims=True)
        dn_ref[...] += dot_nt(da, we_ref[:, pl.ds(at, chunk)])
        return 0
    lax.fori_loop(0, ff // chunk, step, 0)

def ffn_bwd(cot, dm, length, saved, we, wc, gain, chunk=512):
    gp, xhat, r = saved
    s, d = cot.shape
    ff = we.shape[1]
    extra = dm is not None
    vm = pl.BlockSpec(memory_space=pltpu.VMEM)
    sm = pl.BlockSpec(memory_space=pltpu.SMEM)
    return pl.pallas_call(
        functools.partial(ffn_bwd_kernel, chunk, extra),
        out_shape=(jax.ShapeDtypeStruct((s, d), F32), jax.ShapeDtypeStruct((s, ff), BF), jax.ShapeDtypeStruct((s, d), BF),
                   jax.ShapeDtypeStruct((8, d), F32), jax.ShapeDtypeStruct((1, ff), F32)),
        in_specs=[sm] + [vm] * 8, out_specs=(vm,) * 5,
        compiler_params=pltpu.CompilerParams(vmem_limit_bytes=60 << 20),
    )(length.reshape(1, 1), cot, dm if extra else cot, gp, xhat, r, we, wc, gain)

def wgrad_kernel(lengths, *refs):
    n = len(lengths)
    xs, dys, out_ref, xt_ref = refs[:n], refs[n:2*n], refs[2*n], refs[2*n+1]
    @pl.when(pl.program_id(0) == 0)
    def _():
        at = 0
        for x, s in zip(xs, lengths):
            xt_ref[:, at:at+s] = x[...].astype(BF).T
            at += s
    at, total = 0, None
    for dy, s in zip(dys, lengths):
        t = dot(xt_ref[:, at:at+s], dy[...].astype(BF))
        total = t if total is None else total + t
        at += s
    out_ref[...] = total.astype(BF)

def wgrad(xs, dys, tile=768):
    lengths = [x.shape[0] for x in xs]
    k, n = xs[0].shape[1], dys[0].shape[1]
    return pl.pallas_call(
        functools.partial(wgrad_kernel, lengths),
        out_shape=jax.ShapeDtypeStruct((k, n), BF),
        grid=(n // tile,),
        in_specs=[pl.BlockSpec((s, k), lambda i: (0, 0)) for s in lengths] + [pl.BlockSpec((s, tile), lambda i: (0, i)) for s in lengths],
        out_specs=pl.BlockSpec((k, tile), lambda i: (0, i)),
        scratch_shapes=[pltpu.VMEM((k, sum(lengths)), BF)],
        compiler_params=pltpu.CompilerParams(vmem_limit_bytes=60 << 20),
    )(*xs, *dys)


def small_rows(parts):
    total = parts[0]
    for part in parts[1:]:
        total = total + part
    return total


def shards(
    inputs_long,
    inputs_short,
    cotangent_long,
    cotangent_short,
    lengths_long,
    lengths_short,
    self_in_weight,
    self_out_weight,
    expand_weight,
    contract_weight,
    expand_bias,
    layer_biases,
    layer_gains,
    cross_weight,
    cross_biases,
    cross_gain,
):
    decoder = lax.axis_index("section") == 1
    d = inputs_long.shape[-1]
    ff = expand_weight.shape[2]
    w_in, w_out, w_e, w_c = self_in_weight[0], self_out_weight[0], expand_weight[0], contract_weight[0]
    b_e, bias, gain = expand_bias[0], layer_biases[0], layer_gains[0]
    c_gain = cross_gain.reshape(1, d)

    xs = (inputs_short[0, 0], inputs_long[0, 0])
    cots = (cotangent_short[0, 0], cotangent_long[0, 0])
    source = (lengths_short[0, 0], lengths_long[0, 0])
    target = (lengths_short[1, 0], lengths_long[1, 0])
    sizes = tuple(x.shape[0] for x in xs)

    def zeros_like_fwd(s):
        return (
            jnp.zeros((s, d), BF),
            jnp.zeros((s, ff), BF),
            jnp.zeros((s, ff), BF),
            jnp.zeros((s, d), F32),
            jnp.zeros((s, 128), F32),
        )

    def first(i):
        x = xs[i]

        def encode():
            out = attn_fwd(x, None, x, w_in, w_out, bias, gain, source[i], False)
            return out, ffn_fwd(out[5], w_e, w_c, b_e, bias, gain)

        def decode():
            out = attn_fwd(x, None, x, w_in, w_out, bias, gain, target[i], True)
            return out, zeros_like_fwd(sizes[i])

        return lax.cond(decoder, decode, encode)

    def send(value, steps):
        return lax.ppermute(value, "section", [(0, 1)] if steps > 0 else [(1, 0)])

    def middle(i, memory, n1):
        s = sizes[i]

        def decode():
            out = attn_fwd(n1, memory, n1, cross_weight, None, cross_biases, c_gain, source[i], False)
            y, g, gp, xhat, r = ffn_fwd(out[5], w_e, w_c, b_e, bias, gain)
            fb = ffn_bwd(cots[i], None, target[i], (gp, xhat, r), w_e, w_c, gain)
            ab = attn_bwd(fb[0], out[:5], cross_weight, None, c_gain, source[i], False, False)
            return (out[5], g, fb[1], fb[2], out[1], ab[1], ab[2]), ab[0], ab[3], y, (fb[3], fb[4], ab[4])

        def encode():
            return (
                (
                    jnp.zeros((s, d), F32),
                    jnp.zeros((s, ff), BF),
                    jnp.zeros((s, ff), BF),
                    jnp.zeros((s, d), BF),
                    jnp.zeros((s, d), BF),
                    jnp.zeros((s, 3 * d), BF),
                    jnp.zeros((s, d), BF),
                ),
                jnp.zeros((s, d), F32),
                jnp.zeros((s, d), BF),
                jnp.zeros((s, d), BF),
                (jnp.zeros((8, d), F32), jnp.zeros((1, ff), F32), jnp.zeros((8, d), F32)),
            )

        return lax.cond(decoder, decode, encode)

    def last(i, att, ffn, dn_dec, dm):
        s = sizes[i]

        def decode():
            ab = attn_bwd(dn_dec, att[:5], w_in, w_out, gain, target[i], True, True)
            return (
                (ab[0], ab[1], ab[2], ab[4]),
                (jnp.zeros((s, ff), BF), jnp.zeros((s, d), BF), jnp.zeros((8, d), F32), jnp.zeros((1, ff), F32)),
            )

        def encode():
            fb = ffn_bwd(cots[i], dm, source[i], ffn[2:], w_e, w_c, gain)
            ab = attn_bwd(fb[0], att[:5], w_in, w_out, gain, source[i], False, True)
            return (ab[0], ab[1], ab[2], ab[4]), fb[1:]

        return lax.cond(decoder, decode, encode)

    att0, ffn0 = first(0)
    mem0 = send(ffn0[0], 1)
    att1, ffn1 = first(1)
    mem1 = send(ffn1[0], 1)
    keep0, dn0, dm0, y0, sums0 = middle(0, mem0, att0[5])
    back0 = send(dm0, -1)
    keep1, dn1, dm1, y1, sums1 = middle(1, mem1, att1[5])
    back1 = send(dm1, -1)
    self0, enc0 = last(0, att0, ffn0, dn0, back0)
    self1, enc1 = last(1, att1, ffn1, dn1, back1)

    def cross_grads():
        low = (att0[5], att1[5])
        return jnp.concatenate(
            [
                wgrad((keep0[5][:, :d], keep1[5][:, :d]), low),
                wgrad((keep0[5][:, d:], keep1[5][:, d:]), (mem0, mem1)),
                wgrad((keep0[6], keep1[6]), (keep0[4], keep1[4])),
            ],
            0,
        )

    cross_full = lax.cond(decoder, cross_grads, lambda: jnp.zeros((4 * d, d), BF))

    def ffn_grads_dec():
        return (
            wgrad((keep0[0], keep1[0]), (keep0[2], keep1[2])),
            wgrad((keep0[1], keep1[1]), (keep0[3], keep1[3]), 256),
            sums0[0] + sums1[0],
            sums0[1] + sums1[1],
        )

    def ffn_grads_enc():
        return (
            wgrad((att0[5], att1[5]), (enc0[0], enc1[0])),
            wgrad((ffn0[1], ffn1[1]), (enc0[1], enc1[1]), 256),
            enc0[2] + enc1[2],
            enc0[3] + enc1[3],
        )

    g_expand, g_contract, ffn_sums, sum_e = lax.cond(decoder, ffn_grads_dec, ffn_grads_enc)
    g_in = wgrad(xs, (self0[1], self1[1]))
    g_out = wgrad((att0[1], att1[1]), (self0[2], self1[2]))
    self_sums = self0[3] + self1[3]
    cross_sums = sums0[2] + sums1[2]

    def scatter(value, dim):
        return lax.psum_scatter(value, "dp", scatter_dimension=dim, tiled=True)

    packed = scatter(jnp.concatenate([g_in, g_out, g_expand], 1), 0).astype(F32)
    contract = scatter(g_contract, 0).astype(F32)
    dp = lax.axis_size("dp")
    width = 4 * d // (2 * dp)
    halves = cross_full.reshape(2, dp, width, d).transpose(1, 0, 2, 3).reshape(4 * d, d)
    cross_mine = scatter(halves, 0)
    to_enc = send(cross_mine[:width], -1)
    cross_out = jnp.where(decoder, cross_mine[width:], to_enc).astype(F32).T

    rows = jnp.concatenate([self_sums[0:4], ffn_sums[0:2], self_sums[4:5], ffn_sums[2:3], sum_e.reshape(ff // d, d)], 0)
    blank = jnp.zeros_like(rows)
    every = jnp.concatenate([jnp.where(decoder, blank, rows), jnp.where(decoder, rows, blank), cross_sums[0:5]], 0)
    every = lax.psum(every, ("section", "dp"))
    count = rows.shape[0]
    own = jnp.where(decoder, every[count : 2 * count], every[:count])
    me = lax.axis_index("dp")
    cols = d // dp
    piece = lax.dynamic_slice_in_dim(own[:8], me * cols, cols, 1)
    e_piece = lax.dynamic_slice_in_dim(own[8:].reshape(1, ff), me * (ff // dp), ff // dp, 1)
    cross_vec = every[2 * count :]

    outs = [jnp.where(decoder, y, e)[None, None] for y, e in ((y0, ffn0[0]), (y1, ffn1[0]))]
    return (
        outs[1],
        outs[0],
        self1[0][None, None],
        self0[0][None, None],
        packed[None, :, : 3 * d],
        packed[None, :, 3 * d : 4 * d],
        packed[None, :, 4 * d :],
        contract[None],
        e_piece,
        piece[None, :6],
        piece[None, 6:8],
        cross_out,
        cross_vec[:4],
        cross_vec[4],
    )


def solution(mesh):
    in_specs = (
        P("section", "dp", None, None),
        P("section", "dp", None, None),
        P("section", "dp", None, None),
        P("section", "dp", None, None),
        P(None, "dp"),
        P(None, "dp"),
        P("section", None, None),
        P("section", None, None),
        P("section", None, None),
        P("section", None, None),
        P("section", None),
        P("section", None, None),
        P("section", None, None),
        P(),
        P(),
        P(),
    )
    out_specs = (
        P("section", "dp", None, None),
        P("section", "dp", None, None),
        P("section", "dp", None, None),
        P("section", "dp", None, None),
        P("section", "dp", None),
        P("section", "dp", None),
        P("section", "dp", None),
        P("section", "dp", None),
        P("section", "dp"),
        P("section", None, "dp"),
        P("section", None, "dp"),
        P(None, ("section", "dp")),
        P(),
        P(),
    )
    return jax.shard_map(shards, mesh=mesh, in_specs=in_specs, out_specs=out_specs, check_vma=False)
```

```python
import functools
import jax
import jax.numpy as jnp
from jax import lax
from jax.experimental import pallas as pl
from jax.experimental.pallas import tpu as pltpu
from jax.sharding import PartitionSpec as P

BF, F32 = jnp.bfloat16, jnp.float32
NEG = -1e30
NT = (((1,), (1,)), ((), ()))
TN = (((0,), (0,)), ((), ()))

def dot(a, b):
    return jnp.dot(a, b, preferred_element_type=F32)
def dot_nt(a, b):
    return lax.dot_general(a, b, NT, preferred_element_type=F32)
def dot_tn(a, b):
    return lax.dot_general(a, b, TN, preferred_element_type=F32)

def lanes(rows):
    return lax.broadcasted_iota(jnp.int32, (rows, 128), 1)

def split3(v):
    hi = v.astype(BF)
    rest = v - hi.astype(F32)
    mid = rest.astype(BF)
    low = (rest - mid.astype(F32)).astype(BF)
    return hi, mid, low

def blank(*shapes):
    def nothing(*refs):
        pass

    return pl.pallas_call(
        nothing,
        out_shape=[jax.ShapeDtypeStruct(shape, kind) for shape, kind in shapes],
        out_specs=[pl.BlockSpec(memory_space=pl.ANY)] * len(shapes),
    )()


def norm_forward(u, gain, shift):
    mean = jnp.mean(u, axis=-1, keepdims=True)
    c = u - mean
    r = lax.rsqrt(jnp.mean(c * c, axis=-1, keepdims=True) + 1e-5)
    xhat = c * r
    return xhat, r, xhat * gain + shift

def causal_shift(size):
    return jnp.where(lax.axis_index("section") == 1, 0, size)


def attn_fwd_kernel(same, len_ref, xq_ref, xkv_ref, res_ref, wqkv_ref, wo_ref, bias_ref, gain_ref,
                    qkv_ref, o_ref, lse_ref, xhat_ref, r_ref, n_ref):
    s, d = xq_ref.shape
    if not same:
        wo_ref = wqkv_ref.at[:, 3 * d :]
    xq = xq_ref[...].astype(BF)
    xkv = xq if same else xkv_ref[...]
    qkv_ref[:, :d] = (dot(xq, wqkv_ref[:, :d]) + bias_ref[0:1, :]).astype(BF)
    qkv_ref[:, d:2*d] = dot(xkv, wqkv_ref[:, d:2*d]).astype(BF)
    qkv_ref[:, 2*d:] = (dot(xkv, wqkv_ref[:, 2*d:3*d]) + bias_ref[1:2, :]).astype(BF)
    length = len_ref[0, 0]
    lane = lanes(s)
    row = lax.broadcasted_iota(jnp.int32, (s, 128), 0)
    key_bias = jnp.where(row < length, 0.0, NEG).astype(BF)
    if same:
        tri = lax.broadcasted_iota(jnp.int32, (s, s), 1) <= lax.broadcasted_iota(jnp.int32, (s, s), 0) + causal_shift(s)
    one = jnp.ones((s, 128), BF)
    zero = jnp.zeros((s, 128), BF)

    def pair(p, _):
        at = pl.multiple_of(p * 128, 128)
        q = qkv_ref[:, pl.ds(at, 128)] * jnp.asarray(0.125, BF)
        k = qkv_ref[:, pl.ds(d + at, 128)]
        v = qkv_ref[:, pl.ds(2 * d + at, 128)]
        outs, lses = [], []
        for h in range(2):
            mine = (lane < 64) if h == 0 else (lane >= 64)
            other = 64 if h == 0 else 0
            qh = jnp.where(mine, q, jnp.where(lane == other, one, zero))
            kh = jnp.where(mine, k, jnp.where(lane == other, key_bias, zero))
            sc = dot_nt(qh, kh)
            if same:
                sc = jnp.where(tri, sc, NEG)
            m = jnp.max(sc, axis=-1, keepdims=True)
            e = jnp.exp(sc - m)
            l = jnp.sum(e, axis=-1, keepdims=True)
            outs.append(dot(e.astype(BF), v) * (1.0 / l))
            lses.append(m + jnp.log(l))
        o_ref[:, pl.ds(at, 128)] = jnp.where(lane < 64, outs[0], outs[1]).astype(BF)
        lse_ref[:, pl.ds(at, 128)] = jnp.where(lane < 64, lses[1], lses[0])
        return 0
    lax.fori_loop(0, d // 128, pair, 0)
    u = res_ref[...].astype(F32) + dot(o_ref[...], wo_ref[...]) + bias_ref[2:3, :]
    xhat, r, n = norm_forward(u, gain_ref[0:1, :], bias_ref[3:4, :])
    xhat_ref[...] = xhat
    r_ref[...] = jnp.broadcast_to(r, r_ref.shape)
    n_ref[...] = n

def attn_fwd(xq, xkv, res, wqkv, wo, bias, gain, length):
    s, d = xq.shape
    same = xkv is None
    if same:
        xkv = xq
    else:
        wo = gain
    vm = pl.BlockSpec(memory_space=pltpu.VMEM)
    sm = pl.BlockSpec(memory_space=pltpu.SMEM)
    return pl.pallas_call(
        functools.partial(attn_fwd_kernel, same),
        out_shape=(jax.ShapeDtypeStruct((s, 3 * d), BF), jax.ShapeDtypeStruct((s, d), BF), jax.ShapeDtypeStruct((s, d), F32),
                   jax.ShapeDtypeStruct((s, d), F32), jax.ShapeDtypeStruct((s, 128), F32), jax.ShapeDtypeStruct((s, d), F32)),
        in_specs=[sm] + [vm] * 7, out_specs=(vm,) * 6,
        compiler_params=pltpu.CompilerParams(vmem_limit_bytes=60 << 20),
    )(length.reshape(1, 1), xq, xkv, res, wqkv, wo, bias, gain)

def norm_backward(dn, xhat, r, gain):
    h = dn * gain
    return r * (h - jnp.mean(h, axis=-1, keepdims=True) - xhat * jnp.mean(h * xhat, axis=-1, keepdims=True))

def attn_bwd_body(same, between, len_ref, dn_ref, qkv_ref, o_ref, lse_ref, xhat_ref, r_ref, wqkv_ref, wo_ref, gain_ref,
                  dres_ref, dqkv_ref, dt_ref, dkvx_ref, sums_ref, do_ref, dq_ref):
    s, d = dn_ref.shape
    if not same:
        wo_ref = wqkv_ref.at[:, 3 * d :]
    dn = dn_ref[...]
    xhat = xhat_ref[...]
    du = norm_backward(dn, xhat, r_ref[:, :1], gain_ref[0:1, :])
    dt = du.astype(BF)
    dt_ref[...] = dt
    sums_ref[2:3, :] = jnp.sum(dt.astype(F32), axis=0, keepdims=True)
    sums_ref[3:4, :] = jnp.sum(dn, axis=0, keepdims=True)
    sums_ref[4:5, :] = jnp.sum(dn * xhat, axis=0, keepdims=True)
    dres_ref[...] = du
    do_ref[...] = dot_nt(dt, wo_ref[...]).astype(BF)
    length = len_ref[0, 0]
    lane = lanes(s)
    row = lax.broadcasted_iota(jnp.int32, (s, 128), 0)
    key_bias = jnp.where(row < length, 0.0, NEG).astype(BF)
    if same:
        tri = lax.broadcasted_iota(jnp.int32, (s, s), 0) <= lax.broadcasted_iota(jnp.int32, (s, s), 1) + causal_shift(s)
    one = jnp.ones((s, 128), BF)
    zero = jnp.zeros((s, 128), BF)

    def place(base, mine, other, extra):
        out = zero
        for j, val in enumerate(extra):
            out = jnp.where(lane == other + j, val, out)
        return jnp.where(mine, base, out)

    def pair(p, _):
        between(p)
        at = pl.multiple_of(p * 128, 128)
        q = qkv_ref[:, pl.ds(at, 128)] * jnp.asarray(0.125, BF)
        k = qkv_ref[:, pl.ds(d + at, 128)]
        v = qkv_ref[:, pl.ds(2 * d + at, 128)]
        do = do_ref[:, pl.ds(at, 128)]
        lse3 = split3(-lse_ref[:, pl.ds(at, 128)])
        prod = do.astype(F32) * o_ref[:, pl.ds(at, 128)].astype(F32)
        dq, dk, dv = [], [], []
        for h in range(2):
            mine = (lane < 64) if h == 0 else (lane >= 64)
            other = 64 if h == 0 else 0
            inner = jnp.broadcast_to(jnp.sum(jnp.where(mine, prod, 0.0), axis=-1, keepdims=True), (s, 128))
            qh = place(q, mine, other, (*lse3, one))
            kh = place(k, mine, other, (one, one, one, key_bias))
            doh = place(do, mine, other, split3(-inner))
            vh = place(v, mine, other, (one, one, one))
            st = dot_nt(kh, qh)
            if same:
                st = jnp.where(tri, st, NEG)
            pt = jnp.exp(st)
            dst = (pt * dot_nt(vh, doh)).astype(BF)
            dv.append(dot(pt.astype(BF), do))
            dk.append(dot(dst, q))
            dq.append(dot_tn(k, dst))
        m1 = lane < 64
        dq_ref[...] = jnp.where(lax.broadcasted_iota(jnp.int32, (128, s), 0) < 64, dq[0], dq[1])
        dqkv_ref[:, pl.ds(at, 128)] = (dq_ref[...].T * 0.125).astype(BF)
        dqkv_ref[:, pl.ds(d + at, 128)] = jnp.where(m1, dk[0], dk[1]).astype(BF)
        dqkv_ref[:, pl.ds(2 * d + at, 128)] = jnp.where(m1, dv[0], dv[1]).astype(BF)
        return 0
    lax.fori_loop(0, d // 128, pair, 0)
    if same:
        dres_ref[...] += dot_nt(dqkv_ref[...], wqkv_ref[...])
    else:
        dres_ref[...] += dot_nt(dqkv_ref[:, :d], wqkv_ref[:, :d])
        dkvx_ref[...] = dot_nt(dqkv_ref[:, d:], wqkv_ref[:, d:3*d]).astype(BF)
    sums_ref[0:1, :] = jnp.sum(dqkv_ref[:, :d].astype(F32), axis=0, keepdims=True)
    sums_ref[1:2, :] = jnp.sum(dqkv_ref[:, 2*d:].astype(F32), axis=0, keepdims=True)
    sums_ref[5:8, :] = jnp.zeros((3, d), F32)

def attn_bwd_kernel(same, *refs):
    attn_bwd_body(same, lambda p: None, *refs)


def attn_bwd(dn, saved, wqkv, wo, gain, length, same):
    qkv, o, lse, xhat, r = saved
    s, d = dn.shape
    if not same:
        wo = gain
    vm = pl.BlockSpec(memory_space=pltpu.VMEM)
    sm = pl.BlockSpec(memory_space=pltpu.SMEM)
    return pl.pallas_call(
        functools.partial(attn_bwd_kernel, same),
        out_shape=(jax.ShapeDtypeStruct((s, d), F32), jax.ShapeDtypeStruct((s, 3 * d), BF), jax.ShapeDtypeStruct((s, d), BF),
                   jax.ShapeDtypeStruct((8, 128) if same else (s, d), BF), jax.ShapeDtypeStruct((8, d), F32)),
        in_specs=[sm] + [vm] * 9, out_specs=(vm,) * 5,
        scratch_shapes=[pltpu.VMEM((s, d), BF), pltpu.VMEM((128, s), F32)],
        compiler_params=pltpu.CompilerParams(vmem_limit_bytes=60 << 20),
    )(length.reshape(1, 1), dn, qkv, o, lse, xhat, r, wqkv, wo, gain)

def gelu_parts(a):
    e = jnp.exp(-0.5 * a * a)
    t = 1.0 / (1.0 + 0.23164188624 * jnp.abs(a))
    tail = t * (0.127414796 + t * (-0.142248368 + t * (0.7107068705 + t * (-0.7265760135 + t * 0.5307027145)))) * e
    phi_cap = jnp.where(a < 0.0, tail, 1.0 - tail)
    return phi_cap, e * 0.3989422804014327

def ffn_fwd_kernel(chunk, n_ref, we_ref, wc_ref, be_ref, bias_ref, gain_ref,
                   y_ref, g_ref, gp_ref, xhat_ref, r_ref, acc_ref):
    s, d = n_ref.shape
    ff = we_ref.shape[1]
    low = n_ref[...].astype(BF)
    acc_ref[...] = n_ref[...] + bias_ref[4:5, :]

    def step(c, _):
        at = pl.multiple_of(c * chunk, chunk)
        a = dot(low, we_ref[:, pl.ds(at, chunk)]) + be_ref[:, pl.ds(at, chunk)]
        cap, dens = gelu_parts(a)
        g = (a * cap).astype(BF)
        g_ref[:, pl.ds(at, chunk)] = g
        gp_ref[:, pl.ds(at, chunk)] = (cap + a * dens).astype(BF)
        acc_ref[...] += dot(g, wc_ref[pl.ds(at, chunk), :])
        return 0
    lax.fori_loop(0, ff // chunk, step, 0)
    xhat, r, y = norm_forward(acc_ref[...], gain_ref[1:2, :], bias_ref[5:6, :])
    xhat_ref[...] = xhat
    r_ref[...] = jnp.broadcast_to(r, r_ref.shape)
    y_ref[...] = y.astype(BF)

def ffn_fwd(n, we, wc, be, bias, gain, chunk=512):
    s, d = n.shape
    ff = we.shape[1]
    vm = pl.BlockSpec(memory_space=pltpu.VMEM)
    return pl.pallas_call(
        functools.partial(ffn_fwd_kernel, chunk),
        out_shape=(jax.ShapeDtypeStruct((s, d), BF), jax.ShapeDtypeStruct((s, ff), BF), jax.ShapeDtypeStruct((s, ff), BF),
                   jax.ShapeDtypeStruct((s, d), F32), jax.ShapeDtypeStruct((s, 128), F32)),
        in_specs=[vm] * 6, out_specs=(vm,) * 5,
        scratch_shapes=[pltpu.VMEM((s, d), F32)],
        compiler_params=pltpu.CompilerParams(vmem_limit_bytes=60 << 20),
    )(n, we, wc, be.reshape(1, ff), bias, gain)

def ffn_bwd_kernel(chunk, extra, len_ref, cot_ref, dm_ref, gp_ref, xhat_ref, r_ref, we_ref, wc_ref, gain_ref,
                   dn_ref, da_ref, dt_ref, sums_ref, sume_ref):
    s, d = cot_ref.shape
    ff = we_ref.shape[1]
    row = lax.broadcasted_iota(jnp.int32, (s, 1), 0)
    dy = jnp.where(row < len_ref[0, 0], cot_ref[...].astype(F32), 0.0)
    if extra:
        dy = dy + dm_ref[...].astype(F32)
    xhat = xhat_ref[...]
    du = norm_backward(dy, xhat, r_ref[:, :1], gain_ref[1:2, :])
    dt = du.astype(BF)
    dt_ref[...] = dt
    sums_ref[0:1, :] = jnp.sum(dt.astype(F32), axis=0, keepdims=True)
    sums_ref[1:2, :] = jnp.sum(dy, axis=0, keepdims=True)
    sums_ref[2:3, :] = jnp.sum(dy * xhat, axis=0, keepdims=True)
    sums_ref[3:8, :] = jnp.zeros((5, d), F32)
    dn_ref[...] = du

    def step(c, _):
        at = pl.multiple_of(c * chunk, chunk)
        dg = dot_nt(dt_ref[...], wc_ref[pl.ds(at, chunk), :])
        da = (dg * gp_ref[:, pl.ds(at, chunk)].astype(F32)).astype(BF)
        da_ref[:, pl.ds(at, chunk)] = da
        sume_ref[:, pl.ds(at, chunk)] = jnp.sum(da.astype(F32), axis=0, keepdims=True)
        dn_ref[...] += dot_nt(da, we_ref[:, pl.ds(at, chunk)])
        return 0
    lax.fori_loop(0, ff // chunk, step, 0)

def ffn_bwd(cot, dm, length, saved, we, wc, gain, chunk=512):
    gp, xhat, r = saved
    s, d = cot.shape
    ff = we.shape[1]
    extra = dm is not None
    vm = pl.BlockSpec(memory_space=pltpu.VMEM)
    sm = pl.BlockSpec(memory_space=pltpu.SMEM)
    return pl.pallas_call(
        functools.partial(ffn_bwd_kernel, chunk, extra),
        out_shape=(jax.ShapeDtypeStruct((s, d), F32), jax.ShapeDtypeStruct((s, ff), BF), jax.ShapeDtypeStruct((s, d), BF),
                   jax.ShapeDtypeStruct((8, d), F32), jax.ShapeDtypeStruct((1, ff), F32)),
        in_specs=[sm] + [vm] * 8, out_specs=(vm,) * 5,
        compiler_params=pltpu.CompilerParams(vmem_limit_bytes=60 << 20),
    )(length.reshape(1, 1), cot, dm if extra else cot, gp, xhat, r, we, wc, gain)

MESH = pl.DeviceIdType.MESH
LAG = 2


def store_rows(total, out_ref):
    blocks, shards, rows, width = out_ref.shape
    halves = total.shape[1] // width
    groups = blocks // halves
    for k in range(shards):
        for j in range(groups):
            at = (k * groups + j) * rows
            for h in range(halves):
                out_ref[j * halves + h, k] = total[at : at + rows, h * width : (h + 1) * width]


def product(xs, dys):
    total = None
    for x, dy in zip(xs, dys):
        part = dot_tn(x[...].astype(BF), dy[...].astype(BF))
        total = part if total is None else total + part
    return total.astype(BF)


def wgrad_columns_kernel(n, *refs):
    total = product(refs[:n], refs[n : 2 * n])
    out_ref = refs[2 * n]
    rows, width = out_ref.shape[-2:]
    for h in range(out_ref.shape[0]):
        out_ref[h] = total[:, h * width : (h + 1) * width].reshape(-1, rows, width)


def wgrad_rows_kernel(n, *refs):
    store_rows(product(refs[:n], refs[n : 2 * n]), refs[2 * n])


def wgrad_columns(xs, dys, shards):
    sizes = [x.shape[0] for x in xs]
    k, n = xs[0].shape[1], dys[0].shape[1]
    width = k // 2
    return pl.pallas_call(
        functools.partial(wgrad_columns_kernel, len(xs)),
        out_shape=jax.ShapeDtypeStruct((n // width, shards, k // shards, width), BF),
        grid=(n // k,),
        in_specs=[pl.BlockSpec((s, k), lambda i: (0, 0)) for s in sizes]
        + [pl.BlockSpec((s, k), lambda i: (0, i)) for s in sizes],
        out_specs=pl.BlockSpec((2, shards, k // shards, width), lambda i: (i, 0, 0, 0)),
        compiler_params=pltpu.CompilerParams(vmem_limit_bytes=60 << 20),
    )(*xs, *dys)


def wgrad_rows(xs, dys, shards):
    sizes = [x.shape[0] for x in xs]
    n, k = xs[0].shape[1], dys[0].shape[1]
    width, rows = k // 2, k // shards
    groups = n // k
    return pl.pallas_call(
        functools.partial(wgrad_rows_kernel, len(xs)),
        out_shape=jax.ShapeDtypeStruct((2 * groups, shards, rows, width), BF),
        grid=(n // k,),
        in_specs=[pl.BlockSpec((s, k), lambda i: (0, i)) for s in sizes]
        + [pl.BlockSpec((s, k), lambda i: (0, 0)) for s in sizes],
        out_specs=pl.BlockSpec((2 * groups, shards // groups, rows, width), lambda i: (0, i, 0, 0)),
        compiler_params=pltpu.CompilerParams(vmem_limit_bytes=60 << 20),
    )(*xs, *dys)


def wgrad_cross_kernel(n, *refs):
    dqkv, dt, n1, mem, mixed = (refs[j * n : (j + 1) * n] for j in range(5))
    first_ref, second_ref = refs[5 * n :]
    i = pl.program_id(0)
    for at, xs, dys, out_ref in (
        (0, dqkv, n1, first_ref),
        (1, dqkv, mem, first_ref),
        (2, dqkv, mem, second_ref),
        (3, dt, mixed, second_ref),
    ):

        @pl.when(i == at)
        def _():
            store_rows(product(xs, dys), out_ref)


def wgrad_cross(dqkv, dt, n1, mem, mixed, shards):
    sizes = [x.shape[0] for x in dt]
    k = dt[0].shape[1]
    width, rows = k // 2, k // shards
    out = jax.ShapeDtypeStruct((4, shards, rows, width), BF)
    whole = [pl.BlockSpec((s, k), lambda i: (0, 0)) for s in sizes]
    return pl.pallas_call(
        functools.partial(wgrad_cross_kernel, len(sizes)),
        out_shape=(out, out),
        grid=(4,),
        in_specs=[pl.BlockSpec((s, k), lambda i: (0, jnp.minimum(i, 2))) for s in sizes] + whole * 4,
        out_specs=(
            pl.BlockSpec((4, shards // 2, rows, width), lambda i: (0, jnp.minimum(i, 1), 0, 0)),
            pl.BlockSpec((4, shards // 2, rows, width), lambda i: (0, jnp.maximum(i - 2, 0), 0, 0)),
        ),
        compiler_params=pltpu.CompilerParams(vmem_limit_bytes=60 << 20),
    )(*dqkv, *dt, *n1, *mem, *mixed)


def reduce_kernel(counts, *refs):
    (len_ref, dn_ref, qkv_ref, o_ref, lse_ref, xhat_ref, r_ref, wqkv_ref, wo_ref, gain_ref) = refs[:10]
    (x0_ref, x_ref, dqkv0_ref, o0_ref, dt0_ref, expand, contract, cross_first, cross_second) = refs[10:19]
    (ssum_ref, fsum_ref, esum_ref, csum_ref) = refs[19:23]
    (dres_ref, in_ref, out_ref, expand_ref, contract_ref, cross_ref, vsum_ref) = refs[23:30]
    (dqkv_ref, dt_ref, do_ref, dq_ref, sums_ref, made, own, r0, r1, r2, r3, vbuf, vrecv) = refs[30:43]
    send_sem, recv_sem, local_sem, vsend_sem, vrecv_sem = refs[43:]
    d = dn_ref.shape[1]
    n_ffn, n_in, n_out, n_cross = 2 * counts[0], counts[1], counts[2], counts[3]
    blocks = n_ffn + n_in + n_out + n_cross
    rows, width = own.shape[-2:]
    second = lax.axis_index("section") == 1
    me = lax.axis_index("dp")
    c, y, zl, zh = me % 2, (me // 2) % 2, (me // 4) % 2, me // 8
    mates = (me + 1 - 2 * c, me + 2 - 4 * y, me + 4 - 8 * zl, me + 8 - 16 * zh)
    barrier = pltpu.get_barrier_semaphore()
    for mate in mates:
        pl.semaphore_signal(barrier, inc=1, device_id={"dp": mate}, device_id_type=MESH)
    pl.semaphore_wait(barrier, 4)
    order = ((0, 1, 2, 3), (0, 2, 3, 1))

    def remote(src, dst, stage, b, color):
        return pltpu.make_async_remote_copy(
            src_ref=src,
            dst_ref=dst,
            send_sem=send_sem.at[stage, b],
            recv_sem=recv_sem.at[stage, b],
            device_id={"dp": mates[order[color][stage]]},
            device_id_type=MESH,
        )

    def first_copy(part, at, b, color):
        return remote(part.at[at, :, :, :, 1 - c], r0.at[b], 0, b, color)

    def local_copy(part, at, b):
        return pltpu.make_async_copy(part.at[at, :, :, :, c], own.at[b], local_sem.at[b])

    def copy_of(stage, b, color):
        if color == 0:
            src = (own.at[b, :, :, 1 - y], own.at[b, :, 1 - zl, y], own.at[b, 1 - zh, zl, y])
        else:
            src = (own.at[b, :, 1 - zl], own.at[b, 1 - zh, zl], own.at[b, zh, zl, 1 - y])
        return remote(src[stage - 1], (r1, r2, r3)[stage - 1].at[b], stage, b, color)

    def add(left, right):
        return (left.astype(F32) + right.astype(F32)).astype(BF)

    def column(at):
        return pl.ds(pl.multiple_of(at * width, 128), width)

    def put_columns(ref, at, value):
        ref[:, column(at)] = value

    def put_groups(ref, at, value):
        ref[pl.ds(pl.multiple_of((at // 2) * rows, 8), rows), column(at % 2)] = value

    plan = (
        (((expand, None),), counts[0], put_columns, expand_ref),
        (((contract, None),), counts[0], put_groups, contract_ref),
        (((made, None),), n_in, put_columns, in_ref),
        (((made, None),), n_out, put_columns, out_ref),
        (((cross_first, jnp.logical_not(second)), (cross_second, second)), n_cross, put_groups, cross_ref),
    )

    def each(b, visit):
        low = 0
        for sources, count, put, target in plan:
            offset = n_ffn if sources[0][0] is made else low
            inside = (b >= low) & (b < low + count)
            visit(inside, sources, b - offset, put, target, b - low)
            low += count

    def settle(stage, b, color):
        if stage == 0:
            first_copy(expand, 0, b, color).wait()
            local_copy(expand, 0, b).wait()
            own[b] = add(own[b], r0[b])
            return
        copy_of(stage, b, color).wait()
        if stage == 1:
            if color == 0:
                own[b, :, :, y] = add(own[b, :, :, y], r1[b])
            else:
                own[b, :, zl] = add(own[b, :, zl], r1[b])
        elif stage == 2:
            if color == 0:
                own[b, :, zl, y] = add(own[b, :, zl, y], r2[b])
            else:
                own[b, zh, zl] = add(own[b, zh, zl], r2[b])
        else:
            total = own[b, zh, zl, y].astype(F32) + r3[b].astype(F32)

            def finish(inside, sources, at, put, target, place):
                @pl.when(inside)
                def _():
                    put(target, place, total)

            each(b, finish)

    def vcopy(j):
        return pltpu.make_async_remote_copy(
            src_ref=vbuf.at[j],
            dst_ref=vrecv.at[j],
            send_sem=vsend_sem.at[j],
            recv_sem=vrecv_sem.at[j],
            device_id={"dp": mates[j]},
            device_id_type=MESH,
        )

    turned = blocks // 7
    half = turned // 2
    steps = blocks - turned
    gap = steps // turned

    def advance(stage, b, color):
        if stage == 0:

            def launch(inside, sources, at, put, target, place):
                for part, here in sources:

                    @pl.when(inside if here is None else inside & here)
                    def _():
                        first_copy(part, at, b, color).start()
                        local_copy(part, at, b).start()

            each(b, launch)
            return
        settle(stage - 1, b, color)
        if stage < 4:
            copy_of(stage, b, color).start()

    def step(it, _):
        for stage in range(5):
            at = it - LAG * stage

            @pl.when((at >= 0) & (at < steps))
            def _():
                advance(stage, at + jnp.where(at >= n_ffn - half, half, 0), 0)

            @pl.when((at >= 0) & (at < turned * gap) & (at % gap == 1))
            def _():
                j = at // gap
                advance(stage, jnp.where(j < half, n_ffn - half, blocks - turned) + j, 1)

        return 0

    pairs = d // 128
    early = n_ffn - half

    def some(low, high):
        lax.fori_loop(low, high, step, 0)

    beside = early - 5
    attn_bwd_body(
        True, lambda p: some(p * beside // pairs, (p + 1) * beside // pairs),
        len_ref, dn_ref, qkv_ref, o_ref, lse_ref, xhat_ref, r_ref, wqkv_ref, wo_ref, gain_ref,
        dres_ref, dqkv_ref, dt_ref, None, sums_ref, do_ref, dq_ref,
    )
    vbuf[0, 0:4] = sums_ref[0:4, :] + ssum_ref[0:4, :]
    vbuf[0, 4:6] = fsum_ref[0:2, :]
    vbuf[0, 6:7] = sums_ref[4:5, :] + ssum_ref[4:5, :]
    vbuf[0, 7:8] = fsum_ref[2:3, :]
    count = esum_ref.shape[1] // d
    for j in range(count):
        vbuf[0, 8 + j : 9 + j] = esum_ref[:, j * d : (j + 1) * d]
    vbuf[0, 8 + count : 13 + count] = csum_ref[0:5, :]
    vbuf[0, 13 + count :] = jnp.zeros((vbuf.shape[1] - 13 - count, d), F32)
    some(beside, beside + 1)

    def keep(block, total):
        for h in range(2):
            made[block + h] = total[:, h * width : (h + 1) * width].reshape(made.shape[1:]).astype(BF)

    def weight(i, _):
        at = pl.ds(pl.multiple_of(i * d, 128), d)
        keep(2 * i, dot_tn(x0_ref[...], dqkv0_ref[:, at]) + dot_tn(x_ref[...], dqkv_ref[:, at]))
        step(beside + 1 + i, 0)
        return 0

    lax.fori_loop(0, n_in // 2, weight, 0)
    keep(n_in, dot_tn(o0_ref[...], dt0_ref[...]) + dot_tn(o_ref[...], dt_ref[...]))
    begin = beside + 1 + n_in // 2
    vcopy(0).start()

    def rest(it, _):
        step(it, 0)
        for j in range(4):

            @pl.when(it == begin + LAG * (j + 1))
            def _():
                vcopy(j).wait()
                vbuf[j + 1] = vbuf[j] + vrecv[j]
                if j < 3:
                    vcopy(j + 1).start()

        return 0

    lax.fori_loop(begin, steps + 4 * LAG, rest, 0)
    vsum_ref[...] = vbuf[4]


def reduce_scatter(length, dn, saved, w_in, w_out, gain, x0, x1, dqkv0, o0, dt0, parts, sums):
    s, d = dn.shape
    rows, width = parts[0].shape[-2:]
    n_in, n_out = dqkv0.shape[1] // width, dt0.shape[1] // width
    counts = (parts[0].shape[0], n_in, n_out, parts[2].shape[0])
    blocks = 2 * counts[0] + sum(counts[1:])
    parts = [part.reshape(part.shape[0], 2, 2, 2, 2, rows, width) for part in parts]
    ff = sums[2].shape[1]
    vec = (24, d)
    vm = pl.BlockSpec(memory_space=pltpu.VMEM)
    sm = pl.BlockSpec(memory_space=pltpu.SMEM)
    shapes = ((s, d), (rows, n_in * width), (rows, n_out * width), (rows, counts[0] * width),
              (counts[0] // 2 * rows, d), (counts[3] // 2 * rows, d), vec)
    return pl.pallas_call(
        functools.partial(reduce_kernel, counts),
        out_shape=tuple(jax.ShapeDtypeStruct(shape, F32) for shape in shapes),
        in_specs=[sm] + [vm] * 14 + [pl.BlockSpec(memory_space=pl.ANY)] * 4 + [vm] * 4,
        out_specs=(vm,) * 7,
        scratch_shapes=[
            pltpu.VMEM((s, 3 * d), BF),
            pltpu.VMEM((s, d), BF),
            pltpu.VMEM((s, d), BF),
            pltpu.VMEM((128, s), F32),
            pltpu.VMEM((8, d), F32),
            pltpu.VMEM((n_in + n_out, 2, 2, 2, 2, rows, width), BF),
            pltpu.VMEM((blocks, 2, 2, 2, rows, width), BF),
            pltpu.VMEM((blocks, 2, 2, 2, rows, width), BF),
            pltpu.VMEM((blocks, 2, 2, rows, width), BF),
            pltpu.VMEM((blocks, 2, rows, width), BF),
            pltpu.VMEM((blocks, rows, width), BF),
            pltpu.VMEM((5, *vec), F32),
            pltpu.VMEM((4, *vec), F32),
            pltpu.SemaphoreType.DMA((4, blocks)),
            pltpu.SemaphoreType.DMA((4, blocks)),
            pltpu.SemaphoreType.DMA((blocks,)),
            pltpu.SemaphoreType.DMA((4,)),
            pltpu.SemaphoreType.DMA((4,)),
        ],
        compiler_params=pltpu.CompilerParams(collective_id=0, has_side_effects=True, vmem_limit_bytes=67043328),
    )(length.reshape(1, 1), dn, *saved, w_in, w_out, gain, x0, x1, dqkv0, o0, dt0, *parts, *sums)


def shards(
    inputs_long,
    inputs_short,
    cotangent_long,
    cotangent_short,
    lengths_long,
    lengths_short,
    self_in_weight,
    self_out_weight,
    expand_weight,
    contract_weight,
    expand_bias,
    layer_biases,
    layer_gains,
    cross_weight,
    cross_biases,
    cross_gain,
):
    decoder = lax.axis_index("section") == 1
    d = inputs_long.shape[-1]
    ff = expand_weight.shape[2]
    w_in, w_out, w_e, w_c = self_in_weight[0], self_out_weight[0], expand_weight[0], contract_weight[0]
    b_e, bias, gain = expand_bias[0], layer_biases[0], layer_gains[0]
    c_gain = cross_gain.reshape(1, d)

    xs = (inputs_short[0, 0], inputs_long[0, 0])
    cots = (cotangent_short[0, 0], cotangent_long[0, 0])
    source = (lengths_short[0, 0], lengths_long[0, 0])
    target = (lengths_short[1, 0], lengths_long[1, 0])
    sizes = tuple(x.shape[0] for x in xs)

    own = tuple(jnp.where(decoder, t, o) for t, o in zip(target, source))

    def attend(i):
        x = xs[i]
        return attn_fwd(x, None, x, w_in, w_out, bias, gain, own[i])

    def encode_ffn(i, n):
        s = sizes[i]

        def decode():
            return blank(((s, d), BF), ((s, ff), BF), ((s, ff), BF), ((s, d), F32), ((s, 128), F32))

        return lax.cond(decoder, decode, lambda: ffn_fwd(n, w_e, w_c, b_e, bias, gain))

    def send(value, steps):
        return lax.ppermute(value, "section", [(0, 1)] if steps > 0 else [(1, 0)])

    def cross(i, memory, n1):
        s = sizes[i]

        def encode():
            return blank(
                ((s, 3 * d), BF), ((s, d), BF), ((s, d), F32), ((s, d), F32), ((s, 128), F32), ((s, d), F32)
            )

        def decode():
            return attn_fwd(n1, memory, n1, cross_weight, None, cross_biases, c_gain, source[i])

        return lax.cond(decoder, decode, encode)

    def turn(i, out):
        s = sizes[i]

        def decode():
            y, g, gp, xhat, r = ffn_fwd(out[5], w_e, w_c, b_e, bias, gain)
            fb = ffn_bwd(cots[i], None, target[i], (gp, xhat, r), w_e, w_c, gain)
            ab = attn_bwd(fb[0], out[:5], cross_weight, None, c_gain, source[i], False)
            return (g, fb[1], fb[2], ab[1], ab[2]), ab[0], ab[3], y, (fb[3], fb[4], ab[4])

        def encode():
            out = blank(
                ((s, ff), BF),
                ((s, ff), BF),
                ((s, d), BF),
                ((s, 3 * d), BF),
                ((s, d), BF),
                ((s, d), F32),
                ((s, d), BF),
                ((s, d), BF),
                ((8, d), F32),
                ((1, ff), F32),
                ((8, d), F32),
            )
            return tuple(out[:5]), out[5], out[6], out[7], tuple(out[8:])

        return lax.cond(decoder, decode, encode)

    att0 = attend(0)
    ffn0 = encode_ffn(0, att0[5])
    mem0 = send(ffn0[0], 1)
    x_long, _ = lax.optimization_barrier((xs[1], ffn0[0]))
    xs = (xs[0], x_long)
    att1 = attend(1)
    n_long, mem0 = lax.optimization_barrier((att1[5], mem0))
    ffn1 = encode_ffn(1, n_long)
    mem1 = send(ffn1[0], 1)
    n_short, _ = lax.optimization_barrier((att0[5], ffn1[0]))
    out0 = cross(0, mem0, n_short)
    keep0, dn0, dm0, y0, sums0 = turn(0, out0)
    back0 = send(dm0, -1)
    n_long, _ = lax.optimization_barrier((att1[5], dm0))
    out1 = cross(1, mem1, n_long)
    n_long, back0 = lax.optimization_barrier((out1[5], back0))
    out1 = (*out1[:5], n_long)
    keep1, dn1, dm1, y1, sums1 = turn(1, out1)
    back1 = send(dm1, -1)
    dp = lax.axis_size("dp")
    staged = dp == 16 and d % (16 * dp) == 0

    def cross_grads():
        n1, mem = (att0[5], att1[5]), (mem0, mem1)
        dqkv, dt = ((keep0[j], keep1[j]) for j in (3, 4))
        mixed = (out0[1], out1[1])
        if staged:
            return wgrad_cross(dqkv, dt, n1, mem, mixed, dp)
        joint = jnp.concatenate(dqkv, 0)
        low = jnp.concatenate(n1, 0).astype(BF)
        mem = jnp.concatenate(mem, 0)
        rows = (
            dot_tn(joint[:, :d], low),
            dot_tn(joint[:, d : 2 * d], mem),
            dot_tn(joint[:, 2 * d :], mem),
            dot_tn(jnp.concatenate(dt, 0), jnp.concatenate(mixed, 0)),
        )
        return tuple(jnp.concatenate(rows[j : j + 2], 0).astype(BF) for j in (0, 2))

    def cross_blank():
        shape = (4, dp, d // dp, d // 2) if staged else (2 * d, d)
        return tuple(blank((shape, BF), (shape, BF)))

    cross_sums = sums0[2] + sums1[2]
    cross_first, cross_second = lax.cond(decoder, cross_grads, cross_blank)
    back0, _ = lax.optimization_barrier((back0, cross_first))
    dn0, *enc0 = lax.cond(
        decoder,
        lambda: (dn0, *blank(((sizes[0], ff), BF), ((sizes[0], d), BF), ((8, d), F32), ((1, ff), F32))),
        lambda: tuple(ffn_bwd(cots[0], back0, source[0], ffn0[2:], w_e, w_c, gain)),
    )
    self0 = attn_bwd(dn0, att0[:5], w_in, w_out, gain, own[0], True)
    back1, cross_first, cross_sent, _ = lax.optimization_barrier((back1, cross_first, send(cross_sums, -1), self0[0]))
    cross_first = send(cross_first, -1)
    cross_rows = jnp.where(decoder, cross_sums, cross_sent)

    def plain(left, right):
        left, right = (jnp.concatenate([e.astype(BF) for e in side], 0) for side in (left, right))
        return dot_tn(left, right).astype(BF)

    def ffn_grads(n, da, g, dt):
        if staged:
            return wgrad_columns(n, da, dp), wgrad_rows(g, dt, dp)
        return plain(n, da), plain(g, dt)

    def decode_last():
        grads = ffn_grads((out0[5], out1[5]), (keep0[1], keep1[1]), (keep0[0], keep1[0]), (keep0[2], keep1[2]))
        return dn1, *grads, sums0[0] + sums1[0], sums0[1] + sums1[1]

    def encode_last():
        dn, da, dt, sums, sum_e = ffn_bwd(cots[1], back1, source[1], ffn1[2:], w_e, w_c, gain)
        grads = ffn_grads((att0[5], att1[5]), (enc0[0], da), (ffn0[1], ffn1[1]), (enc0[1], dt))
        return dn, *grads, enc0[2] + sums, enc0[3] + sum_e

    dn1, g_expand, g_contract, ffn_sums, sum_e = lax.cond(decoder, decode_last, encode_last)
    if staged:
        dx1, *big, rows = reduce_scatter(
            own[1], dn1, att1[:5], w_in, w_out, gain, xs[0], xs[1], self0[1], att0[1], self0[2],
            (g_expand, g_contract, cross_first, cross_second), (self0[4], ffn_sums, sum_e, cross_rows),
        )
    else:
        self1 = attn_bwd(dn1, att1[:5], w_in, w_out, gain, own[1], True)
        dx1 = self1[0]
        self_sums = self0[4] + self1[4]
        rows = [self_sums[0:4], ffn_sums[0:2], self_sums[4:5], ffn_sums[2:3], sum_e.reshape(ff // d, d), cross_rows[0:5]]
        rows = lax.psum(jnp.concatenate(rows, 0), "dp")
        cross_mine = jnp.where(decoder, cross_second, cross_first)
        in_grad = plain(xs, (self0[1], self1[1]))
        out_grad = plain((att0[1], att1[1]), (self0[2], self1[2]))
        big = [
            lax.psum_scatter(part, "dp", scatter_dimension=0, tiled=True).astype(F32)
            for part in (in_grad, out_grad, g_expand, g_contract, cross_mine)
        ]
    count = 8 + ff // d
    me = lax.axis_index("dp")
    piece = lax.dynamic_slice_in_dim(rows[:8], me * (d // dp), d // dp, 1)
    e_piece = lax.dynamic_slice_in_dim(rows[8:count].reshape(1, ff), me * (ff // dp), ff // dp, 1)
    outs = [jnp.where(decoder, y, e)[None, None] for y, e in ((y0, ffn0[0]), (y1, ffn1[0]))]
    return (
        outs[1],
        outs[0],
        dx1[None, None],
        self0[0][None, None],
        big[0][None],
        big[1][None],
        big[2][None],
        big[3][None],
        e_piece,
        piece[None, :6],
        piece[None, 6:8],
        big[4].T,
        rows[count : count + 4],
        rows[count + 4],
    )


def solution(mesh):
    in_specs = (
        P("section", "dp", None, None),
        P("section", "dp", None, None),
        P("section", "dp", None, None),
        P("section", "dp", None, None),
        P(None, "dp"),
        P(None, "dp"),
        P("section", None, None),
        P("section", None, None),
        P("section", None, None),
        P("section", None, None),
        P("section", None),
        P("section", None, None),
        P("section", None, None),
        P(),
        P(),
        P(),
    )
    out_specs = (
        P("section", "dp", None, None),
        P("section", "dp", None, None),
        P("section", "dp", None, None),
        P("section", "dp", None, None),
        P("section", "dp", None),
        P("section", "dp", None),
        P("section", "dp", None),
        P("section", "dp", None),
        P("section", "dp"),
        P("section", None, "dp"),
        P("section", None, "dp"),
        P(None, ("section", "dp")),
        P(),
        P(),
    )
    return jax.shard_map(shards, mesh=mesh, in_specs=in_specs, out_specs=out_specs, check_vma=False)
```

```python
import functools
import jax
import jax.numpy as jnp
from jax import lax
from jax.experimental import pallas as pl
from jax.experimental.pallas import tpu as pltpu
from jax.sharding import PartitionSpec as P

BF, F32 = jnp.bfloat16, jnp.float32
NEG = -1e30
NT = (((1,), (1,)), ((), ()))
TN = (((0,), (0,)), ((), ()))

def dot(a, b):
    return jnp.dot(a, b, preferred_element_type=F32)
def dot_nt(a, b):
    return lax.dot_general(a, b, NT, preferred_element_type=F32)
def dot_tn(a, b):
    return lax.dot_general(a, b, TN, preferred_element_type=F32)

def lanes(rows):
    return lax.broadcasted_iota(jnp.int32, (rows, 128), 1)

def split3(v):
    hi = v.astype(BF)
    rest = v - hi.astype(F32)
    mid = rest.astype(BF)
    low = (rest - mid.astype(F32)).astype(BF)
    return hi, mid, low

def blank(*shapes):
    def nothing(*refs):
        pass

    return pl.pallas_call(
        nothing,
        out_shape=[jax.ShapeDtypeStruct(shape, kind) for shape, kind in shapes],
        out_specs=[pl.BlockSpec(memory_space=pl.ANY)] * len(shapes),
    )()


def norm_forward(u, gain, shift):
    mean = jnp.mean(u, axis=-1, keepdims=True)
    c = u - mean
    r = lax.rsqrt(jnp.mean(c * c, axis=-1, keepdims=True) + 1e-5)
    xhat = c * r
    return xhat, r, xhat * gain + shift

def causal_shift(size):
    return jnp.where(lax.axis_index("section") == 1, 0, size)


def attn_fwd_kernel(same, len_ref, xq_ref, xkv_ref, res_ref, wqkv_ref, wo_ref, bias_ref, gain_ref,
                    qkv_ref, o_ref, lse_ref, xhat_ref, r_ref, n_ref):
    s, d = xq_ref.shape
    if not same:
        wo_ref = wqkv_ref.at[:, 3 * d :]
    xq = xq_ref[...].astype(BF)
    xkv = xq if same else xkv_ref[...]
    qkv_ref[:, :d] = (dot(xq, wqkv_ref[:, :d]) + bias_ref[0:1, :]).astype(BF)
    qkv_ref[:, d:2*d] = dot(xkv, wqkv_ref[:, d:2*d]).astype(BF)
    qkv_ref[:, 2*d:] = (dot(xkv, wqkv_ref[:, 2*d:3*d]) + bias_ref[1:2, :]).astype(BF)
    length = len_ref[0, 0]
    lane = lanes(s)
    row = lax.broadcasted_iota(jnp.int32, (s, 128), 0)
    key_bias = jnp.where(row < length, 0.0, NEG).astype(BF)
    if same:
        tri = lax.broadcasted_iota(jnp.int32, (s, s), 1) <= lax.broadcasted_iota(jnp.int32, (s, s), 0) + causal_shift(s)
    one = jnp.ones((s, 128), BF)
    zero = jnp.zeros((s, 128), BF)

    def pair(p, _):
        at = pl.multiple_of(p * 128, 128)
        q = qkv_ref[:, pl.ds(at, 128)] * jnp.asarray(0.125, BF)
        k = qkv_ref[:, pl.ds(d + at, 128)]
        v = qkv_ref[:, pl.ds(2 * d + at, 128)]
        outs, lses = [], []
        for h in range(2):
            mine = (lane < 64) if h == 0 else (lane >= 64)
            other = 64 if h == 0 else 0
            qh = jnp.where(mine, q, jnp.where(lane == other, one, zero))
            kh = jnp.where(mine, k, jnp.where(lane == other, key_bias, zero))
            sc = dot_nt(qh, kh)
            if same:
                sc = jnp.where(tri, sc, NEG)
            m = jnp.max(sc, axis=-1, keepdims=True)
            e = jnp.exp(sc - m)
            l = jnp.sum(e, axis=-1, keepdims=True)
            outs.append(dot(e.astype(BF), v) * (1.0 / l))
            lses.append(m + jnp.log(l))
        o_ref[:, pl.ds(at, 128)] = jnp.where(lane < 64, outs[0], outs[1]).astype(BF)
        lse_ref[:, pl.ds(at, 128)] = jnp.where(lane < 64, lses[1], lses[0])
        return 0
    lax.fori_loop(0, d // 128, pair, 0)
    u = res_ref[...].astype(F32) + dot(o_ref[...], wo_ref[...]) + bias_ref[2:3, :]
    xhat, r, n = norm_forward(u, gain_ref[0:1, :], bias_ref[3:4, :])
    xhat_ref[...] = xhat
    r_ref[...] = jnp.broadcast_to(r, r_ref.shape)
    n_ref[...] = n

def attn_fwd(xq, xkv, res, wqkv, wo, bias, gain, length):
    s, d = xq.shape
    same = xkv is None
    if same:
        xkv = xq
    else:
        wo = gain
    vm = pl.BlockSpec(memory_space=pltpu.VMEM)
    sm = pl.BlockSpec(memory_space=pltpu.SMEM)
    return pl.pallas_call(
        functools.partial(attn_fwd_kernel, same),
        out_shape=(jax.ShapeDtypeStruct((s, 3 * d), BF), jax.ShapeDtypeStruct((s, d), BF), jax.ShapeDtypeStruct((s, d), F32),
                   jax.ShapeDtypeStruct((s, d), F32), jax.ShapeDtypeStruct((s, 128), F32), jax.ShapeDtypeStruct((s, d), F32)),
        in_specs=[sm] + [vm] * 7, out_specs=(vm,) * 6,
        compiler_params=pltpu.CompilerParams(vmem_limit_bytes=60 << 20),
    )(length.reshape(1, 1), xq, xkv, res, wqkv, wo, bias, gain)

def norm_backward(dn, xhat, r, gain):
    h = dn * gain
    return r * (h - jnp.mean(h, axis=-1, keepdims=True) - xhat * jnp.mean(h * xhat, axis=-1, keepdims=True))

def attn_bwd_body(same, between, len_ref, dn_ref, qkv_ref, o_ref, lse_ref, xhat_ref, r_ref, wqkv_ref, wo_ref, gain_ref,
                  dres_ref, dqkv_ref, dt_ref, dkvx_ref, sums_ref, do_ref, dq_ref):
    s, d = dn_ref.shape
    if not same:
        wo_ref = wqkv_ref.at[:, 3 * d :]
    dn = dn_ref[...]
    xhat = xhat_ref[...]
    du = norm_backward(dn, xhat, r_ref[:, :1], gain_ref[0:1, :])
    dt = du.astype(BF)
    dt_ref[...] = dt
    sums_ref[2:3, :] = jnp.sum(dt.astype(F32), axis=0, keepdims=True)
    sums_ref[3:4, :] = jnp.sum(dn, axis=0, keepdims=True)
    sums_ref[4:5, :] = jnp.sum(dn * xhat, axis=0, keepdims=True)
    dres_ref[...] = du
    do_ref[...] = dot_nt(dt, wo_ref[...]).astype(BF)
    length = len_ref[0, 0]
    lane = lanes(s)
    row = lax.broadcasted_iota(jnp.int32, (s, 128), 0)
    key_bias = jnp.where(row < length, 0.0, NEG).astype(BF)
    if same:
        tri = lax.broadcasted_iota(jnp.int32, (s, s), 0) <= lax.broadcasted_iota(jnp.int32, (s, s), 1) + causal_shift(s)
    one = jnp.ones((s, 128), BF)
    zero = jnp.zeros((s, 128), BF)

    def place(base, mine, other, extra):
        out = zero
        for j, val in enumerate(extra):
            out = jnp.where(lane == other + j, val, out)
        return jnp.where(mine, base, out)

    def pair(p, _):
        between(p)
        at = pl.multiple_of(p * 128, 128)
        q = qkv_ref[:, pl.ds(at, 128)] * jnp.asarray(0.125, BF)
        k = qkv_ref[:, pl.ds(d + at, 128)]
        v = qkv_ref[:, pl.ds(2 * d + at, 128)]
        do = do_ref[:, pl.ds(at, 128)]
        lse3 = split3(-lse_ref[:, pl.ds(at, 128)])
        prod = do.astype(F32) * o_ref[:, pl.ds(at, 128)].astype(F32)
        dq, dk, dv = [], [], []
        for h in range(2):
            mine = (lane < 64) if h == 0 else (lane >= 64)
            other = 64 if h == 0 else 0
            inner = jnp.broadcast_to(jnp.sum(jnp.where(mine, prod, 0.0), axis=-1, keepdims=True), (s, 128))
            qh = place(q, mine, other, (*lse3, one))
            kh = place(k, mine, other, (one, one, one, key_bias))
            doh = place(do, mine, other, split3(-inner))
            vh = place(v, mine, other, (one, one, one))
            st = dot_nt(kh, qh)
            if same:
                st = jnp.where(tri, st, NEG)
            pt = jnp.exp(st)
            dst = (pt * dot_nt(vh, doh)).astype(BF)
            dv.append(dot(pt.astype(BF), do))
            dk.append(dot(dst, q))
            dq.append(dot_tn(k, dst))
        m1 = lane < 64
        dq_ref[...] = jnp.where(lax.broadcasted_iota(jnp.int32, (128, s), 0) < 64, dq[0], dq[1])
        dqkv_ref[:, pl.ds(at, 128)] = (dq_ref[...].T * 0.125).astype(BF)
        dqkv_ref[:, pl.ds(d + at, 128)] = jnp.where(m1, dk[0], dk[1]).astype(BF)
        dqkv_ref[:, pl.ds(2 * d + at, 128)] = jnp.where(m1, dv[0], dv[1]).astype(BF)
        return 0
    lax.fori_loop(0, d // 128, pair, 0)
    if same:
        dres_ref[...] += dot_nt(dqkv_ref[...], wqkv_ref[...])
    else:
        dres_ref[...] += dot_nt(dqkv_ref[:, :d], wqkv_ref[:, :d])
        dkvx_ref[...] = dot_nt(dqkv_ref[:, d:], wqkv_ref[:, d:3*d]).astype(BF)
    sums_ref[0:1, :] = jnp.sum(dqkv_ref[:, :d].astype(F32), axis=0, keepdims=True)
    sums_ref[1:2, :] = jnp.sum(dqkv_ref[:, 2*d:].astype(F32), axis=0, keepdims=True)
    sums_ref[5:8, :] = jnp.zeros((3, d), F32)

def attn_bwd_kernel(same, *refs):
    attn_bwd_body(same, lambda p: None, *refs)


def attn_bwd(dn, saved, wqkv, wo, gain, length, same):
    qkv, o, lse, xhat, r = saved
    s, d = dn.shape
    if not same:
        wo = gain
    vm = pl.BlockSpec(memory_space=pltpu.VMEM)
    sm = pl.BlockSpec(memory_space=pltpu.SMEM)
    return pl.pallas_call(
        functools.partial(attn_bwd_kernel, same),
        out_shape=(jax.ShapeDtypeStruct((s, d), F32), jax.ShapeDtypeStruct((s, 3 * d), BF), jax.ShapeDtypeStruct((s, d), BF),
                   jax.ShapeDtypeStruct((8, 128) if same else (s, d), BF), jax.ShapeDtypeStruct((8, d), F32)),
        in_specs=[sm] + [vm] * 9, out_specs=(vm,) * 5,
        scratch_shapes=[pltpu.VMEM((s, d), BF), pltpu.VMEM((128, s), F32)],
        compiler_params=pltpu.CompilerParams(vmem_limit_bytes=60 << 20),
    )(length.reshape(1, 1), dn, qkv, o, lse, xhat, r, wqkv, wo, gain)

def gelu_parts(a):
    e = jnp.exp(-0.5 * a * a)
    t = 1.0 / (1.0 + 0.23164188624 * jnp.abs(a))
    tail = t * (0.127414796 + t * (-0.142248368 + t * (0.7107068705 + t * (-0.7265760135 + t * 0.5307027145)))) * e
    phi_cap = jnp.where(a < 0.0, tail, 1.0 - tail)
    return phi_cap, e * 0.3989422804014327

def ffn_fwd_kernel(chunk, n_ref, we_ref, wc_ref, be_ref, bias_ref, gain_ref,
                   y_ref, g_ref, gp_ref, xhat_ref, r_ref, acc_ref):
    s, d = n_ref.shape
    ff = we_ref.shape[1]
    low = n_ref[...].astype(BF)
    acc_ref[...] = n_ref[...] + bias_ref[4:5, :]

    def step(c, _):
        at = pl.multiple_of(c * chunk, chunk)
        a = dot(low, we_ref[:, pl.ds(at, chunk)]) + be_ref[:, pl.ds(at, chunk)]
        cap, dens = gelu_parts(a)
        g = (a * cap).astype(BF)
        g_ref[:, pl.ds(at, chunk)] = g
        gp_ref[:, pl.ds(at, chunk)] = (cap + a * dens).astype(BF)
        acc_ref[...] += dot(g, wc_ref[pl.ds(at, chunk), :])
        return 0
    lax.fori_loop(0, ff // chunk, step, 0)
    xhat, r, y = norm_forward(acc_ref[...], gain_ref[1:2, :], bias_ref[5:6, :])
    xhat_ref[...] = xhat
    r_ref[...] = jnp.broadcast_to(r, r_ref.shape)
    y_ref[...] = y.astype(BF)

def ffn_fwd(n, we, wc, be, bias, gain, chunk=512):
    s, d = n.shape
    ff = we.shape[1]
    vm = pl.BlockSpec(memory_space=pltpu.VMEM)
    return pl.pallas_call(
        functools.partial(ffn_fwd_kernel, chunk),
        out_shape=(jax.ShapeDtypeStruct((s, d), BF), jax.ShapeDtypeStruct((s, ff), BF), jax.ShapeDtypeStruct((s, ff), BF),
                   jax.ShapeDtypeStruct((s, d), F32), jax.ShapeDtypeStruct((s, 128), F32)),
        in_specs=[vm] * 6, out_specs=(vm,) * 5,
        scratch_shapes=[pltpu.VMEM((s, d), F32)],
        compiler_params=pltpu.CompilerParams(vmem_limit_bytes=60 << 20),
    )(n, we, wc, be.reshape(1, ff), bias, gain)

def ffn_bwd_kernel(chunk, extra, len_ref, cot_ref, dm_ref, gp_ref, xhat_ref, r_ref, we_ref, wc_ref, gain_ref,
                   dn_ref, da_ref, dt_ref, sums_ref, sume_ref):
    s, d = cot_ref.shape
    ff = we_ref.shape[1]
    row = lax.broadcasted_iota(jnp.int32, (s, 1), 0)
    dy = jnp.where(row < len_ref[0, 0], cot_ref[...].astype(F32), 0.0)
    if extra:
        dy = dy + dm_ref[...].astype(F32)
    xhat = xhat_ref[...]
    du = norm_backward(dy, xhat, r_ref[:, :1], gain_ref[1:2, :])
    dt = du.astype(BF)
    dt_ref[...] = dt
    sums_ref[0:1, :] = jnp.sum(dt.astype(F32), axis=0, keepdims=True)
    sums_ref[1:2, :] = jnp.sum(dy, axis=0, keepdims=True)
    sums_ref[2:3, :] = jnp.sum(dy * xhat, axis=0, keepdims=True)
    sums_ref[3:8, :] = jnp.zeros((5, d), F32)
    dn_ref[...] = du

    def step(c, _):
        at = pl.multiple_of(c * chunk, chunk)
        dg = dot_nt(dt_ref[...], wc_ref[pl.ds(at, chunk), :])
        da = (dg * gp_ref[:, pl.ds(at, chunk)].astype(F32)).astype(BF)
        da_ref[:, pl.ds(at, chunk)] = da
        sume_ref[:, pl.ds(at, chunk)] = jnp.sum(da.astype(F32), axis=0, keepdims=True)
        dn_ref[...] += dot_nt(da, we_ref[:, pl.ds(at, chunk)])
        return 0
    lax.fori_loop(0, ff // chunk, step, 0)

def ffn_bwd(cot, dm, length, saved, we, wc, gain, chunk=512):
    gp, xhat, r = saved
    s, d = cot.shape
    ff = we.shape[1]
    extra = dm is not None
    vm = pl.BlockSpec(memory_space=pltpu.VMEM)
    sm = pl.BlockSpec(memory_space=pltpu.SMEM)
    return pl.pallas_call(
        functools.partial(ffn_bwd_kernel, chunk, extra),
        out_shape=(jax.ShapeDtypeStruct((s, d), F32), jax.ShapeDtypeStruct((s, ff), BF), jax.ShapeDtypeStruct((s, d), BF),
                   jax.ShapeDtypeStruct((8, d), F32), jax.ShapeDtypeStruct((1, ff), F32)),
        in_specs=[sm] + [vm] * 8, out_specs=(vm,) * 5,
        compiler_params=pltpu.CompilerParams(vmem_limit_bytes=60 << 20),
    )(length.reshape(1, 1), cot, dm if extra else cot, gp, xhat, r, we, wc, gain)

MESH = pl.DeviceIdType.MESH
LAG = 2
RING = 8


def store_rows(total, out_ref):
    blocks, shards, rows, width = out_ref.shape
    halves = total.shape[1] // width
    groups = blocks // halves
    for k in range(shards):
        for j in range(groups):
            at = (k * groups + j) * rows
            for h in range(halves):
                out_ref[j * halves + h, k] = total[at : at + rows, h * width : (h + 1) * width]


def product(xs, dys):
    total = None
    for x, dy in zip(xs, dys):
        part = dot_tn(x[...].astype(BF), dy[...].astype(BF))
        total = part if total is None else total + part
    return total.astype(BF)


def wgrad_rows_kernel(n, *refs):
    store_rows(product(refs[:n], refs[n : 2 * n]), refs[2 * n])


def wgrad_rows(xs, dys, shards):
    sizes = [x.shape[0] for x in xs]
    n, k = xs[0].shape[1], dys[0].shape[1]
    width, rows = k // 2, k // shards
    groups = n // k
    return pl.pallas_call(
        functools.partial(wgrad_rows_kernel, len(xs)),
        out_shape=jax.ShapeDtypeStruct((2 * groups, shards, rows, width), BF),
        grid=(n // k,),
        in_specs=[pl.BlockSpec((s, k), lambda i: (0, i)) for s in sizes]
        + [pl.BlockSpec((s, k), lambda i: (0, 0)) for s in sizes],
        out_specs=pl.BlockSpec((2 * groups, shards // groups, rows, width), lambda i: (0, i, 0, 0)),
        compiler_params=pltpu.CompilerParams(vmem_limit_bytes=60 << 20),
    )(*xs, *dys)


def wgrad_cross_kernel(n, *refs):
    dqkv, dt, n1, mem, mixed = (refs[j * n : (j + 1) * n] for j in range(5))
    first_ref, second_ref = refs[5 * n :]
    i = pl.program_id(0)
    for at, xs, dys, out_ref in (
        (0, dqkv, n1, first_ref),
        (1, dqkv, mem, first_ref),
        (2, dqkv, mem, second_ref),
        (3, dt, mixed, second_ref),
    ):

        @pl.when(i == at)
        def _():
            store_rows(product(xs, dys), out_ref)


def wgrad_cross(dqkv, dt, n1, mem, mixed, shards):
    sizes = [x.shape[0] for x in dt]
    k = dt[0].shape[1]
    width, rows = k // 2, k // shards
    out = jax.ShapeDtypeStruct((4, shards, rows, width), BF)
    whole = [pl.BlockSpec((s, k), lambda i: (0, 0)) for s in sizes]
    return pl.pallas_call(
        functools.partial(wgrad_cross_kernel, len(sizes)),
        out_shape=(out, out),
        grid=(4,),
        in_specs=[pl.BlockSpec((s, k), lambda i: (0, jnp.minimum(i, 2))) for s in sizes] + whole * 4,
        out_specs=(
            pl.BlockSpec((4, shards // 2, rows, width), lambda i: (0, jnp.minimum(i, 1), 0, 0)),
            pl.BlockSpec((4, shards // 2, rows, width), lambda i: (0, jnp.maximum(i - 2, 0), 0, 0)),
        ),
        compiler_params=pltpu.CompilerParams(vmem_limit_bytes=60 << 20),
    )(*dqkv, *dt, *n1, *mem, *mixed)


def reduce_kernel(counts, *refs):
    (len_ref, dn_ref, qkv_ref, o_ref, lse_ref, xhat_ref, r_ref, wqkv_ref, wo_ref, gain_ref) = refs[:10]
    (x0_ref, x_ref, dqkv0_ref, o0_ref, dt0_ref, contract, cross_first, cross_second) = refs[10:18]
    ffn_refs = (refs[18:22], refs[22:26])
    (ssum_ref, fsum_ref, esum_ref, csum_ref) = refs[26:30]
    (dres_ref, in_ref, out_ref, expand_ref, contract_ref, cross_ref, vsum_ref, landed) = refs[30:38]
    (dqkv_ref, dt_ref, do_ref, dq_ref, sums_ref, made, own, r0, r1, r2, r3, vbuf, vrecv) = refs[38:51]
    (n0_buf, n1_buf, da0_buf, da1_buf) = refs[51:55]
    send_sem, recv_sem, local_sem, vsend_sem, vrecv_sem, xsend_sem, xrecv_sem, fetch_sem = refs[55:]
    d = dn_ref.shape[1]
    n_ffn, n_in, n_out, n_cross = 2 * counts[0], counts[1], counts[2], counts[3]
    blocks = n_ffn + n_in + n_out + n_cross
    rows, width = own.shape[-2:]
    second = lax.axis_index("section") == 1
    me = lax.axis_index("dp")
    c, y, zl, zh = me % 2, (me // 2) % 2, (me // 4) % 2, me // 8
    mates = (me + 1 - 2 * c, me + 2 - 4 * y, me + 4 - 8 * zl, me + 8 - 16 * zh)
    barrier = pltpu.get_barrier_semaphore()
    for mate in mates:
        pl.semaphore_signal(barrier, inc=1, device_id={"dp": mate}, device_id_type=MESH)
    across = 1 - lax.axis_index("section")
    pl.semaphore_signal(barrier, inc=1, device_id={"section": across}, device_id_type=MESH)

    def chosen(visit):
        for which, here in enumerate((jnp.logical_not(second), second)):

            @pl.when(here)
            def _():
                visit(ffn_refs[which])

    def fetch_norms(from_refs):
        return [
            pltpu.make_async_copy(from_refs[k], (n0_buf, n1_buf)[k], fetch_sem.at[2, k]) for k in range(2)
        ]

    def fetch_columns(from_refs, i):
        at = pl.ds(pl.multiple_of(i * d, 128), d)
        return [
            pltpu.make_async_copy(
                from_refs[2 + k].at[:, at], (da0_buf, da1_buf)[k].at[i % 2], fetch_sem.at[i % 2, k]
            )
            for k in range(2)
        ]

    def begin_fetch(from_refs):
        for copy in fetch_norms(from_refs) + fetch_columns(from_refs, 0) + fetch_columns(from_refs, 1):
            copy.start()

    chosen(begin_fetch)
    pl.semaphore_wait(barrier, 5)

    def over(j):
        return pltpu.make_async_remote_copy(
            src_ref=cross_first.at[j],
            dst_ref=landed.at[j],
            send_sem=xsend_sem.at[j],
            recv_sem=xrecv_sem.at[j],
            device_id={"section": across},
            device_id_type=MESH,
        )

    @pl.when(second)
    def _():
        for j in (*range(n_cross // 2, n_cross), *range(n_cross // 2)):
            over(j).start()

    order = ((0, 1, 2, 3), (0, 2, 3, 1))

    def remote(src, dst, stage, b, color):
        return pltpu.make_async_remote_copy(
            src_ref=src,
            dst_ref=dst,
            send_sem=send_sem.at[stage, b],
            recv_sem=recv_sem.at[stage, b],
            device_id={"dp": mates[order[color][stage]]},
            device_id_type=MESH,
        )

    turned = blocks // 7
    half = turned // 2
    steps = blocks - turned
    gap = steps // turned
    early = counts[0] - half

    def slot(b, color):
        if color == 0:
            return (b - jnp.where(b >= early, half, 0)) % RING
        return RING + jnp.where(b < steps, b - early, b - steps)

    def first_copy(part, at, b, color):
        return remote(part.at[at, :, :, :, 1 - c], r0.at[slot(b, color)], 0, b, color)

    def local_copy(part, at, b):
        return pltpu.make_async_copy(part.at[at, :, :, :, c], own.at[b], local_sem.at[b])

    def copy_of(stage, b, color):
        if color == 0:
            src = (own.at[b, :, :, 1 - y], own.at[b, :, 1 - zl, y], own.at[b, 1 - zh, zl, y])
        else:
            src = (own.at[b, :, 1 - zl], own.at[b, 1 - zh, zl], own.at[b, zh, zl, 1 - y])
        return remote(src[stage - 1], (r1, r2, r3)[stage - 1].at[b], stage, b, color)

    def add(left, right):
        return (left.astype(F32) + right.astype(F32)).astype(BF)

    def column(at):
        return pl.ds(pl.multiple_of(at * width, 128), width)

    def put_columns(ref, at, value):
        ref[:, column(at)] = value

    def put_groups(ref, at, value):
        ref[pl.ds(pl.multiple_of((at // 2) * rows, 8), rows), column(at % 2)] = value

    plan = (
        (((contract, None),), counts[0], put_groups, contract_ref),
        (((made, None),), counts[0], put_columns, expand_ref),
        (((made, None),), n_in, put_columns, in_ref),
        (((made, None),), n_out, put_columns, out_ref),
        (((landed, jnp.logical_not(second)), (cross_second, second)), n_cross, put_groups, cross_ref),
    )

    def each(b, visit):
        low = 0
        for sources, count, put, target in plan:
            inside = (b >= low) & (b < low + count)
            at = b % counts[0] if sources[0][0] is made else b - low
            visit(inside, sources, at, put, target, b - low)
            low += count

    def settle(stage, b, color):
        if stage == 0:
            first_copy(contract, 0, b, color).wait()
            local_copy(contract, 0, b).wait()
            own[b] = add(own[b], r0[slot(b, color)])
            return
        copy_of(stage, b, color).wait()
        if stage == 1:
            if color == 0:
                own[b, :, :, y] = add(own[b, :, :, y], r1[b])
            else:
                own[b, :, zl] = add(own[b, :, zl], r1[b])
        elif stage == 2:
            if color == 0:
                own[b, :, zl, y] = add(own[b, :, zl, y], r2[b])
            else:
                own[b, zh, zl] = add(own[b, zh, zl], r2[b])
        else:
            total = own[b, zh, zl, y].astype(F32) + r3[b].astype(F32)

            def finish(inside, sources, at, put, target, place):
                @pl.when(inside)
                def _():
                    put(target, place, total)

            each(b, finish)

    def vcopy(j):
        return pltpu.make_async_remote_copy(
            src_ref=vbuf.at[j],
            dst_ref=vrecv.at[j],
            send_sem=vsend_sem.at[j],
            recv_sem=vrecv_sem.at[j],
            device_id={"dp": mates[j]},
            device_id_type=MESH,
        )

    def advance(stage, b, color):
        if stage == 0:

            def launch(inside, sources, at, put, target, place):
                for part, here in sources:

                    @pl.when(inside if here is None else inside & here)
                    def _():
                        if part is landed:
                            over(at).wait_recv()
                        first_copy(part, at, b, color).start()
                        local_copy(part, at, b).start()

            each(b, launch)
            return
        settle(stage - 1, b, color)
        if stage < 4:
            copy_of(stage, b, color).start()

    def step(it, _):
        for stage in range(5):
            at = it - LAG * stage

            @pl.when((at >= 0) & (at < steps))
            def _():
                advance(stage, at + jnp.where(at >= early, half, 0), 0)

            @pl.when((at >= 0) & (at < turned * gap) & (at % gap == 1))
            def _():
                j = at // gap
                advance(stage, jnp.where(j < half, early, steps) + j, 1)

        return 0

    def some(low, high):
        lax.fori_loop(low, high, step, 0)

    def keep(block, total):
        for h in range(2):
            made[block + h] = total[:, h * width : (h + 1) * width].reshape(made.shape[1:]).astype(BF)

    pairs, chunks = d // 128, counts[0] // 2

    def beside(p):
        @pl.when(p < chunks)
        def _():
            @pl.when(p == 0)
            def _():
                for copy in fetch_norms(ffn_refs[0]):
                    copy.wait()

            for copy in fetch_columns(ffn_refs[0], p):
                copy.wait()
            keep(
                2 * p,
                dot_tn(n0_buf[...].astype(BF), da0_buf[p % 2]) + dot_tn(n1_buf[...].astype(BF), da1_buf[p % 2]),
            )

            def next_fetch(from_refs):
                for copy in fetch_columns(from_refs, p + 2):
                    copy.start()

            @pl.when(p + 2 < chunks)
            def _():
                chosen(next_fetch)

        some(jnp.minimum(3 + 2 * p, 7 + p), jnp.minimum(5 + 2 * p, 8 + p))

    some(0, 3)
    attn_bwd_body(
        True, beside,
        len_ref, dn_ref, qkv_ref, o_ref, lse_ref, xhat_ref, r_ref, wqkv_ref, wo_ref, gain_ref,
        dres_ref, dqkv_ref, dt_ref, None, sums_ref, do_ref, dq_ref,
    )
    after = 7 + pairs
    vbuf[0, 0:4] = sums_ref[0:4, :] + ssum_ref[0:4, :]
    vbuf[0, 4:6] = fsum_ref[0:2, :]
    vbuf[0, 6:7] = sums_ref[4:5, :] + ssum_ref[4:5, :]
    vbuf[0, 7:8] = fsum_ref[2:3, :]
    count = esum_ref.shape[1] // d
    for j in range(count):
        vbuf[0, 8 + j : 9 + j] = esum_ref[:, j * d : (j + 1) * d]
    vbuf[0, 8 + count : 13 + count] = csum_ref[0:5, :]
    vbuf[0, 13 + count :] = jnp.zeros((vbuf.shape[1] - 13 - count, d), F32)
    def weight(i, _):
        at = pl.ds(pl.multiple_of(i * d, 128), d)
        keep(2 * i, dot_tn(x0_ref[...], dqkv0_ref[:, at]) + dot_tn(x_ref[...], dqkv_ref[:, at]))
        step(after + i, 0)
        return 0

    lax.fori_loop(0, n_in // 2, weight, 0)
    keep(n_in, dot_tn(o0_ref[...], dt0_ref[...]) + dot_tn(o_ref[...], dt_ref[...]))
    begin = after + n_in // 2
    vcopy(0).start()

    def rest(it, _):
        step(it, 0)
        for j in range(4):

            @pl.when(it == begin + LAG * (j + 1))
            def _():
                vcopy(j).wait()
                vbuf[j + 1] = vbuf[j] + vrecv[j]
                if j < 3:
                    vcopy(j + 1).start()

        return 0

    lax.fori_loop(begin, steps + 4 * LAG, rest, 0)
    vsum_ref[...] = vbuf[4]

    @pl.when(second)
    def _():
        for j in range(n_cross):
            over(j).wait_send()


def reduce_scatter(length, dn, saved, w_in, w_out, gain, x0, x1, dqkv0, o0, dt0, parts, encoder, decoder, sums):
    s, d = dn.shape
    rows, width = parts[0].shape[-2:]
    n_in, n_out = dqkv0.shape[1] // width, dt0.shape[1] // width
    counts = (parts[0].shape[0], n_in, n_out, parts[1].shape[0])
    blocks = 2 * counts[0] + sum(counts[1:])
    parts = [part.reshape(part.shape[0], 2, 2, 2, 2, rows, width) for part in parts]
    short = x0.shape[0]
    vec = (24, d)
    vm = pl.BlockSpec(memory_space=pltpu.VMEM)
    sm = pl.BlockSpec(memory_space=pltpu.SMEM)
    shapes = ((s, d), (rows, n_in * width), (rows, n_out * width), (rows, counts[0] * width),
              (counts[0] // 2 * rows, d), (counts[3] // 2 * rows, d), vec)
    return pl.pallas_call(
        functools.partial(reduce_kernel, counts),
        out_shape=(*(jax.ShapeDtypeStruct(shape, F32) for shape in shapes), jax.ShapeDtypeStruct(parts[1].shape, BF)),
        in_specs=[sm] + [vm] * 14 + [pl.BlockSpec(memory_space=pl.ANY)] * 11 + [vm] * 4,
        out_specs=(*(vm,) * 7, pl.BlockSpec(memory_space=pl.ANY)),
        scratch_shapes=[
            pltpu.VMEM((s, 3 * d), BF),
            pltpu.VMEM((s, d), BF),
            pltpu.VMEM((s, d), BF),
            pltpu.VMEM((128, s), F32),
            pltpu.VMEM((8, d), F32),
            pltpu.VMEM((counts[0], 2, 2, 2, 2, rows, width), BF),
            pltpu.VMEM((blocks, 2, 2, 2, rows, width), BF),
            pltpu.VMEM((RING + blocks // 7, 2, 2, 2, rows, width), BF),
            pltpu.VMEM((blocks, 2, 2, rows, width), BF),
            pltpu.VMEM((blocks, 2, rows, width), BF),
            pltpu.VMEM((blocks, rows, width), BF),
            pltpu.VMEM((5, *vec), F32),
            pltpu.VMEM((4, *vec), F32),
            pltpu.VMEM((short, d), F32),
            pltpu.VMEM((s, d), F32),
            pltpu.VMEM((2, short, d), BF),
            pltpu.VMEM((2, s, d), BF),
            pltpu.SemaphoreType.DMA((4, blocks)),
            pltpu.SemaphoreType.DMA((4, blocks)),
            pltpu.SemaphoreType.DMA((blocks,)),
            pltpu.SemaphoreType.DMA((4,)),
            pltpu.SemaphoreType.DMA((4,)),
            pltpu.SemaphoreType.DMA((counts[3],)),
            pltpu.SemaphoreType.DMA((counts[3],)),
            pltpu.SemaphoreType.DMA((3, 2)),
        ],
        compiler_params=pltpu.CompilerParams(collective_id=0, has_side_effects=True, vmem_limit_bytes=67043328),
    )(length.reshape(1, 1), dn, *saved, w_in, w_out, gain, x0, x1, dqkv0, o0, dt0, *parts, *encoder, *decoder, *sums)[:7]


def shards(
    inputs_long,
    inputs_short,
    cotangent_long,
    cotangent_short,
    lengths_long,
    lengths_short,
    self_in_weight,
    self_out_weight,
    expand_weight,
    contract_weight,
    expand_bias,
    layer_biases,
    layer_gains,
    cross_weight,
    cross_biases,
    cross_gain,
):
    decoder = lax.axis_index("section") == 1
    d = inputs_long.shape[-1]
    ff = expand_weight.shape[2]
    w_in, w_out, w_e, w_c = self_in_weight[0], self_out_weight[0], expand_weight[0], contract_weight[0]
    b_e, bias, gain = expand_bias[0], layer_biases[0], layer_gains[0]
    c_gain = cross_gain.reshape(1, d)

    xs = (inputs_short[0, 0], inputs_long[0, 0])
    cots = (cotangent_short[0, 0], cotangent_long[0, 0])
    source = (lengths_short[0, 0], lengths_long[0, 0])
    target = (lengths_short[1, 0], lengths_long[1, 0])
    sizes = tuple(x.shape[0] for x in xs)

    own = tuple(jnp.where(decoder, t, o) for t, o in zip(target, source))

    def attend(i):
        x = xs[i]
        return attn_fwd(x, None, x, w_in, w_out, bias, gain, own[i])

    def encode_ffn(i, n):
        s = sizes[i]

        def decode():
            return blank(((s, d), BF), ((s, ff), BF), ((s, ff), BF), ((s, d), F32), ((s, 128), F32))

        return lax.cond(decoder, decode, lambda: ffn_fwd(n, w_e, w_c, b_e, bias, gain))

    def send(value, steps):
        return lax.ppermute(value, "section", [(0, 1)] if steps > 0 else [(1, 0)])

    def cross(i, memory, n1):
        s = sizes[i]

        def encode():
            return blank(
                ((s, 3 * d), BF), ((s, d), BF), ((s, d), F32), ((s, d), F32), ((s, 128), F32), ((s, d), F32)
            )

        def decode():
            return attn_fwd(n1, memory, n1, cross_weight, None, cross_biases, c_gain, source[i])

        return lax.cond(decoder, decode, encode)

    def turn(i, out):
        s = sizes[i]

        def decode():
            y, g, gp, xhat, r = ffn_fwd(out[5], w_e, w_c, b_e, bias, gain)
            fb = ffn_bwd(cots[i], None, target[i], (gp, xhat, r), w_e, w_c, gain)
            ab = attn_bwd(fb[0], out[:5], cross_weight, None, c_gain, source[i], False)
            return (g, fb[1], fb[2], ab[1], ab[2]), ab[0], ab[3], y, (fb[3], fb[4], ab[4])

        def encode():
            out = blank(
                ((s, ff), BF),
                ((s, ff), BF),
                ((s, d), BF),
                ((s, 3 * d), BF),
                ((s, d), BF),
                ((s, d), F32),
                ((s, d), BF),
                ((s, d), BF),
                ((8, d), F32),
                ((1, ff), F32),
                ((8, d), F32),
            )
            return tuple(out[:5]), out[5], out[6], out[7], tuple(out[8:])

        return lax.cond(decoder, decode, encode)

    att0 = attend(0)
    ffn0 = encode_ffn(0, att0[5])
    mem0 = send(ffn0[0], 1)
    x_long, _ = lax.optimization_barrier((xs[1], ffn0[0]))
    xs = (xs[0], x_long)
    att1 = attend(1)
    n_long, mem0 = lax.optimization_barrier((att1[5], mem0))
    ffn1 = encode_ffn(1, n_long)
    mem1 = send(ffn1[0], 1)
    n_short, _ = lax.optimization_barrier((att0[5], ffn1[0]))
    out0 = cross(0, mem0, n_short)
    keep0, dn0, dm0, y0, sums0 = turn(0, out0)
    back0 = send(dm0, -1)
    n_long, _ = lax.optimization_barrier((att1[5], dm0))
    out1 = cross(1, mem1, n_long)
    n_long, back0 = lax.optimization_barrier((out1[5], back0))
    out1 = (*out1[:5], n_long)
    keep1, dn1, dm1, y1, sums1 = turn(1, out1)
    back1 = send(dm1, -1)
    dp = lax.axis_size("dp")
    staged = dp == 16 and d % (16 * dp) == 0 and d == 6 * 128 and ff == 4 * d

    def cross_grads():
        n1, mem = (att0[5], att1[5]), (mem0, mem1)
        dqkv, dt = ((keep0[j], keep1[j]) for j in (3, 4))
        mixed = (out0[1], out1[1])
        if staged:
            return wgrad_cross(dqkv, dt, n1, mem, mixed, dp)
        joint = jnp.concatenate(dqkv, 0)
        low = jnp.concatenate(n1, 0).astype(BF)
        mem = jnp.concatenate(mem, 0)
        rows = (
            dot_tn(joint[:, :d], low),
            dot_tn(joint[:, d : 2 * d], mem),
            dot_tn(joint[:, 2 * d :], mem),
            dot_tn(jnp.concatenate(dt, 0), jnp.concatenate(mixed, 0)),
        )
        return tuple(jnp.concatenate(rows[j : j + 2], 0).astype(BF) for j in (0, 2))

    def cross_blank():
        shape = (4, dp, d // dp, d // 2) if staged else (2 * d, d)
        return tuple(blank((shape, BF), (shape, BF)))

    cross_sums = sums0[2] + sums1[2]
    cross_first, cross_second = lax.cond(decoder, cross_grads, cross_blank)
    back0, _ = lax.optimization_barrier((back0, cross_first))
    dn0, *enc0 = lax.cond(
        decoder,
        lambda: (dn0, *blank(((sizes[0], ff), BF), ((sizes[0], d), BF), ((8, d), F32), ((1, ff), F32))),
        lambda: tuple(ffn_bwd(cots[0], back0, source[0], ffn0[2:], w_e, w_c, gain)),
    )
    self0 = attn_bwd(dn0, att0[:5], w_in, w_out, gain, own[0], True)
    back1, cross_sent, _ = lax.optimization_barrier((back1, send(cross_sums, -1), self0[0]))
    cross_rows = jnp.where(decoder, cross_sums, cross_sent)

    def plain(left, right):
        left, right = (jnp.concatenate([e.astype(BF) for e in side], 0) for side in (left, right))
        return dot_tn(left, right).astype(BF)

    def contract_grad(g, dt):
        return wgrad_rows(g, dt, dp) if staged else plain(g, dt)

    def decode_last():
        grad = contract_grad((keep0[0], keep1[0]), (keep0[2], keep1[2]))
        return dn1, *blank(((sizes[1], ff), BF)), grad, sums0[0] + sums1[0], sums0[1] + sums1[1]

    def encode_last():
        dn, da, dt, sums, sum_e = ffn_bwd(cots[1], back1, source[1], ffn1[2:], w_e, w_c, gain)
        return dn, da, contract_grad((ffn0[1], ffn1[1]), (enc0[1], dt)), enc0[2] + sums, enc0[3] + sum_e

    dn1, enc_da, g_contract, ffn_sums, sum_e = lax.cond(decoder, decode_last, encode_last)
    if staged:
        dx1, *big, rows = reduce_scatter(
            own[1], dn1, att1[:5], w_in, w_out, gain, xs[0], xs[1], self0[1], att0[1], self0[2],
            (g_contract, cross_first, cross_second),
            (att0[5], att1[5], enc0[0], enc_da),
            (out0[5], out1[5], keep0[1], keep1[1]),
            (self0[4], ffn_sums, sum_e, cross_rows),
        )
    else:
        self1 = attn_bwd(dn1, att1[:5], w_in, w_out, gain, own[1], True)
        dx1 = self1[0]
        self_sums = self0[4] + self1[4]
        rows = [self_sums[0:4], ffn_sums[0:2], self_sums[4:5], ffn_sums[2:3], sum_e.reshape(ff // d, d), cross_rows[0:5]]
        rows = lax.psum(jnp.concatenate(rows, 0), "dp")
        cross_mine = jnp.where(decoder, cross_second, send(cross_first, -1))
        pairs = (((att0[5], enc0[0]), (att1[5], enc_da)), ((out0[5], keep0[1]), (out1[5], keep1[1])))
        g_expand = lax.cond(decoder, lambda: plain(*zip(*pairs[1])), lambda: plain(*zip(*pairs[0])))
        in_grad = plain(xs, (self0[1], self1[1]))
        out_grad = plain((att0[1], att1[1]), (self0[2], self1[2]))
        big = [
            lax.psum_scatter(part, "dp", scatter_dimension=0, tiled=True).astype(F32)
            for part in (in_grad, out_grad, g_expand, g_contract, cross_mine)
        ]
    count = 8 + ff // d
    me = lax.axis_index("dp")
    piece = lax.dynamic_slice_in_dim(rows[:8], me * (d // dp), d // dp, 1)
    e_piece = lax.dynamic_slice_in_dim(rows[8:count].reshape(1, ff), me * (ff // dp), ff // dp, 1)
    outs = [jnp.where(decoder, y, e)[None, None] for y, e in ((y0, ffn0[0]), (y1, ffn1[0]))]
    return (
        outs[1],
        outs[0],
        dx1[None, None],
        self0[0][None, None],
        big[0][None],
        big[1][None],
        big[2][None],
        big[3][None],
        e_piece,
        piece[None, :6],
        piece[None, 6:8],
        big[4].T,
        rows[count : count + 4],
        rows[count + 4],
    )


def solution(mesh):
    in_specs = (
        P("section", "dp", None, None),
        P("section", "dp", None, None),
        P("section", "dp", None, None),
        P("section", "dp", None, None),
        P(None, "dp"),
        P(None, "dp"),
        P("section", None, None),
        P("section", None, None),
        P("section", None, None),
        P("section", None, None),
        P("section", None),
        P("section", None, None),
        P("section", None, None),
        P(),
        P(),
        P(),
    )
    out_specs = (
        P("section", "dp", None, None),
        P("section", "dp", None, None),
        P("section", "dp", None, None),
        P("section", "dp", None, None),
        P("section", "dp", None),
        P("section", "dp", None),
        P("section", "dp", None),
        P("section", "dp", None),
        P("section", "dp"),
        P("section", None, "dp"),
        P("section", None, "dp"),
        P(None, ("section", "dp")),
        P(),
        P(),
    )
    return jax.shard_map(shards, mesh=mesh, in_specs=in_specs, out_specs=out_specs, check_vma=False)
```

```python
import functools
import jax
import jax.numpy as jnp
from jax import lax
from jax.experimental import pallas as pl
from jax.experimental.pallas import tpu as pltpu
from jax.sharding import PartitionSpec as P

BF, F32 = jnp.bfloat16, jnp.float32
NEG = -1e30
NT = (((1,), (1,)), ((), ()))
TN = (((0,), (0,)), ((), ()))

def dot(a, b):
    return jnp.dot(a, b, preferred_element_type=F32)
def dot_nt(a, b):
    return lax.dot_general(a, b, NT, preferred_element_type=F32)
def dot_tn(a, b):
    return lax.dot_general(a, b, TN, preferred_element_type=F32)

def lanes(rows):
    return lax.broadcasted_iota(jnp.int32, (rows, 128), 1)

def split3(v):
    hi = v.astype(BF)
    rest = v - hi.astype(F32)
    mid = rest.astype(BF)
    low = (rest - mid.astype(F32)).astype(BF)
    return hi, mid, low

def blank(*shapes):
    def nothing(*refs):
        pass

    return pl.pallas_call(
        nothing,
        out_shape=[jax.ShapeDtypeStruct(shape, kind) for shape, kind in shapes],
        out_specs=[pl.BlockSpec(memory_space=pl.ANY)] * len(shapes),
    )()


def norm_forward(u, gain, shift):
    mean = jnp.mean(u, axis=-1, keepdims=True)
    c = u - mean
    r = lax.rsqrt(jnp.mean(c * c, axis=-1, keepdims=True) + 1e-5)
    xhat = c * r
    return xhat, r, xhat * gain + shift

def causal_shift(size):
    return jnp.where(lax.axis_index("section") == 1, 0, size)


def attn_fwd_kernel(same, len_ref, xq_ref, xkv_ref, res_ref, wqkv_ref, wo_ref, bias_ref, gain_ref,
                    qkv_ref, o_ref, lse_ref, xhat_ref, r_ref, n_ref):
    s, d = xq_ref.shape
    if not same:
        wo_ref = wqkv_ref.at[:, 3 * d :]
    xq = xq_ref[...].astype(BF)
    xkv = xq if same else xkv_ref[...]
    qkv_ref[:, :d] = (dot(xq, wqkv_ref[:, :d]) + bias_ref[0:1, :]).astype(BF)
    qkv_ref[:, d:2*d] = dot(xkv, wqkv_ref[:, d:2*d]).astype(BF)
    qkv_ref[:, 2*d:] = (dot(xkv, wqkv_ref[:, 2*d:3*d]) + bias_ref[1:2, :]).astype(BF)
    length = len_ref[0, 0]
    lane = lanes(s)
    row = lax.broadcasted_iota(jnp.int32, (s, 128), 0)
    key_bias = jnp.where(row < length, 0.0, NEG).astype(BF)
    if same:
        tri = lax.broadcasted_iota(jnp.int32, (s, s), 1) <= lax.broadcasted_iota(jnp.int32, (s, s), 0) + causal_shift(s)
    one = jnp.ones((s, 128), BF)
    zero = jnp.zeros((s, 128), BF)

    def pair(p, _):
        at = pl.multiple_of(p * 128, 128)
        q = qkv_ref[:, pl.ds(at, 128)] * jnp.asarray(0.125, BF)
        k = qkv_ref[:, pl.ds(d + at, 128)]
        v = qkv_ref[:, pl.ds(2 * d + at, 128)]
        outs, lses = [], []
        for h in range(2):
            mine = (lane < 64) if h == 0 else (lane >= 64)
            other = 64 if h == 0 else 0
            qh = jnp.where(mine, q, jnp.where(lane == other, one, zero))
            kh = jnp.where(mine, k, jnp.where(lane == other, key_bias, zero))
            sc = dot_nt(qh, kh)
            if same:
                sc = jnp.where(tri, sc, NEG)
            m = jnp.max(sc, axis=-1, keepdims=True)
            e = jnp.exp(sc - m)
            l = jnp.sum(e, axis=-1, keepdims=True)
            outs.append(dot(e.astype(BF), v) * (1.0 / l))
            lses.append(m + jnp.log(l))
        o_ref[:, pl.ds(at, 128)] = jnp.where(lane < 64, outs[0], outs[1]).astype(BF)
        lse_ref[:, pl.ds(at, 128)] = jnp.where(lane < 64, lses[1], lses[0])
        return 0
    lax.fori_loop(0, d // 128, pair, 0)
    u = res_ref[...].astype(F32) + dot(o_ref[...], wo_ref[...]) + bias_ref[2:3, :]
    xhat, r, n = norm_forward(u, gain_ref[0:1, :], bias_ref[3:4, :])
    xhat_ref[...] = xhat
    r_ref[...] = jnp.broadcast_to(r, r_ref.shape)
    n_ref[...] = n

def attn_fwd(xq, xkv, res, wqkv, wo, bias, gain, length):
    s, d = xq.shape
    same = xkv is None
    if same:
        xkv = xq
    else:
        wo = gain
    vm = pl.BlockSpec(memory_space=pltpu.VMEM)
    sm = pl.BlockSpec(memory_space=pltpu.SMEM)
    return pl.pallas_call(
        functools.partial(attn_fwd_kernel, same),
        out_shape=(jax.ShapeDtypeStruct((s, 3 * d), BF), jax.ShapeDtypeStruct((s, d), BF), jax.ShapeDtypeStruct((s, d), F32),
                   jax.ShapeDtypeStruct((s, d), F32), jax.ShapeDtypeStruct((s, 128), F32), jax.ShapeDtypeStruct((s, d), F32)),
        in_specs=[sm] + [vm] * 7, out_specs=(vm,) * 6,
        compiler_params=pltpu.CompilerParams(vmem_limit_bytes=60 << 20),
    )(length.reshape(1, 1), xq, xkv, res, wqkv, wo, bias, gain)

def norm_backward(dn, xhat, r, gain):
    h = dn * gain
    return r * (h - jnp.mean(h, axis=-1, keepdims=True) - xhat * jnp.mean(h * xhat, axis=-1, keepdims=True))

def attn_bwd_body(same, between, len_ref, dn_ref, qkv_ref, o_ref, lse_ref, xhat_ref, r_ref, wqkv_ref, wo_ref, gain_ref,
                  dres_ref, dqkv_ref, dt_ref, dkvx_ref, sums_ref, do_ref, dq_ref):
    s, d = dn_ref.shape
    if not same:
        wo_ref = wqkv_ref.at[:, 3 * d :]
    dn = dn_ref[...]
    xhat = xhat_ref[...]
    du = norm_backward(dn, xhat, r_ref[:, :1], gain_ref[0:1, :])
    dt = du.astype(BF)
    dt_ref[...] = dt
    sums_ref[2:3, :] = jnp.sum(dt.astype(F32), axis=0, keepdims=True)
    sums_ref[3:4, :] = jnp.sum(dn, axis=0, keepdims=True)
    sums_ref[4:5, :] = jnp.sum(dn * xhat, axis=0, keepdims=True)
    dres_ref[...] = du
    do_ref[...] = dot_nt(dt, wo_ref[...]).astype(BF)
    length = len_ref[0, 0]
    lane = lanes(s)
    row = lax.broadcasted_iota(jnp.int32, (s, 128), 0)
    key_bias = jnp.where(row < length, 0.0, NEG).astype(BF)
    if same:
        tri = lax.broadcasted_iota(jnp.int32, (s, s), 0) <= lax.broadcasted_iota(jnp.int32, (s, s), 1) + causal_shift(s)
    one = jnp.ones((s, 128), BF)
    zero = jnp.zeros((s, 128), BF)

    def place(base, mine, other, extra):
        out = zero
        for j, val in enumerate(extra):
            out = jnp.where(lane == other + j, val, out)
        return jnp.where(mine, base, out)

    def pair(p, _):
        between(p)
        at = pl.multiple_of(p * 128, 128)
        q = qkv_ref[:, pl.ds(at, 128)] * jnp.asarray(0.125, BF)
        k = qkv_ref[:, pl.ds(d + at, 128)]
        v = qkv_ref[:, pl.ds(2 * d + at, 128)]
        do = do_ref[:, pl.ds(at, 128)]
        lse3 = split3(-lse_ref[:, pl.ds(at, 128)])
        prod = do.astype(F32) * o_ref[:, pl.ds(at, 128)].astype(F32)
        dq, dk, dv = [], [], []
        for h in range(2):
            mine = (lane < 64) if h == 0 else (lane >= 64)
            other = 64 if h == 0 else 0
            inner = jnp.broadcast_to(jnp.sum(jnp.where(mine, prod, 0.0), axis=-1, keepdims=True), (s, 128))
            qh = place(q, mine, other, (*lse3, one))
            kh = place(k, mine, other, (one, one, one, key_bias))
            doh = place(do, mine, other, split3(-inner))
            vh = place(v, mine, other, (one, one, one))
            st = dot_nt(kh, qh)
            if same:
                st = jnp.where(tri, st, NEG)
            pt = jnp.exp(st)
            dst = (pt * dot_nt(vh, doh)).astype(BF)
            dv.append(dot(pt.astype(BF), do))
            dk.append(dot(dst, q))
            dq.append(dot_tn(k, dst))
        m1 = lane < 64
        dq_ref[...] = jnp.where(lax.broadcasted_iota(jnp.int32, (128, s), 0) < 64, dq[0], dq[1])
        dqkv_ref[:, pl.ds(at, 128)] = (dq_ref[...].T * 0.125).astype(BF)
        dqkv_ref[:, pl.ds(d + at, 128)] = jnp.where(m1, dk[0], dk[1]).astype(BF)
        dqkv_ref[:, pl.ds(2 * d + at, 128)] = jnp.where(m1, dv[0], dv[1]).astype(BF)
        return 0
    lax.fori_loop(0, d // 128, pair, 0)
    if same:
        dres_ref[...] += dot_nt(dqkv_ref[...], wqkv_ref[...])
    else:
        dres_ref[...] += dot_nt(dqkv_ref[:, :d], wqkv_ref[:, :d])
        dkvx_ref[...] = dot_nt(dqkv_ref[:, d:], wqkv_ref[:, d:3*d]).astype(BF)
    sums_ref[0:1, :] = jnp.sum(dqkv_ref[:, :d].astype(F32), axis=0, keepdims=True)
    sums_ref[1:2, :] = jnp.sum(dqkv_ref[:, 2*d:].astype(F32), axis=0, keepdims=True)
    sums_ref[5:8, :] = jnp.zeros((3, d), F32)

def attn_bwd_kernel(same, *refs):
    attn_bwd_body(same, lambda p: None, *refs)


def attn_bwd(dn, saved, wqkv, wo, gain, length, same):
    qkv, o, lse, xhat, r = saved
    s, d = dn.shape
    if not same:
        wo = gain
    vm = pl.BlockSpec(memory_space=pltpu.VMEM)
    sm = pl.BlockSpec(memory_space=pltpu.SMEM)
    return pl.pallas_call(
        functools.partial(attn_bwd_kernel, same),
        out_shape=(jax.ShapeDtypeStruct((s, d), F32), jax.ShapeDtypeStruct((s, 3 * d), BF), jax.ShapeDtypeStruct((s, d), BF),
                   jax.ShapeDtypeStruct((8, 128) if same else (s, d), BF), jax.ShapeDtypeStruct((8, d), F32)),
        in_specs=[sm] + [vm] * 9, out_specs=(vm,) * 5,
        scratch_shapes=[pltpu.VMEM((s, d), BF), pltpu.VMEM((128, s), F32)],
        compiler_params=pltpu.CompilerParams(vmem_limit_bytes=60 << 20),
    )(length.reshape(1, 1), dn, qkv, o, lse, xhat, r, wqkv, wo, gain)

def gelu_parts(a):
    e = jnp.exp(-0.5 * a * a)
    t = 1.0 / (1.0 + 0.23164188624 * jnp.abs(a))
    tail = t * (0.127414796 + t * (-0.142248368 + t * (0.7107068705 + t * (-0.7265760135 + t * 0.5307027145)))) * e
    phi_cap = jnp.where(a < 0.0, tail, 1.0 - tail)
    return phi_cap, e * 0.3989422804014327

def ffn_fwd_kernel(n_ref, we_ref, wc_ref, be_ref, bias_ref, gain_ref,
                   y_ref, g_ref, gp_ref, xhat_ref, r_ref, acc_ref, low_ref):
    @pl.when(pl.program_id(0) == 0)
    def _():
        low_ref[...] = n_ref[...].astype(BF)
        acc_ref[...] = n_ref[...] + bias_ref[4:5, :]

    a = dot(low_ref[...], we_ref[...]) + be_ref[...]
    cap, dens = gelu_parts(a)
    g = (a * cap).astype(BF)
    g_ref[...] = g
    gp_ref[...] = (cap + a * dens).astype(BF)
    acc_ref[...] += dot(g, wc_ref[...])

    @pl.when(pl.program_id(0) == pl.num_programs(0) - 1)
    def _():
        xhat, r, y = norm_forward(acc_ref[...], gain_ref[1:2, :], bias_ref[5:6, :])
        xhat_ref[...] = xhat
        r_ref[...] = jnp.broadcast_to(r, r_ref.shape)
        y_ref[...] = y.astype(BF)


def whole(*shape):
    return pl.BlockSpec(shape, lambda c: (0, 0))


def ffn_fwd(n, we, wc, be, bias, gain, chunk=768):
    s, d = n.shape
    ff = we.shape[1]
    columns = pl.BlockSpec((s, chunk), lambda c: (0, c))
    return pl.pallas_call(
        ffn_fwd_kernel,
        out_shape=(jax.ShapeDtypeStruct((s, d), BF), jax.ShapeDtypeStruct((s, ff), BF), jax.ShapeDtypeStruct((s, ff), BF),
                   jax.ShapeDtypeStruct((s, d), F32), jax.ShapeDtypeStruct((s, 128), F32)),
        grid=(ff // chunk,),
        in_specs=[whole(s, d), pl.BlockSpec((d, chunk), lambda c: (0, c)), pl.BlockSpec((chunk, d), lambda c: (c, 0)),
                  pl.BlockSpec((1, chunk), lambda c: (0, c)), whole(*bias.shape), whole(*gain.shape)],
        out_specs=(whole(s, d), columns, columns, whole(s, d), whole(s, 128)),
        scratch_shapes=[pltpu.VMEM((s, d), F32), pltpu.VMEM((s, d), BF)],
        compiler_params=pltpu.CompilerParams(vmem_limit_bytes=60 << 20),
    )(n, we, wc, be.reshape(1, ff), bias, gain)


def ffn_bwd_kernel(extra, len_ref, cot_ref, dm_ref, gp_ref, xhat_ref, r_ref, we_ref, wc_ref, gain_ref,
                   dn_ref, da_ref, dt_ref, sums_ref, sume_ref):
    s, d = cot_ref.shape

    @pl.when(pl.program_id(0) == 0)
    def _():
        row = lax.broadcasted_iota(jnp.int32, (s, 1), 0)
        dy = jnp.where(row < len_ref[0, 0], cot_ref[...].astype(F32), 0.0)
        if extra:
            dy = dy + dm_ref[...].astype(F32)
        xhat = xhat_ref[...]
        du = norm_backward(dy, xhat, r_ref[:, :1], gain_ref[1:2, :])
        dt = du.astype(BF)
        dt_ref[...] = dt
        sums_ref[0:1, :] = jnp.sum(dt.astype(F32), axis=0, keepdims=True)
        sums_ref[1:2, :] = jnp.sum(dy, axis=0, keepdims=True)
        sums_ref[2:3, :] = jnp.sum(dy * xhat, axis=0, keepdims=True)
        sums_ref[3:8, :] = jnp.zeros((5, d), F32)
        dn_ref[...] = du

    dg = dot_nt(dt_ref[...], wc_ref[...])
    da = (dg * gp_ref[...].astype(F32)).astype(BF)
    da_ref[...] = da
    sume_ref[...] = jnp.sum(da.astype(F32), axis=0, keepdims=True)
    dn_ref[...] += dot_nt(da, we_ref[...])


def ffn_bwd(cot, dm, length, saved, we, wc, gain, chunk=768):
    gp, xhat, r = saved
    s, d = cot.shape
    ff = we.shape[1]
    extra = dm is not None
    sm = pl.BlockSpec(memory_space=pltpu.SMEM)
    columns = pl.BlockSpec((s, chunk), lambda c: (0, c))
    row = pl.BlockSpec((1, chunk), lambda c: (0, c))
    if not extra:
        dm = cot[:8]
    return pl.pallas_call(
        functools.partial(ffn_bwd_kernel, extra),
        out_shape=(jax.ShapeDtypeStruct((s, d), F32), jax.ShapeDtypeStruct((s, ff), BF), jax.ShapeDtypeStruct((s, d), BF),
                   jax.ShapeDtypeStruct((8, d), F32), jax.ShapeDtypeStruct((1, ff), F32)),
        grid=(ff // chunk,),
        in_specs=[sm, whole(s, d), whole(*dm.shape), columns, whole(s, d), whole(s, 128),
                  pl.BlockSpec((d, chunk), lambda c: (0, c)), pl.BlockSpec((chunk, d), lambda c: (c, 0)),
                  whole(*gain.shape)],
        out_specs=(whole(s, d), columns, whole(s, d), whole(8, d), row),
        compiler_params=pltpu.CompilerParams(vmem_limit_bytes=60 << 20),
    )(length.reshape(1, 1), cot, dm, gp, xhat, r, we, wc, gain)


MESH = pl.DeviceIdType.MESH
LAG = 2
RING = 8


def store_rows(total, out_ref):
    blocks, shards, rows, width = out_ref.shape
    halves = total.shape[1] // width
    groups = blocks // halves
    for k in range(shards):
        for j in range(groups):
            at = (k * groups + j) * rows
            for h in range(halves):
                out_ref[j * halves + h, k] = total[at : at + rows, h * width : (h + 1) * width]


def product(xs, dys):
    total = None
    for x, dy in zip(xs, dys):
        part = dot_tn(x[...].astype(BF), dy[...].astype(BF))
        total = part if total is None else total + part
    return total.astype(BF)


def wgrad_rows_kernel(n, *refs):
    store_rows(product(refs[:n], refs[n : 2 * n]), refs[2 * n])


def wgrad_rows(xs, dys, shards):
    sizes = [x.shape[0] for x in xs]
    n, k = xs[0].shape[1], dys[0].shape[1]
    width, rows = k // 2, k // shards
    groups = n // k
    return pl.pallas_call(
        functools.partial(wgrad_rows_kernel, len(xs)),
        out_shape=jax.ShapeDtypeStruct((2 * groups, shards, rows, width), BF),
        grid=(n // k,),
        in_specs=[pl.BlockSpec((s, k), lambda i: (0, i)) for s in sizes]
        + [pl.BlockSpec((s, k), lambda i: (0, 0)) for s in sizes],
        out_specs=pl.BlockSpec((2 * groups, shards // groups, rows, width), lambda i: (0, i, 0, 0)),
        compiler_params=pltpu.CompilerParams(vmem_limit_bytes=60 << 20),
    )(*xs, *dys)


def wgrad_cross_kernel(n, *refs):
    dqkv, dt, n1, mem, mixed = (refs[j * n : (j + 1) * n] for j in range(5))
    first_ref, second_ref = refs[5 * n :]
    i = pl.program_id(0)
    for at, xs, dys, out_ref in (
        (0, dqkv, n1, first_ref),
        (1, dqkv, mem, first_ref),
        (2, dqkv, mem, second_ref),
        (3, dt, mixed, second_ref),
    ):

        @pl.when(i == at)
        def _():
            store_rows(product(xs, dys), out_ref)


def wgrad_cross(dqkv, dt, n1, mem, mixed, shards):
    sizes = [x.shape[0] for x in dt]
    k = dt[0].shape[1]
    width, rows = k // 2, k // shards
    out = jax.ShapeDtypeStruct((4, shards, rows, width), BF)
    whole = [pl.BlockSpec((s, k), lambda i: (0, 0)) for s in sizes]
    return pl.pallas_call(
        functools.partial(wgrad_cross_kernel, len(sizes)),
        out_shape=(out, out),
        grid=(4,),
        in_specs=[pl.BlockSpec((s, k), lambda i: (0, jnp.minimum(i, 2))) for s in sizes] + whole * 4,
        out_specs=(
            pl.BlockSpec((4, shards // 2, rows, width), lambda i: (0, jnp.minimum(i, 1), 0, 0)),
            pl.BlockSpec((4, shards // 2, rows, width), lambda i: (0, jnp.maximum(i - 2, 0), 0, 0)),
        ),
        compiler_params=pltpu.CompilerParams(vmem_limit_bytes=60 << 20),
    )(*dqkv, *dt, *n1, *mem, *mixed)


def reduce_kernel(counts, *refs):
    (len_ref, dn_ref, qkv_ref, o_ref, lse_ref, xhat_ref, r_ref, wqkv_ref, wo_ref, gain_ref) = refs[:10]
    (x0_ref, x_ref, dqkv0_ref, o0_ref, dt0_ref, contract, cross_first, cross_second) = refs[10:18]
    ffn_refs = (refs[18:22], refs[22:26])
    (ssum_ref, fsum_ref, esum_ref, csum_ref) = refs[26:30]
    (dres_ref, in_ref, out_ref, expand_ref, contract_ref, cross_ref, vsum_ref, landed) = refs[30:38]
    (dqkv_ref, dt_ref, do_ref, dq_ref, sums_ref, made, own, r0, r1, r2, r3, vbuf, vrecv) = refs[38:51]
    (n0_buf, n1_buf, da0_buf, da1_buf) = refs[51:55]
    send_sem, recv_sem, local_sem, vsend_sem, vrecv_sem, xsend_sem, xrecv_sem, fetch_sem = refs[55:]
    d = dn_ref.shape[1]
    n_ffn, n_in, n_out, n_cross = 2 * counts[0], counts[1], counts[2], counts[3]
    blocks = n_ffn + n_in + n_out + n_cross
    rows, width = own.shape[-2:]
    second = lax.axis_index("section") == 1
    me = lax.axis_index("dp")
    c, y, zl, zh = me % 2, (me // 2) % 2, (me // 4) % 2, me // 8
    mates = (me + 1 - 2 * c, me + 2 - 4 * y, me + 4 - 8 * zl, me + 8 - 16 * zh)
    barrier = pltpu.get_barrier_semaphore()
    for mate in mates:
        pl.semaphore_signal(barrier, inc=1, device_id={"dp": mate}, device_id_type=MESH)
    across = 1 - lax.axis_index("section")
    pl.semaphore_signal(barrier, inc=1, device_id={"section": across}, device_id_type=MESH)

    def chosen(visit):
        for which, here in enumerate((jnp.logical_not(second), second)):

            @pl.when(here)
            def _():
                visit(ffn_refs[which])

    def fetch_norms(from_refs):
        return [
            pltpu.make_async_copy(from_refs[k], (n0_buf, n1_buf)[k], fetch_sem.at[2, k]) for k in range(2)
        ]

    def fetch_columns(from_refs, i):
        at = pl.ds(pl.multiple_of(i * d, 128), d)
        return [
            pltpu.make_async_copy(
                from_refs[2 + k].at[:, at], (da0_buf, da1_buf)[k].at[i % 2], fetch_sem.at[i % 2, k]
            )
            for k in range(2)
        ]

    def begin_fetch(from_refs):
        for copy in fetch_norms(from_refs) + fetch_columns(from_refs, 0) + fetch_columns(from_refs, 1):
            copy.start()

    chosen(begin_fetch)
    pl.semaphore_wait(barrier, 5)

    def over(j):
        return pltpu.make_async_remote_copy(
            src_ref=cross_first.at[j],
            dst_ref=landed.at[j],
            send_sem=xsend_sem.at[j],
            recv_sem=xrecv_sem.at[j],
            device_id={"section": across},
            device_id_type=MESH,
        )

    @pl.when(second)
    def _():
        for j in (*range(n_cross // 2, n_cross), *range(n_cross // 2)):
            over(j).start()

    order = ((0, 1, 2, 3), (0, 2, 3, 1))

    def remote(src, dst, stage, b, color):
        return pltpu.make_async_remote_copy(
            src_ref=src,
            dst_ref=dst,
            send_sem=send_sem.at[stage, b],
            recv_sem=recv_sem.at[stage, b],
            device_id={"dp": mates[order[color][stage]]},
            device_id_type=MESH,
        )

    turned = blocks // 7
    half = turned // 2
    steps = blocks - turned
    gap = 3
    early = counts[0] - half

    def slot(b, color):
        if color == 0:
            return (b - jnp.where(b >= early, half, 0)) % RING
        return RING + jnp.where(b < steps, b - early, b - steps)

    def first_copy(part, at, b, color):
        return remote(part.at[at, :, :, :, 1 - c], r0.at[slot(b, color)], 0, b, color)

    def local_copy(part, at, b):
        return pltpu.make_async_copy(part.at[at, :, :, :, c], own.at[b], local_sem.at[b])

    def copy_of(stage, b, color):
        if color == 0:
            src = (own.at[b, :, :, 1 - y], own.at[b, :, 1 - zl, y], own.at[b, 1 - zh, zl, y])
        else:
            src = (own.at[b, :, 1 - zl], own.at[b, 1 - zh, zl], own.at[b, zh, zl, 1 - y])
        return remote(src[stage - 1], (r1, r2, r3)[stage - 1].at[b], stage, b, color)

    def add(left, right):
        return (left.astype(F32) + right.astype(F32)).astype(BF)

    def column(at):
        return pl.ds(pl.multiple_of(at * width, 128), width)

    def put_columns(ref, at, value):
        ref[:, column(at)] = value

    def put_groups(ref, at, value):
        ref[pl.ds(pl.multiple_of((at // 2) * rows, 8), rows), column(at % 2)] = value

    plan = (
        (((contract, None),), counts[0], put_groups, contract_ref),
        (((made, None),), counts[0], put_columns, expand_ref),
        (((made, None),), n_in, put_columns, in_ref),
        (((made, None),), n_out, put_columns, out_ref),
        (((landed, jnp.logical_not(second)), (cross_second, second)), n_cross, put_groups, cross_ref),
    )

    def each(b, visit):
        low = 0
        for sources, count, put, target in plan:
            inside = (b >= low) & (b < low + count)
            at = b % counts[0] if sources[0][0] is made else b - low
            visit(inside, sources, at, put, target, b - low)
            low += count

    def settle(stage, b, color):
        if stage == 0:
            first_copy(contract, 0, b, color).wait()
            local_copy(contract, 0, b).wait()
            own[b] = add(own[b], r0[slot(b, color)])
            return
        copy_of(stage, b, color).wait()
        if stage == 1:
            if color == 0:
                own[b, :, :, y] = add(own[b, :, :, y], r1[b])
            else:
                own[b, :, zl] = add(own[b, :, zl], r1[b])
        elif stage == 2:
            if color == 0:
                own[b, :, zl, y] = add(own[b, :, zl, y], r2[b])
            else:
                own[b, zh, zl] = add(own[b, zh, zl], r2[b])
        else:
            total = own[b, zh, zl, y].astype(F32) + r3[b].astype(F32)

            def finish(inside, sources, at, put, target, place):
                @pl.when(inside)
                def _():
                    put(target, place, total)

            each(b, finish)

    def vcopy(j):
        return pltpu.make_async_remote_copy(
            src_ref=vbuf.at[j],
            dst_ref=vrecv.at[j],
            send_sem=vsend_sem.at[j],
            recv_sem=vrecv_sem.at[j],
            device_id={"dp": mates[j]},
            device_id_type=MESH,
        )

    def advance(stage, b, color):
        if stage == 0:

            def launch(inside, sources, at, put, target, place):
                for part, here in sources:

                    @pl.when(inside if here is None else inside & here)
                    def _():
                        if part is landed:
                            over(at).wait_recv()
                        first_copy(part, at, b, color).start()
                        local_copy(part, at, b).start()

            each(b, launch)
            return
        settle(stage - 1, b, color)
        if stage < 4:
            copy_of(stage, b, color).start()

    def step(it, _):
        for stage in range(5):
            at = it - LAG * stage

            @pl.when((at >= 0) & (at < steps))
            def _():
                advance(stage, at + jnp.where(at >= early, half, 0), 0)

            @pl.when((at >= 0) & (at < turned * gap) & (at % gap == 1))
            def _():
                j = at // gap
                advance(stage, jnp.where(j < half, early, steps) + j, 1)

        return 0

    def some(low, high):
        lax.fori_loop(low, high, step, 0)

    def keep(block, total):
        for h in range(2):
            made[block + h] = total[:, h * width : (h + 1) * width].reshape(made.shape[1:]).astype(BF)

    pairs, chunks = d // 128, counts[0] // 2

    def beside(p):
        @pl.when(p < chunks)
        def _():
            @pl.when(p == 0)
            def _():
                for copy in fetch_norms(ffn_refs[0]):
                    copy.wait()

            for copy in fetch_columns(ffn_refs[0], p):
                copy.wait()
            keep(
                2 * p,
                dot_tn(n0_buf[...].astype(BF), da0_buf[p % 2]) + dot_tn(n1_buf[...].astype(BF), da1_buf[p % 2]),
            )

            def next_fetch(from_refs):
                for copy in fetch_columns(from_refs, p + 2):
                    copy.start()

            @pl.when(p + 2 < chunks)
            def _():
                chosen(next_fetch)

        some(jnp.minimum(3 + 2 * p, 7 + p), jnp.minimum(5 + 2 * p, 8 + p))

    some(0, 3)
    attn_bwd_body(
        True, beside,
        len_ref, dn_ref, qkv_ref, o_ref, lse_ref, xhat_ref, r_ref, wqkv_ref, wo_ref, gain_ref,
        dres_ref, dqkv_ref, dt_ref, None, sums_ref, do_ref, dq_ref,
    )
    after = 7 + pairs
    vbuf[0, 0:4] = sums_ref[0:4, :] + ssum_ref[0:4, :]
    vbuf[0, 4:6] = fsum_ref[0:2, :]
    vbuf[0, 6:7] = sums_ref[4:5, :] + ssum_ref[4:5, :]
    vbuf[0, 7:8] = fsum_ref[2:3, :]
    count = esum_ref.shape[1] // d
    for j in range(count):
        vbuf[0, 8 + j : 9 + j] = esum_ref[:, j * d : (j + 1) * d]
    vbuf[0, 8 + count : 13 + count] = csum_ref[0:5, :]
    vbuf[0, 13 + count :] = jnp.zeros((vbuf.shape[1] - 13 - count, d), F32)
    def weight(i, _):
        at = pl.ds(pl.multiple_of(i * d, 128), d)
        keep(2 * i, dot_tn(x0_ref[...], dqkv0_ref[:, at]) + dot_tn(x_ref[...], dqkv_ref[:, at]))
        step(after + i, 0)
        return 0

    lax.fori_loop(0, n_in // 2, weight, 0)
    keep(n_in, dot_tn(o0_ref[...], dt0_ref[...]) + dot_tn(o_ref[...], dt_ref[...]))
    begin = after + n_in // 2
    vcopy(0).start()

    def rest(it, _):
        step(it, 0)
        for j in range(4):

            @pl.when(it == begin + LAG * (j + 1))
            def _():
                vcopy(j).wait()
                vbuf[j + 1] = vbuf[j] + vrecv[j]
                if j < 3:
                    vcopy(j + 1).start()

        return 0

    lax.fori_loop(begin, steps + 4 * LAG, rest, 0)
    vsum_ref[...] = vbuf[4]

    @pl.when(second)
    def _():
        for j in range(n_cross):
            over(j).wait_send()


def reduce_scatter(length, dn, saved, w_in, w_out, gain, x0, x1, dqkv0, o0, dt0, parts, encoder, decoder, sums):
    s, d = dn.shape
    rows, width = parts[0].shape[-2:]
    n_in, n_out = dqkv0.shape[1] // width, dt0.shape[1] // width
    counts = (parts[0].shape[0], n_in, n_out, parts[1].shape[0])
    blocks = 2 * counts[0] + sum(counts[1:])
    parts = [part.reshape(part.shape[0], 2, 2, 2, 2, rows, width) for part in parts]
    short = x0.shape[0]
    vec = (24, d)
    vm = pl.BlockSpec(memory_space=pltpu.VMEM)
    sm = pl.BlockSpec(memory_space=pltpu.SMEM)
    shapes = ((s, d), (rows, n_in * width), (rows, n_out * width), (rows, counts[0] * width),
              (counts[0] // 2 * rows, d), (counts[3] // 2 * rows, d), vec)
    return pl.pallas_call(
        functools.partial(reduce_kernel, counts),
        out_shape=(*(jax.ShapeDtypeStruct(shape, F32) for shape in shapes), jax.ShapeDtypeStruct(parts[1].shape, BF)),
        in_specs=[sm] + [vm] * 14 + [pl.BlockSpec(memory_space=pl.ANY)] * 11 + [vm] * 4,
        out_specs=(*(vm,) * 7, pl.BlockSpec(memory_space=pl.ANY)),
        scratch_shapes=[
            pltpu.VMEM((s, 3 * d), BF),
            pltpu.VMEM((s, d), BF),
            pltpu.VMEM((s, d), BF),
            pltpu.VMEM((128, s), F32),
            pltpu.VMEM((8, d), F32),
            pltpu.VMEM((counts[0], 2, 2, 2, 2, rows, width), BF),
            pltpu.VMEM((blocks, 2, 2, 2, rows, width), BF),
            pltpu.VMEM((RING + blocks // 7, 2, 2, 2, rows, width), BF),
            pltpu.VMEM((blocks, 2, 2, rows, width), BF),
            pltpu.VMEM((blocks, 2, rows, width), BF),
            pltpu.VMEM((blocks, rows, width), BF),
            pltpu.VMEM((5, *vec), F32),
            pltpu.VMEM((4, *vec), F32),
            pltpu.VMEM((short, d), F32),
            pltpu.VMEM((s, d), F32),
            pltpu.VMEM((2, short, d), BF),
            pltpu.VMEM((2, s, d), BF),
            pltpu.SemaphoreType.DMA((4, blocks)),
            pltpu.SemaphoreType.DMA((4, blocks)),
            pltpu.SemaphoreType.DMA((blocks,)),
            pltpu.SemaphoreType.DMA((4,)),
            pltpu.SemaphoreType.DMA((4,)),
            pltpu.SemaphoreType.DMA((counts[3],)),
            pltpu.SemaphoreType.DMA((counts[3],)),
            pltpu.SemaphoreType.DMA((3, 2)),
        ],
        compiler_params=pltpu.CompilerParams(collective_id=0, has_side_effects=True, vmem_limit_bytes=67043328),
    )(length.reshape(1, 1), dn, *saved, w_in, w_out, gain, x0, x1, dqkv0, o0, dt0, *parts, *encoder, *decoder, *sums)[:7]


def shards(
    inputs_long,
    inputs_short,
    cotangent_long,
    cotangent_short,
    lengths_long,
    lengths_short,
    self_in_weight,
    self_out_weight,
    expand_weight,
    contract_weight,
    expand_bias,
    layer_biases,
    layer_gains,
    cross_weight,
    cross_biases,
    cross_gain,
):
    decoder = lax.axis_index("section") == 1
    d = inputs_long.shape[-1]
    ff = expand_weight.shape[2]
    w_in, w_out, w_e, w_c = self_in_weight[0], self_out_weight[0], expand_weight[0], contract_weight[0]
    b_e, bias, gain = expand_bias[0], layer_biases[0], layer_gains[0]
    c_gain = cross_gain.reshape(1, d)

    xs = (inputs_short[0, 0], inputs_long[0, 0])
    cots = (cotangent_short[0, 0], cotangent_long[0, 0])
    source = (lengths_short[0, 0], lengths_long[0, 0])
    target = (lengths_short[1, 0], lengths_long[1, 0])
    sizes = tuple(x.shape[0] for x in xs)

    own = tuple(jnp.where(decoder, t, o) for t, o in zip(target, source))

    def attend(i):
        x = xs[i]
        return attn_fwd(x, None, x, w_in, w_out, bias, gain, own[i])

    def encode_ffn(i, n):
        s = sizes[i]

        def decode():
            return blank(((s, d), BF), ((s, ff), BF), ((s, ff), BF), ((s, d), F32), ((s, 128), F32))

        return lax.cond(decoder, decode, lambda: ffn_fwd(n, w_e, w_c, b_e, bias, gain))

    def send(value, steps):
        return lax.ppermute(value, "section", [(0, 1)] if steps > 0 else [(1, 0)])

    def cross(i, memory, n1):
        s = sizes[i]

        def encode():
            return blank(
                ((s, 3 * d), BF), ((s, d), BF), ((s, d), F32), ((s, d), F32), ((s, 128), F32), ((s, d), F32)
            )

        def decode():
            return attn_fwd(n1, memory, n1, cross_weight, None, cross_biases, c_gain, source[i])

        return lax.cond(decoder, decode, encode)

    def turn(i, out):
        s = sizes[i]

        def decode():
            y, g, gp, xhat, r = ffn_fwd(out[5], w_e, w_c, b_e, bias, gain)
            fb = ffn_bwd(cots[i], None, target[i], (gp, xhat, r), w_e, w_c, gain)
            ab = attn_bwd(fb[0], out[:5], cross_weight, None, c_gain, source[i], False)
            return (g, fb[1], fb[2], ab[1], ab[2]), ab[0], ab[3], y, (fb[3], fb[4], ab[4])

        def encode():
            out = blank(
                ((s, ff), BF),
                ((s, ff), BF),
                ((s, d), BF),
                ((s, 3 * d), BF),
                ((s, d), BF),
                ((s, d), F32),
                ((s, d), BF),
                ((s, d), BF),
                ((8, d), F32),
                ((1, ff), F32),
                ((8, d), F32),
            )
            return tuple(out[:5]), out[5], out[6], out[7], tuple(out[8:])

        return lax.cond(decoder, decode, encode)

    att0 = attend(0)
    ffn0 = encode_ffn(0, att0[5])
    mem0 = send(ffn0[0], 1)
    x_long, _ = lax.optimization_barrier((xs[1], ffn0[0]))
    xs = (xs[0], x_long)
    att1 = attend(1)
    n_long, mem0 = lax.optimization_barrier((att1[5], mem0))
    ffn1 = encode_ffn(1, n_long)
    mem1 = send(ffn1[0], 1)
    n_short, _ = lax.optimization_barrier((att0[5], ffn1[0]))
    out0 = cross(0, mem0, n_short)
    keep0, dn0, dm0, y0, sums0 = turn(0, out0)
    back0 = send(dm0, -1)
    n_long, _ = lax.optimization_barrier((att1[5], dm0))
    out1 = cross(1, mem1, n_long)
    n_long, back0 = lax.optimization_barrier((out1[5], back0))
    out1 = (*out1[:5], n_long)
    keep1, dn1, dm1, y1, sums1 = turn(1, out1)
    back1 = send(dm1, -1)
    dp = lax.axis_size("dp")
    staged = dp == 16 and d % (16 * dp) == 0 and d == 6 * 128 and ff == 4 * d

    def cross_grads():
        n1, mem = (att0[5], att1[5]), (mem0, mem1)
        dqkv, dt = ((keep0[j], keep1[j]) for j in (3, 4))
        mixed = (out0[1], out1[1])
        if staged:
            return wgrad_cross(dqkv, dt, n1, mem, mixed, dp)
        joint = jnp.concatenate(dqkv, 0)
        low = jnp.concatenate(n1, 0).astype(BF)
        mem = jnp.concatenate(mem, 0)
        rows = (
            dot_tn(joint[:, :d], low),
            dot_tn(joint[:, d : 2 * d], mem),
            dot_tn(joint[:, 2 * d :], mem),
            dot_tn(jnp.concatenate(dt, 0), jnp.concatenate(mixed, 0)),
        )
        return tuple(jnp.concatenate(rows[j : j + 2], 0).astype(BF) for j in (0, 2))

    def cross_blank():
        shape = (4, dp, d // dp, d // 2) if staged else (2 * d, d)
        return tuple(blank((shape, BF), (shape, BF)))

    cross_sums = sums0[2] + sums1[2]
    cross_first, cross_second = lax.cond(decoder, cross_grads, cross_blank)
    back0, _ = lax.optimization_barrier((back0, cross_first))
    dn0, *enc0 = lax.cond(
        decoder,
        lambda: (dn0, *blank(((sizes[0], ff), BF), ((sizes[0], d), BF), ((8, d), F32), ((1, ff), F32))),
        lambda: tuple(ffn_bwd(cots[0], back0, source[0], ffn0[2:], w_e, w_c, gain)),
    )
    self0 = attn_bwd(dn0, att0[:5], w_in, w_out, gain, own[0], True)
    back1, cross_sent, _ = lax.optimization_barrier((back1, send(cross_sums, -1), self0[0]))
    cross_rows = jnp.where(decoder, cross_sums, cross_sent)

    def plain(left, right):
        left, right = (jnp.concatenate([e.astype(BF) for e in side], 0) for side in (left, right))
        return dot_tn(left, right).astype(BF)

    def contract_grad(g, dt):
        return wgrad_rows(g, dt, dp) if staged else plain(g, dt)

    def decode_last():
        grad = contract_grad((keep0[0], keep1[0]), (keep0[2], keep1[2]))
        return dn1, *blank(((sizes[1], ff), BF)), grad, sums0[0] + sums1[0], sums0[1] + sums1[1]

    def encode_last():
        dn, da, dt, sums, sum_e = ffn_bwd(cots[1], back1, source[1], ffn1[2:], w_e, w_c, gain)
        return dn, da, contract_grad((ffn0[1], ffn1[1]), (enc0[1], dt)), enc0[2] + sums, enc0[3] + sum_e

    dn1, enc_da, g_contract, ffn_sums, sum_e = lax.cond(decoder, decode_last, encode_last)
    if staged:
        dx1, *big, rows = reduce_scatter(
            own[1], dn1, att1[:5], w_in, w_out, gain, xs[0], xs[1], self0[1], att0[1], self0[2],
            (g_contract, cross_first, cross_second),
            (att0[5], att1[5], enc0[0], enc_da),
            (out0[5], out1[5], keep0[1], keep1[1]),
            (self0[4], ffn_sums, sum_e, cross_rows),
        )
    else:
        self1 = attn_bwd(dn1, att1[:5], w_in, w_out, gain, own[1], True)
        dx1 = self1[0]
        self_sums = self0[4] + self1[4]
        rows = [self_sums[0:4], ffn_sums[0:2], self_sums[4:5], ffn_sums[2:3], sum_e.reshape(ff // d, d), cross_rows[0:5]]
        rows = lax.psum(jnp.concatenate(rows, 0), "dp")
        cross_mine = jnp.where(decoder, cross_second, send(cross_first, -1))
        pairs = (((att0[5], enc0[0]), (att1[5], enc_da)), ((out0[5], keep0[1]), (out1[5], keep1[1])))
        g_expand = lax.cond(decoder, lambda: plain(*zip(*pairs[1])), lambda: plain(*zip(*pairs[0])))
        in_grad = plain(xs, (self0[1], self1[1]))
        out_grad = plain((att0[1], att1[1]), (self0[2], self1[2]))
        big = [
            lax.psum_scatter(part, "dp", scatter_dimension=0, tiled=True).astype(F32)
            for part in (in_grad, out_grad, g_expand, g_contract, cross_mine)
        ]
    count = 8 + ff // d
    me = lax.axis_index("dp")
    piece = lax.dynamic_slice_in_dim(rows[:8], me * (d // dp), d // dp, 1)
    e_piece = lax.dynamic_slice_in_dim(rows[8:count].reshape(1, ff), me * (ff // dp), ff // dp, 1)
    outs = [jnp.where(decoder, y, e)[None, None] for y, e in ((y0, ffn0[0]), (y1, ffn1[0]))]
    return (
        outs[1],
        outs[0],
        dx1[None, None],
        self0[0][None, None],
        big[0][None],
        big[1][None],
        big[2][None],
        big[3][None],
        e_piece,
        piece[None, :6],
        piece[None, 6:8],
        big[4].T,
        rows[count : count + 4],
        rows[count + 4],
    )


def solution(mesh):
    in_specs = (
        P("section", "dp", None, None),
        P("section", "dp", None, None),
        P("section", "dp", None, None),
        P("section", "dp", None, None),
        P(None, "dp"),
        P(None, "dp"),
        P("section", None, None),
        P("section", None, None),
        P("section", None, None),
        P("section", None, None),
        P("section", None),
        P("section", None, None),
        P("section", None, None),
        P(),
        P(),
        P(),
    )
    out_specs = (
        P("section", "dp", None, None),
        P("section", "dp", None, None),
        P("section", "dp", None, None),
        P("section", "dp", None, None),
        P("section", "dp", None),
        P("section", "dp", None),
        P("section", "dp", None),
        P("section", "dp", None),
        P("section", "dp"),
        P("section", None, "dp"),
        P("section", None, "dp"),
        P(None, ("section", "dp")),
        P(),
        P(),
    )
    return jax.shard_map(shards, mesh=mesh, in_specs=in_specs, out_specs=out_specs, check_vma=False)
```

```python
import functools
import jax
import jax.numpy as jnp
from jax import lax
from jax.experimental import pallas as pl
from jax.experimental.pallas import tpu as pltpu
from jax.sharding import PartitionSpec as P

BF, F32 = jnp.bfloat16, jnp.float32
NEG = -1e30
NT = (((1,), (1,)), ((), ()))
TN = (((0,), (0,)), ((), ()))

def dot(a, b):
    return jnp.dot(a, b, preferred_element_type=F32)
def dot_nt(a, b):
    return lax.dot_general(a, b, NT, preferred_element_type=F32)
def dot_tn(a, b):
    return lax.dot_general(a, b, TN, preferred_element_type=F32)

def lanes(rows):
    return lax.broadcasted_iota(jnp.int32, (rows, 128), 1)

def split3(v):
    hi = v.astype(BF)
    rest = v - hi.astype(F32)
    mid = rest.astype(BF)
    low = (rest - mid.astype(F32)).astype(BF)
    return hi, mid, low

def blank(*shapes):
    def nothing(*refs):
        pass

    return pl.pallas_call(
        nothing,
        out_shape=[jax.ShapeDtypeStruct(shape, kind) for shape, kind in shapes],
        out_specs=[pl.BlockSpec(memory_space=pl.ANY)] * len(shapes),
    )()


def norm_forward(u, gain, shift):
    mean = jnp.mean(u, axis=-1, keepdims=True)
    c = u - mean
    r = lax.rsqrt(jnp.mean(c * c, axis=-1, keepdims=True) + 1e-5)
    xhat = c * r
    return xhat, r, xhat * gain + shift

def causal_shift(size):
    return jnp.where(lax.axis_index("section") == 1, 0, size)


def attn_fwd_kernel(same, len_ref, xq_ref, xkv_ref, res_ref, wqkv_ref, wo_ref, bias_ref, gain_ref,
                    qkv_ref, o_ref, lse_ref, xhat_ref, r_ref, n_ref):
    s, d = xq_ref.shape
    if not same:
        wo_ref = wqkv_ref.at[:, 3 * d :]
    xq = xq_ref[...].astype(BF)
    xkv = xq if same else xkv_ref[...]
    qkv_ref[:, :d] = (dot(xq, wqkv_ref[:, :d]) + bias_ref[0:1, :]).astype(BF)
    qkv_ref[:, d:2*d] = dot(xkv, wqkv_ref[:, d:2*d]).astype(BF)
    qkv_ref[:, 2*d:] = (dot(xkv, wqkv_ref[:, 2*d:3*d]) + bias_ref[1:2, :]).astype(BF)
    length = len_ref[0, 0]
    lane = lanes(s)
    row = lax.broadcasted_iota(jnp.int32, (s, 128), 0)
    key_bias = jnp.where(row < length, 0.0, NEG).astype(BF)
    if same:
        tri = lax.broadcasted_iota(jnp.int32, (s, s), 1) <= lax.broadcasted_iota(jnp.int32, (s, s), 0) + causal_shift(s)
    one = jnp.ones((s, 128), BF)
    zero = jnp.zeros((s, 128), BF)

    def pair(p, _):
        at = pl.multiple_of(p * 128, 128)
        q = qkv_ref[:, pl.ds(at, 128)] * jnp.asarray(0.125, BF)
        k = qkv_ref[:, pl.ds(d + at, 128)]
        v = qkv_ref[:, pl.ds(2 * d + at, 128)]
        outs, lses = [], []
        for h in range(2):
            mine = (lane < 64) if h == 0 else (lane >= 64)
            other = 64 if h == 0 else 0
            qh = jnp.where(mine, q, jnp.where(lane == other, one, zero))
            kh = jnp.where(mine, k, jnp.where(lane == other, key_bias, zero))
            sc = dot_nt(qh, kh)
            if same:
                sc = jnp.where(tri, sc, NEG)
            m = jnp.max(sc, axis=-1, keepdims=True)
            e = jnp.exp(sc - m)
            l = jnp.sum(e, axis=-1, keepdims=True)
            outs.append(dot(e.astype(BF), v) * (1.0 / l))
            lses.append(m + jnp.log(l))
        o_ref[:, pl.ds(at, 128)] = jnp.where(lane < 64, outs[0], outs[1]).astype(BF)
        lse_ref[:, pl.ds(at, 128)] = jnp.where(lane < 64, lses[1], lses[0])
        return 0
    lax.fori_loop(0, d // 128, pair, 0)
    u = res_ref[...].astype(F32) + dot(o_ref[...], wo_ref[...]) + bias_ref[2:3, :]
    xhat, r, n = norm_forward(u, gain_ref[0:1, :], bias_ref[3:4, :])
    xhat_ref[...] = xhat
    r_ref[...] = jnp.broadcast_to(r, r_ref.shape)
    n_ref[...] = n

def attn_fwd(xq, xkv, res, wqkv, wo, bias, gain, length):
    s, d = xq.shape
    same = xkv is None
    if same:
        xkv = xq
    else:
        wo = gain
    vm = pl.BlockSpec(memory_space=pltpu.VMEM)
    sm = pl.BlockSpec(memory_space=pltpu.SMEM)
    return pl.pallas_call(
        functools.partial(attn_fwd_kernel, same),
        out_shape=(jax.ShapeDtypeStruct((s, 3 * d), BF), jax.ShapeDtypeStruct((s, d), BF), jax.ShapeDtypeStruct((s, d), F32),
                   jax.ShapeDtypeStruct((s, d), F32), jax.ShapeDtypeStruct((s, 128), F32), jax.ShapeDtypeStruct((s, d), F32)),
        in_specs=[sm] + [vm] * 7, out_specs=(vm,) * 6,
        compiler_params=pltpu.CompilerParams(vmem_limit_bytes=60 << 20),
    )(length.reshape(1, 1), xq, xkv, res, wqkv, wo, bias, gain)

def norm_backward(dn, xhat, r, gain):
    h = dn * gain
    return r * (h - jnp.mean(h, axis=-1, keepdims=True) - xhat * jnp.mean(h * xhat, axis=-1, keepdims=True))

def attn_bwd_body(same, between, ready, len_ref, dn_ref, qkv_ref, o_ref, lse_ref, xhat_ref, r_ref, wqkv_ref, wo_ref, gain_ref,
                  dres_ref, dqkv_ref, dt_ref, dkvx_ref, sums_ref, do_ref, dq_ref):
    s, d = dn_ref.shape
    dn = dn_ref[...]
    xhat = xhat_ref[...]
    du = norm_backward(dn, xhat, r_ref[:, :1], gain_ref[0:1, :])
    dt = du.astype(BF)
    dt_ref[...] = dt
    sums_ref[2:3, :] = jnp.sum(dt.astype(F32), axis=0, keepdims=True)
    sums_ref[3:4, :] = jnp.sum(dn, axis=0, keepdims=True)
    sums_ref[4:5, :] = jnp.sum(dn * xhat, axis=0, keepdims=True)
    dres_ref[...] = du
    ready(2)
    do_ref[...] = dot_nt(dt, wo_ref[...]).astype(BF)
    length = len_ref[0, 0]
    lane = lanes(s)
    row = lax.broadcasted_iota(jnp.int32, (s, 128), 0)
    key_bias = jnp.where(row < length, 0.0, NEG).astype(BF)
    if same:
        tri = lax.broadcasted_iota(jnp.int32, (s, s), 0) <= lax.broadcasted_iota(jnp.int32, (s, s), 1) + causal_shift(s)
    one = jnp.ones((s, 128), BF)
    zero = jnp.zeros((s, 128), BF)

    def place(base, mine, other, extra):
        out = zero
        for j, val in enumerate(extra):
            out = jnp.where(lane == other + j, val, out)
        return jnp.where(mine, base, out)

    def pair(p, _):
        between(p)
        at = pl.multiple_of(p * 128, 128)
        q = qkv_ref[:, pl.ds(at, 128)] * jnp.asarray(0.125, BF)
        k = qkv_ref[:, pl.ds(d + at, 128)]
        v = qkv_ref[:, pl.ds(2 * d + at, 128)]
        do = do_ref[:, pl.ds(at, 128)]
        lse3 = split3(-lse_ref[:, pl.ds(at, 128)])
        prod = do.astype(F32) * o_ref[:, pl.ds(at, 128)].astype(F32)
        dq, dk, dv = [], [], []
        for h in range(2):
            mine = (lane < 64) if h == 0 else (lane >= 64)
            other = 64 if h == 0 else 0
            inner = jnp.broadcast_to(jnp.sum(jnp.where(mine, prod, 0.0), axis=-1, keepdims=True), (s, 128))
            qh = place(q, mine, other, (*lse3, one))
            kh = place(k, mine, other, (one, one, one, key_bias))
            doh = place(do, mine, other, split3(-inner))
            vh = place(v, mine, other, (one, one, one))
            st = dot_nt(kh, qh)
            if same:
                st = jnp.where(tri, st, NEG)
            pt = jnp.exp(st)
            dst = (pt * dot_nt(vh, doh)).astype(BF)
            dv.append(dot(pt.astype(BF), do))
            dk.append(dot(dst, q))
            dq.append(dot_tn(k, dst))
        m1 = lane < 64
        dq_ref[...] = jnp.where(lax.broadcasted_iota(jnp.int32, (128, s), 0) < 64, dq[0], dq[1])
        dqkv_ref[:, pl.ds(at, 128)] = (dq_ref[...].T * 0.125).astype(BF)
        dqkv_ref[:, pl.ds(d + at, 128)] = jnp.where(m1, dk[0], dk[1]).astype(BF)
        dqkv_ref[:, pl.ds(2 * d + at, 128)] = jnp.where(m1, dv[0], dv[1]).astype(BF)
        return 0
    ready(0)
    lax.fori_loop(0, d // 128, pair, 0)
    ready(1)
    if same:
        dres_ref[...] += dot_nt(dqkv_ref[...], wqkv_ref[...])
    else:
        dres_ref[...] += dot_nt(dqkv_ref[:, :d], wqkv_ref[:, :d])
        dkvx_ref[...] = dot_nt(dqkv_ref[:, d:], wqkv_ref[:, d:3*d]).astype(BF)
    sums_ref[0:1, :] = jnp.sum(dqkv_ref[:, :d].astype(F32), axis=0, keepdims=True)
    sums_ref[1:2, :] = jnp.sum(dqkv_ref[:, 2*d:].astype(F32), axis=0, keepdims=True)
    sums_ref[5:8, :] = jnp.zeros((3, d), F32)

def incoming(sources, targets, sems):
    return [pltpu.make_async_copy(src, dst, sems.at[k]) for k, (src, dst) in enumerate(zip(sources, targets))]


def attn_bwd_kernel(len_ref, dn_ref, qkv_hbm, o_hbm, lse_hbm, xhat_ref, r_ref, w_hbm, wo_hbm, gain_ref,
                    dres_ref, dqkv_ref, dt_ref, dkvx_ref, sums_ref, do_ref, dq_ref, qkv_ref, o_ref, lse_ref, w_ref, wo_ref, sems):
    d = dn_ref.shape[1]
    same = wo_hbm.shape[1] == d
    copies = incoming(
        (wo_hbm.at[:, wo_hbm.shape[1] - d :], qkv_hbm, o_hbm, lse_hbm, w_hbm.at[:, : 3 * d]),
        (wo_ref, qkv_ref, o_ref, lse_ref, w_ref),
        sems,
    )
    for copy in copies:
        copy.start()

    def ready(stage):
        for copy in (copies[1:4], copies[4:], copies[:1])[stage]:
            copy.wait()

    attn_bwd_body(same, lambda p: None, ready, len_ref, dn_ref, qkv_ref, o_ref, lse_ref, xhat_ref, r_ref, w_ref, wo_ref,
                  gain_ref, dres_ref, dqkv_ref, dt_ref, dkvx_ref, sums_ref, do_ref, dq_ref)


def attn_bwd(dn, saved, wqkv, wo, gain, length, same):
    qkv, o, lse, xhat, r = saved
    s, d = dn.shape
    vm = pl.BlockSpec(memory_space=pltpu.VMEM)
    sm = pl.BlockSpec(memory_space=pltpu.SMEM)
    hbm = pl.BlockSpec(memory_space=pl.ANY)
    return pl.pallas_call(
        attn_bwd_kernel,
        out_shape=(jax.ShapeDtypeStruct((s, d), F32), jax.ShapeDtypeStruct((s, 3 * d), BF), jax.ShapeDtypeStruct((s, d), BF),
                   jax.ShapeDtypeStruct((8, 128) if same else (s, d), BF), jax.ShapeDtypeStruct((8, d), F32)),
        in_specs=[sm, vm, hbm, hbm, hbm, vm, vm, hbm, hbm, vm], out_specs=(vm,) * 5,
        scratch_shapes=[pltpu.VMEM((s, d), BF), pltpu.VMEM((128, s), F32), pltpu.VMEM((s, 3 * d), BF),
                        pltpu.VMEM((s, d), BF), pltpu.VMEM((s, d), F32), pltpu.VMEM((d, 3 * d), BF),
                        pltpu.VMEM((d, d), BF), pltpu.SemaphoreType.DMA((5,))],
        compiler_params=pltpu.CompilerParams(vmem_limit_bytes=60 << 20),
    )(length.reshape(1, 1), dn, qkv, o, lse, xhat, r, wqkv, wo if same else wqkv, gain)


def gelu_parts(a):
    e = jnp.exp(-0.5 * a * a)
    t = 1.0 / (1.0 + 0.23164188624 * jnp.abs(a))
    tail = t * (0.127414796 + t * (-0.142248368 + t * (0.7107068705 + t * (-0.7265760135 + t * 0.5307027145)))) * e
    phi_cap = jnp.where(a < 0.0, tail, 1.0 - tail)
    return phi_cap, e * 0.3989422804014327

def ffn_fwd_kernel(n_ref, we_ref, wc_ref, be_ref, bias_ref, gain_ref,
                   y_ref, g_ref, gp_ref, xhat_ref, r_ref, acc_ref, low_ref):
    @pl.when(pl.program_id(0) == 0)
    def _():
        low_ref[...] = n_ref[...].astype(BF)
        acc_ref[...] = n_ref[...] + bias_ref[4:5, :]

    a = dot(low_ref[...], we_ref[...]) + be_ref[...]
    cap, dens = gelu_parts(a)
    g = (a * cap).astype(BF)
    g_ref[...] = g
    gp_ref[...] = (cap + a * dens).astype(BF)
    acc_ref[...] += dot(g, wc_ref[...])

    @pl.when(pl.program_id(0) == pl.num_programs(0) - 1)
    def _():
        xhat, r, y = norm_forward(acc_ref[...], gain_ref[1:2, :], bias_ref[5:6, :])
        xhat_ref[...] = xhat
        r_ref[...] = jnp.broadcast_to(r, r_ref.shape)
        y_ref[...] = y.astype(BF)


def whole(*shape):
    return pl.BlockSpec(shape, lambda c: (0, 0))


def ffn_fwd(n, we, wc, be, bias, gain, chunk=768):
    s, d = n.shape
    ff = we.shape[1]
    columns = pl.BlockSpec((s, chunk), lambda c: (0, c))
    return pl.pallas_call(
        ffn_fwd_kernel,
        out_shape=(jax.ShapeDtypeStruct((s, d), BF), jax.ShapeDtypeStruct((s, ff), BF), jax.ShapeDtypeStruct((s, ff), BF),
                   jax.ShapeDtypeStruct((s, d), F32), jax.ShapeDtypeStruct((s, 128), F32)),
        grid=(ff // chunk,),
        in_specs=[whole(s, d), pl.BlockSpec((d, chunk), lambda c: (0, c)), pl.BlockSpec((chunk, d), lambda c: (c, 0)),
                  pl.BlockSpec((1, chunk), lambda c: (0, c)), whole(*bias.shape), whole(*gain.shape)],
        out_specs=(whole(s, d), columns, columns, whole(s, d), whole(s, 128)),
        scratch_shapes=[pltpu.VMEM((s, d), F32), pltpu.VMEM((s, d), BF)],
        compiler_params=pltpu.CompilerParams(vmem_limit_bytes=60 << 20),
    )(n, we, wc, be.reshape(1, ff), bias, gain)


def ffn_bwd_kernel(extra, len_ref, cot_ref, dm_ref, gp_ref, xhat_ref, r_ref, we_ref, wc_ref, gain_ref,
                   dn_ref, da_ref, dt_ref, sums_ref, sume_ref):
    s, d = cot_ref.shape

    @pl.when(pl.program_id(0) == 0)
    def _():
        row = lax.broadcasted_iota(jnp.int32, (s, 1), 0)
        dy = jnp.where(row < len_ref[0, 0], cot_ref[...].astype(F32), 0.0)
        if extra:
            dy = dy + dm_ref[...].astype(F32)
        xhat = xhat_ref[...]
        du = norm_backward(dy, xhat, r_ref[:, :1], gain_ref[1:2, :])
        dt = du.astype(BF)
        dt_ref[...] = dt
        sums_ref[0:1, :] = jnp.sum(dt.astype(F32), axis=0, keepdims=True)
        sums_ref[1:2, :] = jnp.sum(dy, axis=0, keepdims=True)
        sums_ref[2:3, :] = jnp.sum(dy * xhat, axis=0, keepdims=True)
        sums_ref[3:8, :] = jnp.zeros((5, d), F32)
        dn_ref[...] = du

    dg = dot_nt(dt_ref[...], wc_ref[...])
    da = (dg * gp_ref[...].astype(F32)).astype(BF)
    da_ref[...] = da
    sume_ref[...] = jnp.sum(da.astype(F32), axis=0, keepdims=True)
    dn_ref[...] += dot_nt(da, we_ref[...])


def ffn_bwd(cot, dm, length, saved, we, wc, gain, chunk=768):
    gp, xhat, r = saved
    s, d = cot.shape
    ff = we.shape[1]
    extra = dm is not None
    sm = pl.BlockSpec(memory_space=pltpu.SMEM)
    columns = pl.BlockSpec((s, chunk), lambda c: (0, c))
    row = pl.BlockSpec((1, chunk), lambda c: (0, c))
    if not extra:
        dm = gain
    return pl.pallas_call(
        functools.partial(ffn_bwd_kernel, extra),
        out_shape=(jax.ShapeDtypeStruct((s, d), F32), jax.ShapeDtypeStruct((s, ff), BF), jax.ShapeDtypeStruct((s, d), BF),
                   jax.ShapeDtypeStruct((8, d), F32), jax.ShapeDtypeStruct((1, ff), F32)),
        grid=(ff // chunk,),
        in_specs=[sm, whole(s, d), whole(*dm.shape), columns, whole(s, d), whole(s, 128),
                  pl.BlockSpec((d, chunk), lambda c: (0, c)), pl.BlockSpec((chunk, d), lambda c: (c, 0)),
                  whole(*gain.shape)],
        out_specs=(whole(s, d), columns, whole(s, d), whole(8, d), row),
        compiler_params=pltpu.CompilerParams(vmem_limit_bytes=60 << 20),
    )(length.reshape(1, 1), cot, dm, gp, xhat, r, we, wc, gain)


MESH = pl.DeviceIdType.MESH
LAG = 2
RING = 8


def store_rows(total, out_ref):
    blocks, shards, rows, width = out_ref.shape
    halves = total.shape[1] // width
    groups = blocks // halves
    for k in range(shards):
        for j in range(groups):
            at = (k * groups + j) * rows
            for h in range(halves):
                out_ref[j * halves + h, k] = total[at : at + rows, h * width : (h + 1) * width]


def product(xs, dys):
    total = None
    for x, dy in zip(xs, dys):
        part = dot_tn(x[...].astype(BF), dy[...].astype(BF))
        total = part if total is None else total + part
    return total.astype(BF)


def wgrad_rows_kernel(n, *refs):
    store_rows(product(refs[:n], refs[n : 2 * n]), refs[2 * n])


def wgrad_rows(xs, dys, shards):
    sizes = [x.shape[0] for x in xs]
    n, k = xs[0].shape[1], dys[0].shape[1]
    width, rows = k // 2, k // shards
    groups = n // k
    return pl.pallas_call(
        functools.partial(wgrad_rows_kernel, len(xs)),
        out_shape=jax.ShapeDtypeStruct((2 * groups, shards, rows, width), BF),
        grid=(n // k,),
        in_specs=[pl.BlockSpec((s, k), lambda i: (0, i)) for s in sizes]
        + [pl.BlockSpec((s, k), lambda i: (0, 0)) for s in sizes],
        out_specs=pl.BlockSpec((2 * groups, shards // groups, rows, width), lambda i: (0, i, 0, 0)),
        compiler_params=pltpu.CompilerParams(vmem_limit_bytes=60 << 20),
    )(*xs, *dys)


def wgrad_cross_kernel(n, *refs):
    dqkv, dt, n1, mem, mixed = (refs[j * n : (j + 1) * n] for j in range(5))
    first_ref, second_ref = refs[5 * n :]
    i = pl.program_id(0)
    for at, xs, dys, out_ref in (
        (0, dqkv, n1, first_ref),
        (1, dqkv, mem, first_ref),
        (2, dqkv, mem, second_ref),
        (3, dt, mixed, second_ref),
    ):

        @pl.when(i == at)
        def _():
            store_rows(product(xs, dys), out_ref)


def wgrad_cross(dqkv, dt, n1, mem, mixed, shards):
    sizes = [x.shape[0] for x in dt]
    k = dt[0].shape[1]
    width, rows = k // 2, k // shards
    out = jax.ShapeDtypeStruct((4, shards, rows, width), BF)
    whole = [pl.BlockSpec((s, k), lambda i: (0, 0)) for s in sizes]
    return pl.pallas_call(
        functools.partial(wgrad_cross_kernel, len(sizes)),
        out_shape=(out, out),
        grid=(4,),
        in_specs=[pl.BlockSpec((s, k), lambda i: (0, jnp.minimum(i, 2))) for s in sizes] + whole * 4,
        out_specs=(
            pl.BlockSpec((4, shards // 2, rows, width), lambda i: (0, jnp.minimum(i, 1), 0, 0)),
            pl.BlockSpec((4, shards // 2, rows, width), lambda i: (0, jnp.maximum(i - 2, 0), 0, 0)),
        ),
        compiler_params=pltpu.CompilerParams(vmem_limit_bytes=60 << 20),
    )(*dqkv, *dt, *n1, *mem, *mixed)


def reduce_kernel(counts, *refs):
    (len_ref, dn_ref, qkv_hbm, o_hbm, lse_hbm, xhat_ref, r_ref, w_hbm, wo_ref, gain_ref) = refs[:10]
    (contract, cross_first, cross_second) = refs[15:18]
    ffn_refs = (refs[18:22], refs[22:26])
    (ssum_ref, fsum_ref, esum_ref, csum_ref) = refs[26:30]
    (dres_ref, in_ref, out_ref, expand_ref, contract_ref, cross_ref, vsum_ref, landed) = refs[30:38]
    (dqkv_ref, dt_ref, do_ref, dq_ref, sums_ref, made, own, r0, r1, r2, r3, vbuf, vrecv) = refs[38:51]
    (n0_buf, n1_buf, da0_buf, da1_buf) = refs[51:55]
    held = refs[55:64]
    (qkv_ref, o_ref, lse_ref, wqkv_ref, x0_ref, x_ref, dqkv0_ref, o0_ref, dt0_ref) = held
    send_sem, recv_sem, local_sem, vsend_sem, vrecv_sem, xsend_sem, xrecv_sem, fetch_sem, held_sem = refs[64:]
    copies = incoming((qkv_hbm, o_hbm, lse_hbm, w_hbm, *refs[10:15]), held, held_sem)
    for copy in copies[:3]:
        copy.start()
    d = dn_ref.shape[1]
    n_ffn, n_in, n_out, n_cross = 2 * counts[0], counts[1], counts[2], counts[3]
    blocks = n_ffn + n_in + n_out + n_cross
    rows, width = own.shape[-2:]
    second = lax.axis_index("section") == 1
    me = lax.axis_index("dp")
    c, y, zl, zh = me % 2, (me // 2) % 2, (me // 4) % 2, me // 8
    mates = (me + 1 - 2 * c, me + 2 - 4 * y, me + 4 - 8 * zl, me + 8 - 16 * zh)
    barrier = pltpu.get_barrier_semaphore()
    for mate in mates:
        pl.semaphore_signal(barrier, inc=1, device_id={"dp": mate}, device_id_type=MESH)
    across = 1 - lax.axis_index("section")
    pl.semaphore_signal(barrier, inc=1, device_id={"section": across}, device_id_type=MESH)

    def chosen(visit):
        for which, here in enumerate((jnp.logical_not(second), second)):

            @pl.when(here)
            def _():
                visit(ffn_refs[which])

    def fetch_norms(from_refs):
        return [
            pltpu.make_async_copy(from_refs[k], (n0_buf, n1_buf)[k], fetch_sem.at[2, k]) for k in range(2)
        ]

    def fetch_columns(from_refs, i):
        at = pl.ds(pl.multiple_of(i * d, 128), d)
        return [
            pltpu.make_async_copy(
                from_refs[2 + k].at[:, at], (da0_buf, da1_buf)[k].at[i % 2], fetch_sem.at[i % 2, k]
            )
            for k in range(2)
        ]

    def begin_fetch(from_refs):
        for copy in fetch_norms(from_refs) + fetch_columns(from_refs, 0) + fetch_columns(from_refs, 1):
            copy.start()

    chosen(begin_fetch)
    for copy in copies[3:]:
        copy.start()
    pl.semaphore_wait(barrier, 5)

    def over(j):
        return pltpu.make_async_remote_copy(
            src_ref=cross_first.at[j],
            dst_ref=landed.at[j],
            send_sem=xsend_sem.at[j],
            recv_sem=xrecv_sem.at[j],
            device_id={"section": across},
            device_id_type=MESH,
        )

    @pl.when(second)
    def _():
        for j in (*range(n_cross // 2, n_cross), *range(n_cross // 2)):
            over(j).start()

    order = ((0, 1, 2, 3), (0, 2, 3, 1))

    def remote(src, dst, stage, b, color):
        return pltpu.make_async_remote_copy(
            src_ref=src,
            dst_ref=dst,
            send_sem=send_sem.at[stage, b],
            recv_sem=recv_sem.at[stage, b],
            device_id={"dp": mates[order[color][stage]]},
            device_id_type=MESH,
        )

    turned = blocks // 7
    half = turned // 2
    steps = blocks - turned
    gap = 3
    early = counts[0] - half

    def slot(b, color):
        if color == 0:
            return (b - jnp.where(b >= early, half, 0)) % RING
        return RING + jnp.where(b < steps, b - early, b - steps)

    def first_copy(part, at, b, color):
        return remote(part.at[at, :, :, :, 1 - c], r0.at[slot(b, color)], 0, b, color)

    def local_copy(part, at, b):
        return pltpu.make_async_copy(part.at[at, :, :, :, c], own.at[b], local_sem.at[b])

    def copy_of(stage, b, color):
        if color == 0:
            src = (own.at[b, :, :, 1 - y], own.at[b, :, 1 - zl, y], own.at[b, 1 - zh, zl, y])
        else:
            src = (own.at[b, :, 1 - zl], own.at[b, 1 - zh, zl], own.at[b, zh, zl, 1 - y])
        return remote(src[stage - 1], (r1, r2, r3)[stage - 1].at[b], stage, b, color)

    def add(left, right):
        return (left.astype(F32) + right.astype(F32)).astype(BF)

    def column(at):
        return pl.ds(pl.multiple_of(at * width, 128), width)

    def put_columns(ref, at, value):
        ref[:, column(at)] = value

    def put_groups(ref, at, value):
        ref[pl.ds(pl.multiple_of((at // 2) * rows, 8), rows), column(at % 2)] = value

    plan = (
        (((contract, None),), counts[0], put_groups, contract_ref),
        (((made, None),), counts[0], put_columns, expand_ref),
        (((made, None),), n_in, put_columns, in_ref),
        (((made, None),), n_out, put_columns, out_ref),
        (((landed, jnp.logical_not(second)), (cross_second, second)), n_cross, put_groups, cross_ref),
    )

    def each(b, visit):
        low = 0
        for sources, count, put, target in plan:
            inside = (b >= low) & (b < low + count)
            at = b % counts[0] if sources[0][0] is made else b - low
            visit(inside, sources, at, put, target, b - low)
            low += count

    def settle(stage, b, color):
        if stage == 0:
            first_copy(contract, 0, b, color).wait()
            local_copy(contract, 0, b).wait()
            own[b] = add(own[b], r0[slot(b, color)])
            return
        copy_of(stage, b, color).wait()
        if stage == 1:
            if color == 0:
                own[b, :, :, y] = add(own[b, :, :, y], r1[b])
            else:
                own[b, :, zl] = add(own[b, :, zl], r1[b])
        elif stage == 2:
            if color == 0:
                own[b, :, zl, y] = add(own[b, :, zl, y], r2[b])
            else:
                own[b, zh, zl] = add(own[b, zh, zl], r2[b])
        else:
            total = own[b, zh, zl, y].astype(F32) + r3[b].astype(F32)

            def finish(inside, sources, at, put, target, place):
                @pl.when(inside)
                def _():
                    put(target, place, total)

            each(b, finish)

    def vcopy(j):
        return pltpu.make_async_remote_copy(
            src_ref=vbuf.at[j],
            dst_ref=vrecv.at[j],
            send_sem=vsend_sem.at[j],
            recv_sem=vrecv_sem.at[j],
            device_id={"dp": mates[j]},
            device_id_type=MESH,
        )

    def advance(stage, b, color):
        if stage == 0:

            def launch(inside, sources, at, put, target, place):
                for part, here in sources:

                    @pl.when(inside if here is None else inside & here)
                    def _():
                        if part is landed:
                            over(at).wait_recv()
                        first_copy(part, at, b, color).start()
                        local_copy(part, at, b).start()

            each(b, launch)
            return
        settle(stage - 1, b, color)
        if stage < 4:
            copy_of(stage, b, color).start()

    def step(it, _):
        for stage in range(5):
            at = it - LAG * stage

            @pl.when((at >= 0) & (at < steps))
            def _():
                advance(stage, at + jnp.where(at >= early, half, 0), 0)

            @pl.when((at >= 0) & (at < turned * gap) & (at % gap == 1))
            def _():
                j = at // gap
                advance(stage, jnp.where(j < half, early, steps) + j, 1)

        return 0

    def some(low, high):
        lax.fori_loop(low, high, step, 0)

    def keep(block, total):
        for h in range(2):
            made[block + h] = total[:, h * width : (h + 1) * width].reshape(made.shape[1:]).astype(BF)

    pairs, chunks = d // 128, counts[0] // 2

    def beside(p):
        @pl.when(p < chunks)
        def _():
            @pl.when(p == 0)
            def _():
                for copy in fetch_norms(ffn_refs[0]):
                    copy.wait()

            for copy in fetch_columns(ffn_refs[0], p):
                copy.wait()
            keep(
                2 * p,
                dot_tn(n0_buf[...].astype(BF), da0_buf[p % 2]) + dot_tn(n1_buf[...].astype(BF), da1_buf[p % 2]),
            )

            def next_fetch(from_refs):
                for copy in fetch_columns(from_refs, p + 2):
                    copy.start()

            @pl.when(p + 2 < chunks)
            def _():
                chosen(next_fetch)

        some(jnp.minimum(3 + 2 * p, 7 + p), jnp.minimum(5 + 2 * p, 8 + p))

    def ready(stage):
        for copy in (copies[:3], copies[3:], ())[stage]:
            copy.wait()

    some(0, 3)
    attn_bwd_body(
        True, beside, ready,
        len_ref, dn_ref, qkv_ref, o_ref, lse_ref, xhat_ref, r_ref, wqkv_ref, wo_ref, gain_ref,
        dres_ref, dqkv_ref, dt_ref, None, sums_ref, do_ref, dq_ref,
    )
    after = 7 + pairs
    vbuf[0, 0:4] = sums_ref[0:4, :] + ssum_ref[0:4, :]
    vbuf[0, 4:6] = fsum_ref[0:2, :]
    vbuf[0, 6:7] = sums_ref[4:5, :] + ssum_ref[4:5, :]
    vbuf[0, 7:8] = fsum_ref[2:3, :]
    count = esum_ref.shape[1] // d
    for j in range(count):
        vbuf[0, 8 + j : 9 + j] = esum_ref[:, j * d : (j + 1) * d]
    vbuf[0, 8 + count : 13 + count] = csum_ref[0:5, :]
    vbuf[0, 13 + count :] = jnp.zeros((vbuf.shape[1] - 13 - count, d), F32)
    def weight(i, _):
        at = pl.ds(pl.multiple_of(i * d, 128), d)
        keep(2 * i, dot_tn(x0_ref[...], dqkv0_ref[:, at]) + dot_tn(x_ref[...], dqkv_ref[:, at]))
        step(after + i, 0)
        return 0

    lax.fori_loop(0, n_in // 2, weight, 0)
    keep(n_in, dot_tn(o0_ref[...], dt0_ref[...]) + dot_tn(o_ref[...], dt_ref[...]))
    begin = after + n_in // 2
    vcopy(0).start()

    def rest(it, _):
        step(it, 0)
        for j in range(4):

            @pl.when(it == begin + LAG * (j + 1))
            def _():
                vcopy(j).wait()
                vbuf[j + 1] = vbuf[j] + vrecv[j]
                if j < 3:
                    vcopy(j + 1).start()

        return 0

    lax.fori_loop(begin, steps + 4 * LAG, rest, 0)
    vsum_ref[...] = vbuf[4]

    @pl.when(second)
    def _():
        for j in range(n_cross):
            over(j).wait_send()


def reduce_scatter(length, dn, saved, w_in, w_out, gain, x0, x1, dqkv0, o0, dt0, parts, encoder, decoder, sums):
    s, d = dn.shape
    rows, width = parts[0].shape[-2:]
    n_in, n_out = dqkv0.shape[1] // width, dt0.shape[1] // width
    counts = (parts[0].shape[0], n_in, n_out, parts[1].shape[0])
    blocks = 2 * counts[0] + sum(counts[1:])
    parts = [part.reshape(part.shape[0], 2, 2, 2, 2, rows, width) for part in parts]
    short = x0.shape[0]
    vec = (24, d)
    vm = pl.BlockSpec(memory_space=pltpu.VMEM)
    sm = pl.BlockSpec(memory_space=pltpu.SMEM)
    hbm = pl.BlockSpec(memory_space=pl.ANY)
    shapes = ((s, d), (rows, n_in * width), (rows, n_out * width), (rows, counts[0] * width),
              (counts[0] // 2 * rows, d), (counts[3] // 2 * rows, d), vec)
    return pl.pallas_call(
        functools.partial(reduce_kernel, counts),
        out_shape=(*(jax.ShapeDtypeStruct(shape, F32) for shape in shapes), jax.ShapeDtypeStruct(parts[1].shape, BF)),
        in_specs=[sm, vm, hbm, hbm, hbm, vm, vm, hbm, vm, vm] + [hbm] * 16 + [vm] * 4,
        out_specs=(*(vm,) * 7, hbm),
        scratch_shapes=[
            pltpu.VMEM((s, 3 * d), BF),
            pltpu.VMEM((s, d), BF),
            pltpu.VMEM((s, d), BF),
            pltpu.VMEM((128, s), F32),
            pltpu.VMEM((8, d), F32),
            pltpu.VMEM((counts[0], 2, 2, 2, 2, rows, width), BF),
            pltpu.VMEM((blocks, 2, 2, 2, rows, width), BF),
            pltpu.VMEM((RING + blocks // 7, 2, 2, 2, rows, width), BF),
            pltpu.VMEM((blocks, 2, 2, rows, width), BF),
            pltpu.VMEM((blocks, 2, rows, width), BF),
            pltpu.VMEM((blocks, rows, width), BF),
            pltpu.VMEM((5, *vec), F32),
            pltpu.VMEM((4, *vec), F32),
            pltpu.VMEM((short, d), F32),
            pltpu.VMEM((s, d), F32),
            pltpu.VMEM((2, short, d), BF),
            pltpu.VMEM((2, s, d), BF),
            pltpu.VMEM((s, 3 * d), BF),
            pltpu.VMEM((s, d), BF),
            pltpu.VMEM((s, d), F32),
            pltpu.VMEM((d, 3 * d), BF),
            pltpu.VMEM((short, d), BF),
            pltpu.VMEM((s, d), BF),
            pltpu.VMEM((short, 3 * d), BF),
            pltpu.VMEM((short, d), BF),
            pltpu.VMEM((short, d), BF),
            pltpu.SemaphoreType.DMA((4, blocks)),
            pltpu.SemaphoreType.DMA((4, blocks)),
            pltpu.SemaphoreType.DMA((blocks,)),
            pltpu.SemaphoreType.DMA((4,)),
            pltpu.SemaphoreType.DMA((4,)),
            pltpu.SemaphoreType.DMA((counts[3],)),
            pltpu.SemaphoreType.DMA((counts[3],)),
            pltpu.SemaphoreType.DMA((3, 2)),
            pltpu.SemaphoreType.DMA((9,)),
        ],
        compiler_params=pltpu.CompilerParams(collective_id=0, has_side_effects=True, vmem_limit_bytes=67043328),
    )(length.reshape(1, 1), dn, *saved, w_in, w_out, gain, x0, x1, dqkv0, o0, dt0, *parts, *encoder, *decoder, *sums)[:7]


def shards(
    inputs_long,
    inputs_short,
    cotangent_long,
    cotangent_short,
    lengths_long,
    lengths_short,
    self_in_weight,
    self_out_weight,
    expand_weight,
    contract_weight,
    expand_bias,
    layer_biases,
    layer_gains,
    cross_weight,
    cross_biases,
    cross_gain,
):
    decoder = lax.axis_index("section") == 1
    d = inputs_long.shape[-1]
    ff = expand_weight.shape[2]
    w_in, w_out, w_e, w_c = self_in_weight[0], self_out_weight[0], expand_weight[0], contract_weight[0]
    b_e, bias, gain = expand_bias[0], layer_biases[0], layer_gains[0]
    c_gain = cross_gain.reshape(1, d)

    xs = (inputs_short[0, 0], inputs_long[0, 0])
    cots = (cotangent_short[0, 0], cotangent_long[0, 0])
    source = (lengths_short[0, 0], lengths_long[0, 0])
    target = (lengths_short[1, 0], lengths_long[1, 0])
    sizes = tuple(x.shape[0] for x in xs)

    own = tuple(jnp.where(decoder, t, o) for t, o in zip(target, source))

    def attend(i):
        x = xs[i]
        return attn_fwd(x, None, x, w_in, w_out, bias, gain, own[i])

    def encode_ffn(i, n):
        s = sizes[i]

        def decode():
            return blank(((s, d), BF), ((s, ff), BF), ((s, ff), BF), ((s, d), F32), ((s, 128), F32))

        return lax.cond(decoder, decode, lambda: ffn_fwd(n, w_e, w_c, b_e, bias, gain))

    def send(value, steps):
        return lax.ppermute(value, "section", [(0, 1)] if steps > 0 else [(1, 0)])

    def cross(i, memory, n1):
        s = sizes[i]

        def encode():
            return blank(
                ((s, 3 * d), BF), ((s, d), BF), ((s, d), F32), ((s, d), F32), ((s, 128), F32), ((s, d), F32)
            )

        def decode():
            return attn_fwd(n1, memory, n1, cross_weight, None, cross_biases, c_gain, source[i])

        return lax.cond(decoder, decode, encode)

    def turn(i, out):
        s = sizes[i]

        def decode():
            y, g, gp, xhat, r = ffn_fwd(out[5], w_e, w_c, b_e, bias, gain)
            fb = ffn_bwd(cots[i], None, target[i], (gp, xhat, r), w_e, w_c, gain)
            ab = attn_bwd(fb[0], out[:5], cross_weight, None, c_gain, source[i], False)
            return (g, fb[1], fb[2], ab[1], ab[2]), ab[0], ab[3], y, (fb[3], fb[4], ab[4])

        def encode():
            out = blank(
                ((s, ff), BF),
                ((s, ff), BF),
                ((s, d), BF),
                ((s, 3 * d), BF),
                ((s, d), BF),
                ((s, d), F32),
                ((s, d), BF),
                ((s, d), BF),
                ((8, d), F32),
                ((1, ff), F32),
                ((8, d), F32),
            )
            return tuple(out[:5]), out[5], out[6], out[7], tuple(out[8:])

        return lax.cond(decoder, decode, encode)

    att0 = attend(0)
    ffn0 = encode_ffn(0, att0[5])
    mem0 = send(ffn0[0], 1)
    x_long, _ = lax.optimization_barrier((xs[1], ffn0[0]))
    xs = (xs[0], x_long)
    att1 = attend(1)
    n_long, mem0 = lax.optimization_barrier((att1[5], mem0))
    ffn1 = encode_ffn(1, n_long)
    mem1 = send(ffn1[0], 1)
    n_short, _ = lax.optimization_barrier((att0[5], ffn1[0]))
    out0 = cross(0, mem0, n_short)
    keep0, dn0, dm0, y0, sums0 = turn(0, out0)
    back0 = send(dm0, -1)
    n_long, _ = lax.optimization_barrier((att1[5], dm0))
    out1 = cross(1, mem1, n_long)
    n_long, back0 = lax.optimization_barrier((out1[5], back0))
    out1 = (*out1[:5], n_long)
    keep1, dn1, dm1, y1, sums1 = turn(1, out1)
    back1 = send(dm1, -1)
    dp = lax.axis_size("dp")
    staged = dp == 16 and d % (16 * dp) == 0 and d == 6 * 128 and ff == 4 * d

    def cross_grads():
        n1, mem = (att0[5], att1[5]), (mem0, mem1)
        dqkv, dt = ((keep0[j], keep1[j]) for j in (3, 4))
        mixed = (out0[1], out1[1])
        if staged:
            return wgrad_cross(dqkv, dt, n1, mem, mixed, dp)
        joint = jnp.concatenate(dqkv, 0)
        low = jnp.concatenate(n1, 0).astype(BF)
        mem = jnp.concatenate(mem, 0)
        rows = (
            dot_tn(joint[:, :d], low),
            dot_tn(joint[:, d : 2 * d], mem),
            dot_tn(joint[:, 2 * d :], mem),
            dot_tn(jnp.concatenate(dt, 0), jnp.concatenate(mixed, 0)),
        )
        return tuple(jnp.concatenate(rows[j : j + 2], 0).astype(BF) for j in (0, 2))

    def cross_blank():
        shape = (4, dp, d // dp, d // 2) if staged else (2 * d, d)
        return tuple(blank((shape, BF), (shape, BF)))

    cross_sums = sums0[2] + sums1[2]
    cross_first, cross_second = lax.cond(decoder, cross_grads, cross_blank)
    back0, _ = lax.optimization_barrier((back0, cross_first))
    dn0, *enc0 = lax.cond(
        decoder,
        lambda: (dn0, *blank(((sizes[0], ff), BF), ((sizes[0], d), BF), ((8, d), F32), ((1, ff), F32))),
        lambda: tuple(ffn_bwd(cots[0], back0, source[0], ffn0[2:], w_e, w_c, gain)),
    )
    self0 = attn_bwd(dn0, att0[:5], w_in, w_out, gain, own[0], True)
    back1, cross_sent, _ = lax.optimization_barrier((back1, send(cross_sums, -1), self0[0]))
    cross_rows = jnp.where(decoder, cross_sums, cross_sent)

    def plain(left, right):
        left, right = (jnp.concatenate([e.astype(BF) for e in side], 0) for side in (left, right))
        return dot_tn(left, right).astype(BF)

    def contract_grad(g, dt):
        return wgrad_rows(g, dt, dp) if staged else plain(g, dt)

    def decode_last():
        grad = contract_grad((keep0[0], keep1[0]), (keep0[2], keep1[2]))
        return dn1, *blank(((sizes[1], ff), BF)), grad, sums0[0] + sums1[0], sums0[1] + sums1[1]

    def encode_last():
        dn, da, dt, sums, sum_e = ffn_bwd(cots[1], back1, source[1], ffn1[2:], w_e, w_c, gain)
        return dn, da, contract_grad((ffn0[1], ffn1[1]), (enc0[1], dt)), enc0[2] + sums, enc0[3] + sum_e

    dn1, enc_da, g_contract, ffn_sums, sum_e = lax.cond(decoder, decode_last, encode_last)
    if staged:
        dx1, *big, rows = reduce_scatter(
            own[1], dn1, att1[:5], w_in, w_out, gain, xs[0], xs[1], self0[1], att0[1], self0[2],
            (g_contract, cross_first, cross_second),
            (att0[5], att1[5], enc0[0], enc_da),
            (out0[5], out1[5], keep0[1], keep1[1]),
            (self0[4], ffn_sums, sum_e, cross_rows),
        )
    else:
        self1 = attn_bwd(dn1, att1[:5], w_in, w_out, gain, own[1], True)
        dx1 = self1[0]
        self_sums = self0[4] + self1[4]
        rows = [self_sums[0:4], ffn_sums[0:2], self_sums[4:5], ffn_sums[2:3], sum_e.reshape(ff // d, d), cross_rows[0:5]]
        rows = lax.psum(jnp.concatenate(rows, 0), "dp")
        cross_mine = jnp.where(decoder, cross_second, send(cross_first, -1))
        pairs = (((att0[5], enc0[0]), (att1[5], enc_da)), ((out0[5], keep0[1]), (out1[5], keep1[1])))
        g_expand = lax.cond(decoder, lambda: plain(*zip(*pairs[1])), lambda: plain(*zip(*pairs[0])))
        in_grad = plain(xs, (self0[1], self1[1]))
        out_grad = plain((att0[1], att1[1]), (self0[2], self1[2]))
        big = [
            lax.psum_scatter(part, "dp", scatter_dimension=0, tiled=True).astype(F32)
            for part in (in_grad, out_grad, g_expand, g_contract, cross_mine)
        ]
    count = 8 + ff // d
    me = lax.axis_index("dp")
    piece = lax.dynamic_slice_in_dim(rows[:8], me * (d // dp), d // dp, 1)
    e_piece = lax.dynamic_slice_in_dim(rows[8:count].reshape(1, ff), me * (ff // dp), ff // dp, 1)
    outs = [jnp.where(decoder, y, e)[None, None] for y, e in ((y0, ffn0[0]), (y1, ffn1[0]))]
    return (
        outs[1],
        outs[0],
        dx1[None, None],
        self0[0][None, None],
        big[0][None],
        big[1][None],
        big[2][None],
        big[3][None],
        e_piece,
        piece[None, :6],
        piece[None, 6:8],
        big[4].T,
        rows[count : count + 4],
        rows[count + 4],
    )


def solution(mesh):
    in_specs = (
        P("section", "dp", None, None),
        P("section", "dp", None, None),
        P("section", "dp", None, None),
        P("section", "dp", None, None),
        P(None, "dp"),
        P(None, "dp"),
        P("section", None, None),
        P("section", None, None),
        P("section", None, None),
        P("section", None, None),
        P("section", None),
        P("section", None, None),
        P("section", None, None),
        P(),
        P(),
        P(),
    )
    out_specs = (
        P("section", "dp", None, None),
        P("section", "dp", None, None),
        P("section", "dp", None, None),
        P("section", "dp", None, None),
        P("section", "dp", None),
        P("section", "dp", None),
        P("section", "dp", None),
        P("section", "dp", None),
        P("section", "dp"),
        P("section", None, "dp"),
        P("section", None, "dp"),
        P(None, ("section", "dp")),
        P(),
        P(),
    )
    return jax.shard_map(shards, mesh=mesh, in_specs=in_specs, out_specs=out_specs, check_vma=False)
```

```python
import functools
import jax
import jax.numpy as jnp
from jax import lax
from jax.experimental import pallas as pl
from jax.experimental.pallas import tpu as pltpu
from jax.sharding import PartitionSpec as P

BF, F32 = jnp.bfloat16, jnp.float32
NEG = -1e30
NT = (((1,), (1,)), ((), ()))
TN = (((0,), (0,)), ((), ()))

def dot(a, b):
    return jnp.dot(a, b, preferred_element_type=F32)
def dot_nt(a, b):
    return lax.dot_general(a, b, NT, preferred_element_type=F32)
def dot_tn(a, b):
    return lax.dot_general(a, b, TN, preferred_element_type=F32)

def lanes(rows):
    return lax.broadcasted_iota(jnp.int32, (rows, 128), 1)

def split3(v):
    hi = v.astype(BF)
    rest = v - hi.astype(F32)
    mid = rest.astype(BF)
    low = (rest - mid.astype(F32)).astype(BF)
    return hi, mid, low

def blank(*shapes):
    def nothing(*refs):
        pass

    return pl.pallas_call(
        nothing,
        out_shape=[jax.ShapeDtypeStruct(shape, kind) for shape, kind in shapes],
        out_specs=[pl.BlockSpec(memory_space=pl.ANY)] * len(shapes),
    )()


def norm_forward(u, gain, shift):
    mean = jnp.mean(u, axis=-1, keepdims=True)
    c = u - mean
    r = lax.rsqrt(jnp.mean(c * c, axis=-1, keepdims=True) + 1e-5)
    xhat = c * r
    return xhat, r, xhat * gain + shift

def incoming(sources, targets, sems):
    return [pltpu.make_async_copy(src, dst, sems.at[k]) for k, (src, dst) in enumerate(zip(sources, targets))]


def causal_shift(size):
    return jnp.where(lax.axis_index("section") == 1, 0, size)


def attn_fwd_kernel(same, len_ref, xq_ref, *refs):
    xkv_ref, refs = (xq_ref, refs) if same else (refs[0], refs[1:])
    (w_hbm, wo_hbm, bias_ref, gain_ref, qkv_hbm, o_hbm, lse_hbm, xhat_ref, r_ref, n_ref) = refs[:10]
    (qkv_ref, o_ref, lse_ref, w_ref, wo_ref, in_sems, out_sems) = refs[10:]
    s, d = xq_ref.shape
    parts = [slice(j * d, (j + 1) * d) for j in range(3)]
    weights = incoming(
        (*(w_hbm.at[:, part] for part in parts), wo_hbm.at[:, wo_hbm.shape[1] - d :]),
        (*(w_ref.at[:, part] for part in parts), wo_ref),
        in_sems,
    )
    results = incoming((qkv_ref, o_ref, lse_ref), (qkv_hbm, o_hbm, lse_hbm), out_sems)
    for copy in weights:
        copy.start()
    xq = xq_ref[...].astype(BF)
    xkv = xq if same else xkv_ref[...]
    for x, part, weight, shift in zip((xq, xkv, xkv), parts, weights, (bias_ref[0:1, :], None, bias_ref[1:2, :])):
        weight.wait()
        total = dot(x, w_ref[:, part])
        qkv_ref[:, part] = (total if shift is None else total + shift).astype(BF)
    results[0].start()
    length = len_ref[0, 0]
    lane = lanes(s)
    row = lax.broadcasted_iota(jnp.int32, (s, 128), 0)
    key_bias = jnp.where(row < length, 0.0, NEG).astype(BF)
    if same:
        tri = lax.broadcasted_iota(jnp.int32, (s, s), 1) <= lax.broadcasted_iota(jnp.int32, (s, s), 0) + causal_shift(s)
    one = jnp.ones((s, 128), BF)
    zero = jnp.zeros((s, 128), BF)

    def pair(p, _):
        at = pl.multiple_of(p * 128, 128)
        q = qkv_ref[:, pl.ds(at, 128)] * jnp.asarray(0.125, BF)
        k = qkv_ref[:, pl.ds(d + at, 128)]
        v = qkv_ref[:, pl.ds(2 * d + at, 128)]
        outs, lses = [], []
        for h in range(2):
            mine = (lane < 64) if h == 0 else (lane >= 64)
            other = 64 if h == 0 else 0
            qh = jnp.where(mine, q, jnp.where(lane == other, one, zero))
            kh = jnp.where(mine, k, jnp.where(lane == other, key_bias, zero))
            sc = dot_nt(qh, kh)
            if same:
                sc = jnp.where(tri, sc, NEG)
            m = jnp.max(sc, axis=-1, keepdims=True)
            e = jnp.exp(sc - m)
            l = jnp.sum(e, axis=-1, keepdims=True)
            outs.append(dot(e.astype(BF), v) * (1.0 / l))
            lses.append(m + jnp.log(l))
        o_ref[:, pl.ds(at, 128)] = jnp.where(lane < 64, outs[0], outs[1]).astype(BF)
        lse_ref[:, pl.ds(at, 128)] = jnp.where(lane < 64, lses[1], lses[0])
        return 0
    lax.fori_loop(0, d // 128, pair, 0)
    for copy in results[1:]:
        copy.start()
    weights[3].wait()
    u = xq_ref[...].astype(F32) + dot(o_ref[...], wo_ref[...]) + bias_ref[2:3, :]
    xhat, r, n = norm_forward(u, gain_ref[0:1, :], bias_ref[3:4, :])
    xhat_ref[...] = xhat
    r_ref[...] = jnp.broadcast_to(r, r_ref.shape)
    n_ref[...] = n
    for copy in results:
        copy.wait()


def attn_fwd(xq, xkv, wqkv, wo, bias, gain, length):
    s, d = xq.shape
    same = xkv is None
    vm = pl.BlockSpec(memory_space=pltpu.VMEM)
    sm = pl.BlockSpec(memory_space=pltpu.SMEM)
    hbm = pl.BlockSpec(memory_space=pl.ANY)
    rows = (xq,) if same else (xq, xkv)
    return pl.pallas_call(
        functools.partial(attn_fwd_kernel, same),
        out_shape=(jax.ShapeDtypeStruct((s, 3 * d), BF), jax.ShapeDtypeStruct((s, d), BF), jax.ShapeDtypeStruct((s, d), F32),
                   jax.ShapeDtypeStruct((s, d), F32), jax.ShapeDtypeStruct((s, 128), F32), jax.ShapeDtypeStruct((s, d), F32)),
        in_specs=[sm] + [vm] * len(rows) + [hbm, hbm, vm, vm], out_specs=(hbm, hbm, hbm, vm, vm, vm),
        scratch_shapes=[pltpu.VMEM((s, 3 * d), BF), pltpu.VMEM((s, d), BF), pltpu.VMEM((s, d), F32),
                        pltpu.VMEM((d, 3 * d), BF), pltpu.VMEM((d, d), BF),
                        pltpu.SemaphoreType.DMA((4,)), pltpu.SemaphoreType.DMA((3,))],
        compiler_params=pltpu.CompilerParams(vmem_limit_bytes=60 << 20),
    )(length.reshape(1, 1), *rows, wqkv, wqkv if wo is None else wo, bias, gain)

def norm_backward(dn, xhat, r, gain):
    h = dn * gain
    return r * (h - jnp.mean(h, axis=-1, keepdims=True) - xhat * jnp.mean(h * xhat, axis=-1, keepdims=True))

def attn_bwd_body(same, between, ready, len_ref, dn_ref, qkv_ref, o_ref, lse_ref, xhat_ref, r_ref, wqkv_ref, wo_ref, gain_ref,
                  dres_ref, dqkv_ref, dt_ref, dkvx_ref, sums_ref, do_ref, dq_ref):
    s, d = dn_ref.shape
    dn = dn_ref[...]
    xhat = xhat_ref[...]
    du = norm_backward(dn, xhat, r_ref[:, :1], gain_ref[0:1, :])
    dt = du.astype(BF)
    dt_ref[...] = dt
    sums_ref[2:3, :] = jnp.sum(dt.astype(F32), axis=0, keepdims=True)
    sums_ref[3:4, :] = jnp.sum(dn, axis=0, keepdims=True)
    sums_ref[4:5, :] = jnp.sum(dn * xhat, axis=0, keepdims=True)
    dres_ref[...] = du
    ready(2)
    do_ref[...] = dot_nt(dt, wo_ref[...]).astype(BF)
    length = len_ref[0, 0]
    lane = lanes(s)
    row = lax.broadcasted_iota(jnp.int32, (s, 128), 0)
    key_bias = jnp.where(row < length, 0.0, NEG).astype(BF)
    if same:
        tri = lax.broadcasted_iota(jnp.int32, (s, s), 0) <= lax.broadcasted_iota(jnp.int32, (s, s), 1) + causal_shift(s)
    one = jnp.ones((s, 128), BF)
    zero = jnp.zeros((s, 128), BF)

    def place(base, mine, other, extra):
        out = zero
        for j, val in enumerate(extra):
            out = jnp.where(lane == other + j, val, out)
        return jnp.where(mine, base, out)

    def pair(p, _):
        between(p)
        at = pl.multiple_of(p * 128, 128)
        q = qkv_ref[:, pl.ds(at, 128)] * jnp.asarray(0.125, BF)
        k = qkv_ref[:, pl.ds(d + at, 128)]
        v = qkv_ref[:, pl.ds(2 * d + at, 128)]
        do = do_ref[:, pl.ds(at, 128)]
        lse3 = split3(-lse_ref[:, pl.ds(at, 128)])
        prod = do.astype(F32) * o_ref[:, pl.ds(at, 128)].astype(F32)
        dq, dk, dv = [], [], []
        for h in range(2):
            mine = (lane < 64) if h == 0 else (lane >= 64)
            other = 64 if h == 0 else 0
            inner = jnp.broadcast_to(jnp.sum(jnp.where(mine, prod, 0.0), axis=-1, keepdims=True), (s, 128))
            qh = place(q, mine, other, (*lse3, one))
            kh = place(k, mine, other, (one, one, one, key_bias))
            doh = place(do, mine, other, split3(-inner))
            vh = place(v, mine, other, (one, one, one))
            st = dot_nt(kh, qh)
            if same:
                st = jnp.where(tri, st, NEG)
            pt = jnp.exp(st)
            dst = (pt * dot_nt(vh, doh)).astype(BF)
            dv.append(dot(pt.astype(BF), do))
            dk.append(dot(dst, q))
            dq.append(dot_tn(k, dst))
        m1 = lane < 64
        dq_ref[...] = jnp.where(lax.broadcasted_iota(jnp.int32, (128, s), 0) < 64, dq[0], dq[1])
        dqkv_ref[:, pl.ds(at, 128)] = (dq_ref[...].T * 0.125).astype(BF)
        dqkv_ref[:, pl.ds(d + at, 128)] = jnp.where(m1, dk[0], dk[1]).astype(BF)
        dqkv_ref[:, pl.ds(2 * d + at, 128)] = jnp.where(m1, dv[0], dv[1]).astype(BF)
        return 0
    ready(0)
    lax.fori_loop(0, d // 128, pair, 0)
    ready(1)
    if same:
        dres_ref[...] += dot_nt(dqkv_ref[...], wqkv_ref[...])
    else:
        dres_ref[...] += dot_nt(dqkv_ref[:, :d], wqkv_ref[:, :d])
        dkvx_ref[...] = dot_nt(dqkv_ref[:, d:], wqkv_ref[:, d:3*d]).astype(BF)
    sums_ref[0:1, :] = jnp.sum(dqkv_ref[:, :d].astype(F32), axis=0, keepdims=True)
    sums_ref[1:2, :] = jnp.sum(dqkv_ref[:, 2*d:].astype(F32), axis=0, keepdims=True)
    sums_ref[5:8, :] = jnp.zeros((3, d), F32)

def attn_bwd_kernel(len_ref, dn_ref, qkv_hbm, o_hbm, lse_hbm, xhat_ref, r_ref, w_hbm, wo_hbm, gain_ref,
                    dres_ref, dqkv_ref, dt_ref, dkvx_ref, sums_ref, do_ref, dq_ref, qkv_ref, o_ref, lse_ref, w_ref, wo_ref, sems):
    d = dn_ref.shape[1]
    same = wo_hbm.shape[1] == d
    copies = incoming(
        (wo_hbm.at[:, wo_hbm.shape[1] - d :], qkv_hbm, o_hbm, lse_hbm, w_hbm.at[:, : 3 * d]),
        (wo_ref, qkv_ref, o_ref, lse_ref, w_ref),
        sems,
    )
    for copy in copies:
        copy.start()

    def ready(stage):
        for copy in (copies[1:4], copies[4:], copies[:1])[stage]:
            copy.wait()

    attn_bwd_body(same, lambda p: None, ready, len_ref, dn_ref, qkv_ref, o_ref, lse_ref, xhat_ref, r_ref, w_ref, wo_ref,
                  gain_ref, dres_ref, dqkv_ref, dt_ref, dkvx_ref, sums_ref, do_ref, dq_ref)


def attn_bwd(dn, saved, wqkv, wo, gain, length, same):
    qkv, o, lse, xhat, r = saved
    s, d = dn.shape
    vm = pl.BlockSpec(memory_space=pltpu.VMEM)
    sm = pl.BlockSpec(memory_space=pltpu.SMEM)
    hbm = pl.BlockSpec(memory_space=pl.ANY)
    return pl.pallas_call(
        attn_bwd_kernel,
        out_shape=(jax.ShapeDtypeStruct((s, d), F32), jax.ShapeDtypeStruct((s, 3 * d), BF), jax.ShapeDtypeStruct((s, d), BF),
                   jax.ShapeDtypeStruct((8, 128) if same else (s, d), BF), jax.ShapeDtypeStruct((8, d), F32)),
        in_specs=[sm, vm, hbm, hbm, hbm, vm, vm, hbm, hbm, vm], out_specs=(vm,) * 5,
        scratch_shapes=[pltpu.VMEM((s, d), BF), pltpu.VMEM((128, s), F32), pltpu.VMEM((s, 3 * d), BF),
                        pltpu.VMEM((s, d), BF), pltpu.VMEM((s, d), F32), pltpu.VMEM((d, 3 * d), BF),
                        pltpu.VMEM((d, d), BF), pltpu.SemaphoreType.DMA((5,))],
        compiler_params=pltpu.CompilerParams(vmem_limit_bytes=60 << 20),
    )(length.reshape(1, 1), dn, qkv, o, lse, xhat, r, wqkv, wo if same else wqkv, gain)


def gelu_parts(a):
    e = jnp.exp(-0.5 * a * a)
    t = 1.0 / (1.0 + 0.23164188624 * jnp.abs(a))
    tail = t * (0.127414796 + t * (-0.142248368 + t * (0.7107068705 + t * (-0.7265760135 + t * 0.5307027145)))) * e
    phi_cap = jnp.where(a < 0.0, tail, 1.0 - tail)
    return phi_cap, e * 0.3989422804014327

def ffn_fwd_kernel(n_ref, we_ref, wc_ref, be_ref, bias_ref, gain_ref,
                   y_ref, g_ref, gp_ref, xhat_ref, r_ref, acc_ref, low_ref):
    @pl.when(pl.program_id(0) == 0)
    def _():
        low_ref[...] = n_ref[...].astype(BF)
        acc_ref[...] = n_ref[...] + bias_ref[4:5, :]

    a = dot(low_ref[...], we_ref[...]) + be_ref[...]
    cap, dens = gelu_parts(a)
    g = (a * cap).astype(BF)
    g_ref[...] = g
    gp_ref[...] = (cap + a * dens).astype(BF)
    acc_ref[...] += dot(g, wc_ref[...])

    @pl.when(pl.program_id(0) == pl.num_programs(0) - 1)
    def _():
        xhat, r, y = norm_forward(acc_ref[...], gain_ref[1:2, :], bias_ref[5:6, :])
        xhat_ref[...] = xhat
        r_ref[...] = jnp.broadcast_to(r, r_ref.shape)
        y_ref[...] = y.astype(BF)


def whole(*shape):
    return pl.BlockSpec(shape, lambda c: (0, 0))


def ffn_fwd(n, we, wc, be, bias, gain, chunk=768):
    s, d = n.shape
    ff = we.shape[1]
    columns = pl.BlockSpec((s, chunk), lambda c: (0, c))
    return pl.pallas_call(
        ffn_fwd_kernel,
        out_shape=(jax.ShapeDtypeStruct((s, d), BF), jax.ShapeDtypeStruct((s, ff), BF), jax.ShapeDtypeStruct((s, ff), BF),
                   jax.ShapeDtypeStruct((s, d), F32), jax.ShapeDtypeStruct((s, 128), F32)),
        grid=(ff // chunk,),
        in_specs=[whole(s, d), pl.BlockSpec((d, chunk), lambda c: (0, c)), pl.BlockSpec((chunk, d), lambda c: (c, 0)),
                  pl.BlockSpec((1, chunk), lambda c: (0, c)), whole(*bias.shape), whole(*gain.shape)],
        out_specs=(whole(s, d), columns, columns, whole(s, d), whole(s, 128)),
        scratch_shapes=[pltpu.VMEM((s, d), F32), pltpu.VMEM((s, d), BF)],
        compiler_params=pltpu.CompilerParams(vmem_limit_bytes=60 << 20),
    )(n, we, wc, be.reshape(1, ff), bias, gain)


def ffn_bwd_kernel(extra, len_ref, cot_ref, dm_ref, gp_ref, xhat_ref, r_ref, we_ref, wc_ref, gain_ref,
                   dn_ref, da_ref, dt_ref, sums_ref, sume_ref):
    s, d = cot_ref.shape

    @pl.when(pl.program_id(0) == 0)
    def _():
        row = lax.broadcasted_iota(jnp.int32, (s, 1), 0)
        dy = jnp.where(row < len_ref[0, 0], cot_ref[...].astype(F32), 0.0)
        if extra:
            dy = dy + dm_ref[...].astype(F32)
        xhat = xhat_ref[...]
        du = norm_backward(dy, xhat, r_ref[:, :1], gain_ref[1:2, :])
        dt = du.astype(BF)
        dt_ref[...] = dt
        sums_ref[0:1, :] = jnp.sum(dt.astype(F32), axis=0, keepdims=True)
        sums_ref[1:2, :] = jnp.sum(dy, axis=0, keepdims=True)
        sums_ref[2:3, :] = jnp.sum(dy * xhat, axis=0, keepdims=True)
        sums_ref[3:8, :] = jnp.zeros((5, d), F32)
        dn_ref[...] = du

    dg = dot_nt(dt_ref[...], wc_ref[...])
    da = (dg * gp_ref[...].astype(F32)).astype(BF)
    da_ref[...] = da
    sume_ref[...] = jnp.sum(da.astype(F32), axis=0, keepdims=True)
    dn_ref[...] += dot_nt(da, we_ref[...])


def ffn_bwd(cot, dm, length, saved, we, wc, gain, chunk=768):
    gp, xhat, r = saved
    s, d = cot.shape
    ff = we.shape[1]
    extra = dm is not None
    sm = pl.BlockSpec(memory_space=pltpu.SMEM)
    columns = pl.BlockSpec((s, chunk), lambda c: (0, c))
    row = pl.BlockSpec((1, chunk), lambda c: (0, c))
    if not extra:
        dm = gain
    return pl.pallas_call(
        functools.partial(ffn_bwd_kernel, extra),
        out_shape=(jax.ShapeDtypeStruct((s, d), F32), jax.ShapeDtypeStruct((s, ff), BF), jax.ShapeDtypeStruct((s, d), BF),
                   jax.ShapeDtypeStruct((8, d), F32), jax.ShapeDtypeStruct((1, ff), F32)),
        grid=(ff // chunk,),
        in_specs=[sm, whole(s, d), whole(*dm.shape), columns, whole(s, d), whole(s, 128),
                  pl.BlockSpec((d, chunk), lambda c: (0, c)), pl.BlockSpec((chunk, d), lambda c: (c, 0)),
                  whole(*gain.shape)],
        out_specs=(whole(s, d), columns, whole(s, d), whole(8, d), row),
        compiler_params=pltpu.CompilerParams(vmem_limit_bytes=60 << 20),
    )(length.reshape(1, 1), cot, dm, gp, xhat, r, we, wc, gain)


MESH = pl.DeviceIdType.MESH
LAG = 2
RING = 8


def store_rows(total, out_ref):
    blocks, shards, rows, width = out_ref.shape
    halves = total.shape[1] // width
    groups = blocks // halves
    for k in range(shards):
        for j in range(groups):
            at = (k * groups + j) * rows
            for h in range(halves):
                out_ref[j * halves + h, k] = total[at : at + rows, h * width : (h + 1) * width]


def product(xs, dys):
    total = None
    for x, dy in zip(xs, dys):
        part = dot_tn(x[...].astype(BF), dy[...].astype(BF))
        total = part if total is None else total + part
    return total.astype(BF)


def wgrad_rows_kernel(n, *refs):
    store_rows(product(refs[:n], refs[n : 2 * n]), refs[2 * n])


def wgrad_rows(xs, dys, shards):
    sizes = [x.shape[0] for x in xs]
    n, k = xs[0].shape[1], dys[0].shape[1]
    width, rows = k // 2, k // shards
    groups = n // k
    return pl.pallas_call(
        functools.partial(wgrad_rows_kernel, len(xs)),
        out_shape=jax.ShapeDtypeStruct((2 * groups, shards, rows, width), BF),
        grid=(n // k,),
        in_specs=[pl.BlockSpec((s, k), lambda i: (0, i)) for s in sizes]
        + [pl.BlockSpec((s, k), lambda i: (0, 0)) for s in sizes],
        out_specs=pl.BlockSpec((2 * groups, shards // groups, rows, width), lambda i: (0, i, 0, 0)),
        compiler_params=pltpu.CompilerParams(vmem_limit_bytes=60 << 20),
    )(*xs, *dys)


def wgrad_cross_kernel(n, *refs):
    dqkv, dt, n1, mem, mixed = (refs[j * n : (j + 1) * n] for j in range(5))
    first_ref, second_ref = refs[5 * n :]
    i = pl.program_id(0)
    for at, xs, dys, out_ref in (
        (0, dqkv, n1, first_ref),
        (1, dqkv, mem, first_ref),
        (2, dqkv, mem, second_ref),
        (3, dt, mixed, second_ref),
    ):

        @pl.when(i == at)
        def _():
            store_rows(product(xs, dys), out_ref)


def wgrad_cross(dqkv, dt, n1, mem, mixed, shards):
    sizes = [x.shape[0] for x in dt]
    k = dt[0].shape[1]
    width, rows = k // 2, k // shards
    out = jax.ShapeDtypeStruct((4, shards, rows, width), BF)
    whole = [pl.BlockSpec((s, k), lambda i: (0, 0)) for s in sizes]
    return pl.pallas_call(
        functools.partial(wgrad_cross_kernel, len(sizes)),
        out_shape=(out, out),
        grid=(4,),
        in_specs=[pl.BlockSpec((s, k), lambda i: (0, jnp.minimum(i, 2))) for s in sizes] + whole * 4,
        out_specs=(
            pl.BlockSpec((4, shards // 2, rows, width), lambda i: (0, jnp.minimum(i, 1), 0, 0)),
            pl.BlockSpec((4, shards // 2, rows, width), lambda i: (0, jnp.maximum(i - 2, 0), 0, 0)),
        ),
        compiler_params=pltpu.CompilerParams(vmem_limit_bytes=60 << 20),
    )(*dqkv, *dt, *n1, *mem, *mixed)


def reduce_kernel(counts, *refs):
    (len_ref, dn_ref, qkv_hbm, o_hbm, lse_hbm, xhat_ref, r_ref, w_hbm, wo_ref, gain_ref) = refs[:10]
    (contract, cross_first, cross_second) = refs[15:18]
    ffn_refs = (refs[18:22], refs[22:26])
    (ssum_ref, fsum_ref, esum_ref, csum_ref) = refs[26:30]
    (dres_ref, in_ref, out_ref, expand_ref, contract_ref, cross_ref, vsum_ref, landed) = refs[30:38]
    (dqkv_ref, dt_ref, do_ref, dq_ref, sums_ref, made, own, r0, r1, r2, r3, vbuf, vrecv) = refs[38:51]
    (n0_buf, n1_buf, da0_buf, da1_buf) = refs[51:55]
    held = refs[55:64]
    (qkv_ref, o_ref, lse_ref, wqkv_ref, x0_ref, x_ref, dqkv0_ref, o0_ref, dt0_ref) = held
    send_sem, recv_sem, local_sem, vsend_sem, vrecv_sem, xsend_sem, xrecv_sem, fetch_sem, held_sem = refs[64:]
    copies = incoming((qkv_hbm, o_hbm, lse_hbm, w_hbm, *refs[10:15]), held, held_sem)
    for copy in copies[:3]:
        copy.start()
    d = dn_ref.shape[1]
    n_ffn, n_in, n_out, n_cross = 2 * counts[0], counts[1], counts[2], counts[3]
    blocks = n_ffn + n_in + n_out + n_cross
    rows, width = own.shape[-2:]
    second = lax.axis_index("section") == 1
    me = lax.axis_index("dp")
    c, y, zl, zh = me % 2, (me // 2) % 2, (me // 4) % 2, me // 8
    mates = (me + 1 - 2 * c, me + 2 - 4 * y, me + 4 - 8 * zl, me + 8 - 16 * zh)
    barrier = pltpu.get_barrier_semaphore()
    for mate in mates:
        pl.semaphore_signal(barrier, inc=1, device_id={"dp": mate}, device_id_type=MESH)
    across = 1 - lax.axis_index("section")
    pl.semaphore_signal(barrier, inc=1, device_id={"section": across}, device_id_type=MESH)

    def chosen(visit):
        for which, here in enumerate((jnp.logical_not(second), second)):

            @pl.when(here)
            def _():
                visit(ffn_refs[which])

    def fetch_norms(from_refs):
        return [
            pltpu.make_async_copy(from_refs[k], (n0_buf, n1_buf)[k], fetch_sem.at[2, k]) for k in range(2)
        ]

    def fetch_columns(from_refs, i):
        at = pl.ds(pl.multiple_of(i * d, 128), d)
        return [
            pltpu.make_async_copy(
                from_refs[2 + k].at[:, at], (da0_buf, da1_buf)[k].at[i % 2], fetch_sem.at[i % 2, k]
            )
            for k in range(2)
        ]

    def begin_fetch(from_refs):
        for copy in fetch_norms(from_refs) + fetch_columns(from_refs, 0) + fetch_columns(from_refs, 1):
            copy.start()

    chosen(begin_fetch)
    for copy in copies[3:]:
        copy.start()
    pl.semaphore_wait(barrier, 5)

    def over(j):
        return pltpu.make_async_remote_copy(
            src_ref=cross_first.at[j],
            dst_ref=landed.at[j],
            send_sem=xsend_sem.at[j],
            recv_sem=xrecv_sem.at[j],
            device_id={"section": across},
            device_id_type=MESH,
        )

    @pl.when(second)
    def _():
        for j in (*range(n_cross // 2, n_cross), *range(n_cross // 2)):
            over(j).start()

    order = ((0, 1, 2, 3), (0, 2, 3, 1))

    def remote(src, dst, stage, b, color):
        return pltpu.make_async_remote_copy(
            src_ref=src,
            dst_ref=dst,
            send_sem=send_sem.at[stage, b],
            recv_sem=recv_sem.at[stage, b],
            device_id={"dp": mates[order[color][stage]]},
            device_id_type=MESH,
        )

    turned = blocks // 7
    half = turned // 2
    steps = blocks - turned
    gap = 3
    early = counts[0] - half

    def slot(b, color):
        if color == 0:
            return (b - jnp.where(b >= early, half, 0)) % RING
        return RING + jnp.where(b < steps, b - early, b - steps)

    def first_copy(part, at, b, color):
        return remote(part.at[at, :, :, :, 1 - c], r0.at[slot(b, color)], 0, b, color)

    def local_copy(part, at, b):
        return pltpu.make_async_copy(part.at[at, :, :, :, c], own.at[b], local_sem.at[b])

    def copy_of(stage, b, color):
        if color == 0:
            src = (own.at[b, :, :, 1 - y], own.at[b, :, 1 - zl, y], own.at[b, 1 - zh, zl, y])
        else:
            src = (own.at[b, :, 1 - zl], own.at[b, 1 - zh, zl], own.at[b, zh, zl, 1 - y])
        return remote(src[stage - 1], (r1, r2, r3)[stage - 1].at[b], stage, b, color)

    def add(left, right):
        return (left.astype(F32) + right.astype(F32)).astype(BF)

    def column(at):
        return pl.ds(pl.multiple_of(at * width, 128), width)

    def put_columns(ref, at, value):
        ref[:, column(at)] = value

    def put_groups(ref, at, value):
        ref[pl.ds(pl.multiple_of((at // 2) * rows, 8), rows), column(at % 2)] = value

    plan = (
        (((contract, None),), counts[0], put_groups, contract_ref),
        (((made, None),), counts[0], put_columns, expand_ref),
        (((made, None),), n_in, put_columns, in_ref),
        (((made, None),), n_out, put_columns, out_ref),
        (((landed, jnp.logical_not(second)), (cross_second, second)), n_cross, put_groups, cross_ref),
    )

    def each(b, visit):
        low = 0
        for sources, count, put, target in plan:
            inside = (b >= low) & (b < low + count)
            at = b % counts[0] if sources[0][0] is made else b - low
            visit(inside, sources, at, put, target, b - low)
            low += count

    def settle(stage, b, color):
        if stage == 0:
            first_copy(contract, 0, b, color).wait()
            local_copy(contract, 0, b).wait()
            own[b] = add(own[b], r0[slot(b, color)])
            return
        copy_of(stage, b, color).wait()
        if stage == 1:
            if color == 0:
                own[b, :, :, y] = add(own[b, :, :, y], r1[b])
            else:
                own[b, :, zl] = add(own[b, :, zl], r1[b])
        elif stage == 2:
            if color == 0:
                own[b, :, zl, y] = add(own[b, :, zl, y], r2[b])
            else:
                own[b, zh, zl] = add(own[b, zh, zl], r2[b])
        else:
            total = own[b, zh, zl, y].astype(F32) + r3[b].astype(F32)

            def finish(inside, sources, at, put, target, place):
                @pl.when(inside)
                def _():
                    put(target, place, total)

            each(b, finish)

    def vcopy(j):
        return pltpu.make_async_remote_copy(
            src_ref=vbuf.at[j],
            dst_ref=vrecv.at[j],
            send_sem=vsend_sem.at[j],
            recv_sem=vrecv_sem.at[j],
            device_id={"dp": mates[j]},
            device_id_type=MESH,
        )

    def advance(stage, b, color):
        if stage == 0:

            def launch(inside, sources, at, put, target, place):
                for part, here in sources:

                    @pl.when(inside if here is None else inside & here)
                    def _():
                        if part is landed:
                            over(at).wait_recv()
                        first_copy(part, at, b, color).start()
                        local_copy(part, at, b).start()

            each(b, launch)
            return
        settle(stage - 1, b, color)
        if stage < 4:
            copy_of(stage, b, color).start()

    def step(it, _):
        for stage in range(5):
            at = it - LAG * stage

            @pl.when((at >= 0) & (at < steps))
            def _():
                advance(stage, at + jnp.where(at >= early, half, 0), 0)

            @pl.when((at >= 0) & (at < turned * gap) & (at % gap == 1))
            def _():
                j = at // gap
                advance(stage, jnp.where(j < half, early, steps) + j, 1)

        return 0

    def some(low, high):
        lax.fori_loop(low, high, step, 0)

    def keep(block, total):
        for h in range(2):
            made[block + h] = total[:, h * width : (h + 1) * width].reshape(made.shape[1:]).astype(BF)

    pairs, chunks = d // 128, counts[0] // 2

    def beside(p):
        @pl.when(p < chunks)
        def _():
            @pl.when(p == 0)
            def _():
                for copy in fetch_norms(ffn_refs[0]):
                    copy.wait()

            for copy in fetch_columns(ffn_refs[0], p):
                copy.wait()
            keep(
                2 * p,
                dot_tn(n0_buf[...].astype(BF), da0_buf[p % 2]) + dot_tn(n1_buf[...].astype(BF), da1_buf[p % 2]),
            )

            def next_fetch(from_refs):
                for copy in fetch_columns(from_refs, p + 2):
                    copy.start()

            @pl.when(p + 2 < chunks)
            def _():
                chosen(next_fetch)

        some(jnp.minimum(3 + 2 * p, 7 + p), jnp.minimum(5 + 2 * p, 8 + p))

    def ready(stage):
        for copy in (copies[:3], copies[3:], ())[stage]:
            copy.wait()

    some(0, 3)
    attn_bwd_body(
        True, beside, ready,
        len_ref, dn_ref, qkv_ref, o_ref, lse_ref, xhat_ref, r_ref, wqkv_ref, wo_ref, gain_ref,
        dres_ref, dqkv_ref, dt_ref, None, sums_ref, do_ref, dq_ref,
    )
    after = 7 + pairs
    vbuf[0, 0:4] = sums_ref[0:4, :] + ssum_ref[0:4, :]
    vbuf[0, 4:6] = fsum_ref[0:2, :]
    vbuf[0, 6:7] = sums_ref[4:5, :] + ssum_ref[4:5, :]
    vbuf[0, 7:8] = fsum_ref[2:3, :]
    count = esum_ref.shape[1] // d
    for j in range(count):
        vbuf[0, 8 + j : 9 + j] = esum_ref[:, j * d : (j + 1) * d]
    vbuf[0, 8 + count : 13 + count] = csum_ref[0:5, :]
    vbuf[0, 13 + count :] = jnp.zeros((vbuf.shape[1] - 13 - count, d), F32)
    def weight(i, _):
        at = pl.ds(pl.multiple_of(i * d, 128), d)
        keep(2 * i, dot_tn(x0_ref[...], dqkv0_ref[:, at]) + dot_tn(x_ref[...], dqkv_ref[:, at]))
        step(after + i, 0)
        return 0

    lax.fori_loop(0, n_in // 2, weight, 0)
    keep(n_in, dot_tn(o0_ref[...], dt0_ref[...]) + dot_tn(o_ref[...], dt_ref[...]))
    begin = after + n_in // 2
    vcopy(0).start()

    def rest(it, _):
        step(it, 0)
        for j in range(4):

            @pl.when(it == begin + LAG * (j + 1))
            def _():
                vcopy(j).wait()
                vbuf[j + 1] = vbuf[j] + vrecv[j]
                if j < 3:
                    vcopy(j + 1).start()

        return 0

    lax.fori_loop(begin, steps + 4 * LAG, rest, 0)
    vsum_ref[...] = vbuf[4]

    @pl.when(second)
    def _():
        for j in range(n_cross):
            over(j).wait_send()


def reduce_scatter(length, dn, saved, w_in, w_out, gain, x0, x1, dqkv0, o0, dt0, parts, encoder, decoder, sums):
    s, d = dn.shape
    rows, width = parts[0].shape[-2:]
    n_in, n_out = dqkv0.shape[1] // width, dt0.shape[1] // width
    counts = (parts[0].shape[0], n_in, n_out, parts[1].shape[0])
    blocks = 2 * counts[0] + sum(counts[1:])
    parts = [part.reshape(part.shape[0], 2, 2, 2, 2, rows, width) for part in parts]
    short = x0.shape[0]
    vec = (24, d)
    vm = pl.BlockSpec(memory_space=pltpu.VMEM)
    sm = pl.BlockSpec(memory_space=pltpu.SMEM)
    hbm = pl.BlockSpec(memory_space=pl.ANY)
    shapes = ((s, d), (rows, n_in * width), (rows, n_out * width), (rows, counts[0] * width),
              (counts[0] // 2 * rows, d), (counts[3] // 2 * rows, d), vec)
    return pl.pallas_call(
        functools.partial(reduce_kernel, counts),
        out_shape=(*(jax.ShapeDtypeStruct(shape, F32) for shape in shapes), jax.ShapeDtypeStruct(parts[1].shape, BF)),
        in_specs=[sm, vm, hbm, hbm, hbm, vm, vm, hbm, vm, vm] + [hbm] * 16 + [vm] * 4,
        out_specs=(*(vm,) * 7, hbm),
        scratch_shapes=[
            pltpu.VMEM((s, 3 * d), BF),
            pltpu.VMEM((s, d), BF),
            pltpu.VMEM((s, d), BF),
            pltpu.VMEM((128, s), F32),
            pltpu.VMEM((8, d), F32),
            pltpu.VMEM((counts[0], 2, 2, 2, 2, rows, width), BF),
            pltpu.VMEM((blocks, 2, 2, 2, rows, width), BF),
            pltpu.VMEM((RING + blocks // 7, 2, 2, 2, rows, width), BF),
            pltpu.VMEM((blocks, 2, 2, rows, width), BF),
            pltpu.VMEM((blocks, 2, rows, width), BF),
            pltpu.VMEM((blocks, rows, width), BF),
            pltpu.VMEM((5, *vec), F32),
            pltpu.VMEM((4, *vec), F32),
            pltpu.VMEM((short, d), F32),
            pltpu.VMEM((s, d), F32),
            pltpu.VMEM((2, short, d), BF),
            pltpu.VMEM((2, s, d), BF),
            pltpu.VMEM((s, 3 * d), BF),
            pltpu.VMEM((s, d), BF),
            pltpu.VMEM((s, d), F32),
            pltpu.VMEM((d, 3 * d), BF),
            pltpu.VMEM((short, d), BF),
            pltpu.VMEM((s, d), BF),
            pltpu.VMEM((short, 3 * d), BF),
            pltpu.VMEM((short, d), BF),
            pltpu.VMEM((short, d), BF),
            pltpu.SemaphoreType.DMA((4, blocks)),
            pltpu.SemaphoreType.DMA((4, blocks)),
            pltpu.SemaphoreType.DMA((blocks,)),
            pltpu.SemaphoreType.DMA((4,)),
            pltpu.SemaphoreType.DMA((4,)),
            pltpu.SemaphoreType.DMA((counts[3],)),
            pltpu.SemaphoreType.DMA((counts[3],)),
            pltpu.SemaphoreType.DMA((3, 2)),
            pltpu.SemaphoreType.DMA((9,)),
        ],
        compiler_params=pltpu.CompilerParams(collective_id=0, has_side_effects=True, vmem_limit_bytes=67043328),
    )(length.reshape(1, 1), dn, *saved, w_in, w_out, gain, x0, x1, dqkv0, o0, dt0, *parts, *encoder, *decoder, *sums)[:7]


def shards(
    inputs_long,
    inputs_short,
    cotangent_long,
    cotangent_short,
    lengths_long,
    lengths_short,
    self_in_weight,
    self_out_weight,
    expand_weight,
    contract_weight,
    expand_bias,
    layer_biases,
    layer_gains,
    cross_weight,
    cross_biases,
    cross_gain,
):
    decoder = lax.axis_index("section") == 1
    d = inputs_long.shape[-1]
    ff = expand_weight.shape[2]
    w_in, w_out, w_e, w_c = self_in_weight[0], self_out_weight[0], expand_weight[0], contract_weight[0]
    b_e, bias, gain = expand_bias[0], layer_biases[0], layer_gains[0]
    c_gain = cross_gain.reshape(1, d)

    xs = (inputs_short[0, 0], inputs_long[0, 0])
    cots = (cotangent_short[0, 0], cotangent_long[0, 0])
    source = (lengths_short[0, 0], lengths_long[0, 0])
    target = (lengths_short[1, 0], lengths_long[1, 0])
    sizes = tuple(x.shape[0] for x in xs)

    own = tuple(jnp.where(decoder, t, o) for t, o in zip(target, source))

    def attend(i):
        x = xs[i]
        return attn_fwd(x, None, w_in, w_out, bias, gain, own[i])

    def encode_ffn(i, n):
        s = sizes[i]

        def decode():
            return blank(((s, d), BF), ((s, ff), BF), ((s, ff), BF), ((s, d), F32), ((s, 128), F32))

        return lax.cond(decoder, decode, lambda: ffn_fwd(n, w_e, w_c, b_e, bias, gain))

    def send(value, steps):
        return lax.ppermute(value, "section", [(0, 1)] if steps > 0 else [(1, 0)])

    def cross(i, memory, n1):
        s = sizes[i]

        def encode():
            return blank(
                ((s, 3 * d), BF), ((s, d), BF), ((s, d), F32), ((s, d), F32), ((s, 128), F32), ((s, d), F32)
            )

        def decode():
            return attn_fwd(n1, memory, cross_weight, None, cross_biases, c_gain, source[i])

        return lax.cond(decoder, decode, encode)

    def turn(i, out):
        s = sizes[i]

        def decode():
            y, g, gp, xhat, r = ffn_fwd(out[5], w_e, w_c, b_e, bias, gain)
            fb = ffn_bwd(cots[i], None, target[i], (gp, xhat, r), w_e, w_c, gain)
            ab = attn_bwd(fb[0], out[:5], cross_weight, None, c_gain, source[i], False)
            return (g, fb[1], fb[2], ab[1], ab[2]), ab[0], ab[3], y, (fb[3], fb[4], ab[4])

        def encode():
            out = blank(
                ((s, ff), BF),
                ((s, ff), BF),
                ((s, d), BF),
                ((s, 3 * d), BF),
                ((s, d), BF),
                ((s, d), F32),
                ((s, d), BF),
                ((s, d), BF),
                ((8, d), F32),
                ((1, ff), F32),
                ((8, d), F32),
            )
            return tuple(out[:5]), out[5], out[6], out[7], tuple(out[8:])

        return lax.cond(decoder, decode, encode)

    att0 = attend(0)
    ffn0 = encode_ffn(0, att0[5])
    mem0 = send(ffn0[0], 1)
    x_long, _ = lax.optimization_barrier((xs[1], ffn0[0]))
    xs = (xs[0], x_long)
    att1 = attend(1)
    n_long, mem0 = lax.optimization_barrier((att1[5], mem0))
    ffn1 = encode_ffn(1, n_long)
    mem1 = send(ffn1[0], 1)
    n_short, _ = lax.optimization_barrier((att0[5], ffn1[0]))
    out0 = cross(0, mem0, n_short)
    keep0, dn0, dm0, y0, sums0 = turn(0, out0)
    back0 = send(dm0, -1)
    n_long, _ = lax.optimization_barrier((att1[5], dm0))
    out1 = cross(1, mem1, n_long)
    n_long, back0 = lax.optimization_barrier((out1[5], back0))
    out1 = (*out1[:5], n_long)
    keep1, dn1, dm1, y1, sums1 = turn(1, out1)
    back1 = send(dm1, -1)
    dp = lax.axis_size("dp")
    staged = dp == 16 and d % (16 * dp) == 0 and d == 6 * 128 and ff == 4 * d

    def cross_grads():
        n1, mem = (att0[5], att1[5]), (mem0, mem1)
        dqkv, dt = ((keep0[j], keep1[j]) for j in (3, 4))
        mixed = (out0[1], out1[1])
        if staged:
            return wgrad_cross(dqkv, dt, n1, mem, mixed, dp)
        joint = jnp.concatenate(dqkv, 0)
        low = jnp.concatenate(n1, 0).astype(BF)
        mem = jnp.concatenate(mem, 0)
        rows = (
            dot_tn(joint[:, :d], low),
            dot_tn(joint[:, d : 2 * d], mem),
            dot_tn(joint[:, 2 * d :], mem),
            dot_tn(jnp.concatenate(dt, 0), jnp.concatenate(mixed, 0)),
        )
        return tuple(jnp.concatenate(rows[j : j + 2], 0).astype(BF) for j in (0, 2))

    def cross_blank():
        shape = (4, dp, d // dp, d // 2) if staged else (2 * d, d)
        return tuple(blank((shape, BF), (shape, BF)))

    cross_sums = sums0[2] + sums1[2]
    cross_first, cross_second = lax.cond(decoder, cross_grads, cross_blank)
    back0, _ = lax.optimization_barrier((back0, cross_first))
    dn0, *enc0 = lax.cond(
        decoder,
        lambda: (dn0, *blank(((sizes[0], ff), BF), ((sizes[0], d), BF), ((8, d), F32), ((1, ff), F32))),
        lambda: tuple(ffn_bwd(cots[0], back0, source[0], ffn0[2:], w_e, w_c, gain)),
    )
    self0 = attn_bwd(dn0, att0[:5], w_in, w_out, gain, own[0], True)
    back1, cross_sent, _ = lax.optimization_barrier((back1, send(cross_sums, -1), self0[0]))
    cross_rows = jnp.where(decoder, cross_sums, cross_sent)

    def plain(left, right):
        left, right = (jnp.concatenate([e.astype(BF) for e in side], 0) for side in (left, right))
        return dot_tn(left, right).astype(BF)

    def contract_grad(g, dt):
        return wgrad_rows(g, dt, dp) if staged else plain(g, dt)

    def decode_last():
        grad = contract_grad((keep0[0], keep1[0]), (keep0[2], keep1[2]))
        return dn1, *blank(((sizes[1], ff), BF)), grad, sums0[0] + sums1[0], sums0[1] + sums1[1]

    def encode_last():
        dn, da, dt, sums, sum_e = ffn_bwd(cots[1], back1, source[1], ffn1[2:], w_e, w_c, gain)
        return dn, da, contract_grad((ffn0[1], ffn1[1]), (enc0[1], dt)), enc0[2] + sums, enc0[3] + sum_e

    dn1, enc_da, g_contract, ffn_sums, sum_e = lax.cond(decoder, decode_last, encode_last)
    if staged:
        dx1, *big, rows = reduce_scatter(
            own[1], dn1, att1[:5], w_in, w_out, gain, xs[0], xs[1], self0[1], att0[1], self0[2],
            (g_contract, cross_first, cross_second),
            (att0[5], att1[5], enc0[0], enc_da),
            (out0[5], out1[5], keep0[1], keep1[1]),
            (self0[4], ffn_sums, sum_e, cross_rows),
        )
    else:
        self1 = attn_bwd(dn1, att1[:5], w_in, w_out, gain, own[1], True)
        dx1 = self1[0]
        self_sums = self0[4] + self1[4]
        rows = [self_sums[0:4], ffn_sums[0:2], self_sums[4:5], ffn_sums[2:3], sum_e.reshape(ff // d, d), cross_rows[0:5]]
        rows = lax.psum(jnp.concatenate(rows, 0), "dp")
        cross_mine = jnp.where(decoder, cross_second, send(cross_first, -1))
        pairs = (((att0[5], enc0[0]), (att1[5], enc_da)), ((out0[5], keep0[1]), (out1[5], keep1[1])))
        g_expand = lax.cond(decoder, lambda: plain(*zip(*pairs[1])), lambda: plain(*zip(*pairs[0])))
        in_grad = plain(xs, (self0[1], self1[1]))
        out_grad = plain((att0[1], att1[1]), (self0[2], self1[2]))
        big = [
            lax.psum_scatter(part, "dp", scatter_dimension=0, tiled=True).astype(F32)
            for part in (in_grad, out_grad, g_expand, g_contract, cross_mine)
        ]
    count = 8 + ff // d
    me = lax.axis_index("dp")
    piece = lax.dynamic_slice_in_dim(rows[:8], me * (d // dp), d // dp, 1)
    e_piece = lax.dynamic_slice_in_dim(rows[8:count].reshape(1, ff), me * (ff // dp), ff // dp, 1)
    outs = [jnp.where(decoder, y, e)[None, None] for y, e in ((y0, ffn0[0]), (y1, ffn1[0]))]
    return (
        outs[1],
        outs[0],
        dx1[None, None],
        self0[0][None, None],
        big[0][None],
        big[1][None],
        big[2][None],
        big[3][None],
        e_piece,
        piece[None, :6],
        piece[None, 6:8],
        big[4].T,
        rows[count : count + 4],
        rows[count + 4],
    )


def solution(mesh):
    in_specs = (
        P("section", "dp", None, None),
        P("section", "dp", None, None),
        P("section", "dp", None, None),
        P("section", "dp", None, None),
        P(None, "dp"),
        P(None, "dp"),
        P("section", None, None),
        P("section", None, None),
        P("section", None, None),
        P("section", None, None),
        P("section", None),
        P("section", None, None),
        P("section", None, None),
        P(),
        P(),
        P(),
    )
    out_specs = (
        P("section", "dp", None, None),
        P("section", "dp", None, None),
        P("section", "dp", None, None),
        P("section", "dp", None, None),
        P("section", "dp", None),
        P("section", "dp", None),
        P("section", "dp", None),
        P("section", "dp", None),
        P("section", "dp"),
        P("section", None, "dp"),
        P("section", None, "dp"),
        P(None, ("section", "dp")),
        P(),
        P(),
    )
    return jax.shard_map(shards, mesh=mesh, in_specs=in_specs, out_specs=out_specs, check_vma=False)
```

```python
import functools
import jax
import jax.numpy as jnp
from jax import lax
from jax.experimental import pallas as pl
from jax.experimental.pallas import tpu as pltpu
from jax.sharding import PartitionSpec as P

BF, F32 = jnp.bfloat16, jnp.float32
NEG = -1e30
NT = (((1,), (1,)), ((), ()))
TN = (((0,), (0,)), ((), ()))

def dot(a, b):
    return jnp.dot(a, b, preferred_element_type=F32)
def dot_nt(a, b):
    return lax.dot_general(a, b, NT, preferred_element_type=F32)
def dot_tn(a, b):
    return lax.dot_general(a, b, TN, preferred_element_type=F32)

def lanes(rows):
    return lax.broadcasted_iota(jnp.int32, (rows, 128), 1)

def split3(v):
    hi = v.astype(BF)
    rest = v - hi.astype(F32)
    mid = rest.astype(BF)
    low = (rest - mid.astype(F32)).astype(BF)
    return hi, mid, low

def blank(*shapes):
    def nothing(*refs):
        pass

    return pl.pallas_call(
        nothing,
        out_shape=[jax.ShapeDtypeStruct(shape, kind) for shape, kind in shapes],
        out_specs=[pl.BlockSpec(memory_space=pl.ANY)] * len(shapes),
    )()


def norm_forward(u, gain, shift):
    mean = jnp.mean(u, axis=-1, keepdims=True)
    c = u - mean
    r = lax.rsqrt(jnp.mean(c * c, axis=-1, keepdims=True) + 1e-5)
    xhat = c * r
    return xhat, r, xhat * gain + shift

def causal_shift(size):
    return jnp.where(lax.axis_index("section") == 1, 0, size)


def attn_fwd_kernel(same, len_ref, xq_ref, xkv_ref, res_ref, wqkv_ref, wo_ref, bias_ref, gain_ref,
                    qkv_ref, o_ref, lse_ref, xhat_ref, r_ref, n_ref):
    s, d = xq_ref.shape
    if not same:
        wo_ref = wqkv_ref.at[:, 3 * d :]
    xq = xq_ref[...].astype(BF)
    xkv = xq if same else xkv_ref[...]
    qkv_ref[:, :d] = (dot(xq, wqkv_ref[:, :d]) + bias_ref[0:1, :]).astype(BF)
    qkv_ref[:, d:2*d] = dot(xkv, wqkv_ref[:, d:2*d]).astype(BF)
    qkv_ref[:, 2*d:] = (dot(xkv, wqkv_ref[:, 2*d:3*d]) + bias_ref[1:2, :]).astype(BF)
    length = len_ref[0, 0]
    lane = lanes(s)
    row = lax.broadcasted_iota(jnp.int32, (s, 128), 0)
    key_bias = jnp.where(row < length, 0.0, NEG).astype(BF)
    if same:
        tri = lax.broadcasted_iota(jnp.int32, (s, s), 1) <= lax.broadcasted_iota(jnp.int32, (s, s), 0) + causal_shift(s)
    one = jnp.ones((s, 128), BF)
    zero = jnp.zeros((s, 128), BF)

    def pair(p, _):
        at = pl.multiple_of(p * 128, 128)
        q = qkv_ref[:, pl.ds(at, 128)] * jnp.asarray(0.125, BF)
        k = qkv_ref[:, pl.ds(d + at, 128)]
        v = qkv_ref[:, pl.ds(2 * d + at, 128)]
        outs, lses = [], []
        for h in range(2):
            mine = (lane < 64) if h == 0 else (lane >= 64)
            other = 64 if h == 0 else 0
            qh = jnp.where(mine, q, jnp.where(lane == other, one, zero))
            kh = jnp.where(mine, k, jnp.where(lane == other, key_bias, zero))
            sc = dot_nt(qh, kh)
            if same:
                sc = jnp.where(tri, sc, NEG)
            m = jnp.max(sc, axis=-1, keepdims=True)
            e = jnp.exp(sc - m)
            l = jnp.sum(e, axis=-1, keepdims=True)
            outs.append(dot(e.astype(BF), v) * (1.0 / l))
            lses.append(m + jnp.log(l))
        o_ref[:, pl.ds(at, 128)] = jnp.where(lane < 64, outs[0], outs[1]).astype(BF)
        lse_ref[:, pl.ds(at, 128)] = jnp.where(lane < 64, lses[1], lses[0])
        return 0
    lax.fori_loop(0, d // 128, pair, 0)
    u = res_ref[...].astype(F32) + dot(o_ref[...], wo_ref[...]) + bias_ref[2:3, :]
    xhat, r, n = norm_forward(u, gain_ref[0:1, :], bias_ref[3:4, :])
    xhat_ref[...] = xhat
    r_ref[...] = jnp.broadcast_to(r, r_ref.shape)
    n_ref[...] = n

def attn_fwd(xq, xkv, res, wqkv, wo, bias, gain, length):
    s, d = xq.shape
    same = xkv is None
    if same:
        xkv = xq
    else:
        wo = gain
    vm = pl.BlockSpec(memory_space=pltpu.VMEM)
    sm = pl.BlockSpec(memory_space=pltpu.SMEM)
    return pl.pallas_call(
        functools.partial(attn_fwd_kernel, same),
        out_shape=(jax.ShapeDtypeStruct((s, 3 * d), BF), jax.ShapeDtypeStruct((s, d), BF), jax.ShapeDtypeStruct((s, d), F32),
                   jax.ShapeDtypeStruct((s, d), F32), jax.ShapeDtypeStruct((s, 128), F32), jax.ShapeDtypeStruct((s, d), F32)),
        in_specs=[sm] + [vm] * 7, out_specs=(vm,) * 6,
        compiler_params=pltpu.CompilerParams(vmem_limit_bytes=60 << 20),
    )(length.reshape(1, 1), xq, xkv, res, wqkv, wo, bias, gain)

def norm_backward(dn, xhat, r, gain):
    h = dn * gain
    return r * (h - jnp.mean(h, axis=-1, keepdims=True) - xhat * jnp.mean(h * xhat, axis=-1, keepdims=True))

def attn_bwd_body(same, between, ready, len_ref, dn_ref, qkv_ref, o_ref, lse_ref, xhat_ref, r_ref, wqkv_ref, wo_ref, gain_ref,
                  dres_ref, dqkv_ref, dt_ref, dkvx_ref, sums_ref, do_ref, dq_ref):
    s, d = dn_ref.shape
    dn = dn_ref[...]
    xhat = xhat_ref[...]
    du = norm_backward(dn, xhat, r_ref[:, :1], gain_ref[0:1, :])
    dt = du.astype(BF)
    dt_ref[...] = dt
    sums_ref[2:3, :] = jnp.sum(dt.astype(F32), axis=0, keepdims=True)
    sums_ref[3:4, :] = jnp.sum(dn, axis=0, keepdims=True)
    sums_ref[4:5, :] = jnp.sum(dn * xhat, axis=0, keepdims=True)
    dres_ref[...] = du
    ready(2)
    do_ref[...] = dot_nt(dt, wo_ref[...]).astype(BF)
    length = len_ref[0, 0]
    lane = lanes(s)
    row = lax.broadcasted_iota(jnp.int32, (s, 128), 0)
    key_bias = jnp.where(row < length, 0.0, NEG).astype(BF)
    if same:
        tri = lax.broadcasted_iota(jnp.int32, (s, s), 0) <= lax.broadcasted_iota(jnp.int32, (s, s), 1) + causal_shift(s)
    one = jnp.ones((s, 128), BF)
    zero = jnp.zeros((s, 128), BF)

    def place(base, mine, other, extra):
        out = zero
        for j, val in enumerate(extra):
            out = jnp.where(lane == other + j, val, out)
        return jnp.where(mine, base, out)

    def pair(p, _):
        between(p)
        at = pl.multiple_of(p * 128, 128)
        q = qkv_ref[:, pl.ds(at, 128)] * jnp.asarray(0.125, BF)
        k = qkv_ref[:, pl.ds(d + at, 128)]
        v = qkv_ref[:, pl.ds(2 * d + at, 128)]
        do = do_ref[:, pl.ds(at, 128)]
        lse3 = split3(-lse_ref[:, pl.ds(at, 128)])
        prod = do.astype(F32) * o_ref[:, pl.ds(at, 128)].astype(F32)
        dq, dk, dv = [], [], []
        for h in range(2):
            mine = (lane < 64) if h == 0 else (lane >= 64)
            other = 64 if h == 0 else 0
            inner = jnp.broadcast_to(jnp.sum(jnp.where(mine, prod, 0.0), axis=-1, keepdims=True), (s, 128))
            qh = place(q, mine, other, (*lse3, one))
            kh = place(k, mine, other, (one, one, one, key_bias))
            doh = place(do, mine, other, split3(-inner))
            vh = place(v, mine, other, (one, one, one))
            st = dot_nt(kh, qh)
            if same:
                st = jnp.where(tri, st, NEG)
            pt = jnp.exp(st)
            dst = (pt * dot_nt(vh, doh)).astype(BF)
            dv.append(dot(pt.astype(BF), do))
            dk.append(dot(dst, q))
            dq.append(dot_tn(k, dst))
        m1 = lane < 64
        dq_ref[...] = jnp.where(lax.broadcasted_iota(jnp.int32, (128, s), 0) < 64, dq[0], dq[1])
        dqkv_ref[:, pl.ds(at, 128)] = (dq_ref[...].T * 0.125).astype(BF)
        dqkv_ref[:, pl.ds(d + at, 128)] = jnp.where(m1, dk[0], dk[1]).astype(BF)
        dqkv_ref[:, pl.ds(2 * d + at, 128)] = jnp.where(m1, dv[0], dv[1]).astype(BF)
        return 0
    ready(0)
    lax.fori_loop(0, d // 128, pair, 0)
    ready(1)
    if same:
        dres_ref[...] += dot_nt(dqkv_ref[...], wqkv_ref[...])
    else:
        dres_ref[...] += dot_nt(dqkv_ref[:, :d], wqkv_ref[:, :d])
        dkvx_ref[...] = dot_nt(dqkv_ref[:, d:], wqkv_ref[:, d:3*d]).astype(BF)
    sums_ref[0:1, :] = jnp.sum(dqkv_ref[:, :d].astype(F32), axis=0, keepdims=True)
    sums_ref[1:2, :] = jnp.sum(dqkv_ref[:, 2*d:].astype(F32), axis=0, keepdims=True)
    sums_ref[5:8, :] = jnp.zeros((3, d), F32)

def incoming(sources, targets, sems):
    return [pltpu.make_async_copy(src, dst, sems.at[k]) for k, (src, dst) in enumerate(zip(sources, targets))]


def attn_bwd_kernel(len_ref, dn_ref, qkv_hbm, o_hbm, lse_hbm, xhat_ref, r_ref, w_hbm, wo_hbm, gain_ref,
                    dres_ref, dqkv_ref, dt_ref, dkvx_ref, sums_ref, do_ref, dq_ref, qkv_ref, o_ref, lse_ref, w_ref, wo_ref, sems):
    d = dn_ref.shape[1]
    same = wo_hbm.shape[1] == d
    copies = incoming(
        (wo_hbm.at[:, wo_hbm.shape[1] - d :], qkv_hbm, o_hbm, lse_hbm, w_hbm.at[:, : 3 * d]),
        (wo_ref, qkv_ref, o_ref, lse_ref, w_ref),
        sems,
    )
    for copy in copies:
        copy.start()

    def ready(stage):
        for copy in (copies[1:4], copies[4:], copies[:1])[stage]:
            copy.wait()

    attn_bwd_body(same, lambda p: None, ready, len_ref, dn_ref, qkv_ref, o_ref, lse_ref, xhat_ref, r_ref, w_ref, wo_ref,
                  gain_ref, dres_ref, dqkv_ref, dt_ref, dkvx_ref, sums_ref, do_ref, dq_ref)


def attn_bwd(dn, saved, wqkv, wo, gain, length, same):
    qkv, o, lse, xhat, r = saved
    s, d = dn.shape
    vm = pl.BlockSpec(memory_space=pltpu.VMEM)
    sm = pl.BlockSpec(memory_space=pltpu.SMEM)
    hbm = pl.BlockSpec(memory_space=pl.ANY)
    return pl.pallas_call(
        attn_bwd_kernel,
        out_shape=(jax.ShapeDtypeStruct((s, d), F32), jax.ShapeDtypeStruct((s, 3 * d), BF), jax.ShapeDtypeStruct((s, d), BF),
                   jax.ShapeDtypeStruct((8, 128) if same else (s, d), BF), jax.ShapeDtypeStruct((8, d), F32)),
        in_specs=[sm, vm, hbm, hbm, hbm, vm, vm, hbm, hbm, vm], out_specs=(vm,) * 5,
        scratch_shapes=[pltpu.VMEM((s, d), BF), pltpu.VMEM((128, s), F32), pltpu.VMEM((s, 3 * d), BF),
                        pltpu.VMEM((s, d), BF), pltpu.VMEM((s, d), F32), pltpu.VMEM((d, 3 * d), BF),
                        pltpu.VMEM((d, d), BF), pltpu.SemaphoreType.DMA((5,))],
        compiler_params=pltpu.CompilerParams(vmem_limit_bytes=60 << 20),
    )(length.reshape(1, 1), dn, qkv, o, lse, xhat, r, wqkv, wo if same else wqkv, gain)


def gelu_parts(a):
    e = jnp.exp(-0.5 * a * a)
    t = 1.0 / (1.0 + 0.23164188624 * jnp.abs(a))
    tail = t * (0.127414796 + t * (-0.142248368 + t * (0.7107068705 + t * (-0.7265760135 + t * 0.5307027145)))) * e
    phi_cap = jnp.where(a < 0.0, tail, 1.0 - tail)
    return phi_cap, e * 0.3989422804014327

def ffn_fwd_kernel(n_ref, we_ref, wc_ref, be_ref, bias_ref, gain_ref,
                   y_ref, g_ref, gp_ref, xhat_ref, r_ref, acc_ref, low_ref):
    @pl.when(pl.program_id(0) == 0)
    def _():
        low_ref[...] = n_ref[...].astype(BF)
        acc_ref[...] = n_ref[...] + bias_ref[4:5, :]

    a = dot(low_ref[...], we_ref[...]) + be_ref[...]
    cap, dens = gelu_parts(a)
    g = (a * cap).astype(BF)
    g_ref[...] = g
    gp_ref[...] = (cap + a * dens).astype(BF)
    acc_ref[...] += dot(g, wc_ref[...])

    @pl.when(pl.program_id(0) == pl.num_programs(0) - 1)
    def _():
        xhat, r, y = norm_forward(acc_ref[...], gain_ref[1:2, :], bias_ref[5:6, :])
        xhat_ref[...] = xhat
        r_ref[...] = jnp.broadcast_to(r, r_ref.shape)
        y_ref[...] = y.astype(BF)


def whole(*shape):
    return pl.BlockSpec(shape, lambda c: (0, 0))


def ffn_fwd(n, we, wc, be, bias, gain, chunk=768):
    s, d = n.shape
    ff = we.shape[1]
    columns = pl.BlockSpec((s, chunk), lambda c: (0, c))
    return pl.pallas_call(
        ffn_fwd_kernel,
        out_shape=(jax.ShapeDtypeStruct((s, d), BF), jax.ShapeDtypeStruct((s, ff), BF), jax.ShapeDtypeStruct((s, ff), BF),
                   jax.ShapeDtypeStruct((s, d), F32), jax.ShapeDtypeStruct((s, 128), F32)),
        grid=(ff // chunk,),
        in_specs=[whole(s, d), pl.BlockSpec((d, chunk), lambda c: (0, c)), pl.BlockSpec((chunk, d), lambda c: (c, 0)),
                  pl.BlockSpec((1, chunk), lambda c: (0, c)), whole(*bias.shape), whole(*gain.shape)],
        out_specs=(whole(s, d), columns, columns, whole(s, d), whole(s, 128)),
        scratch_shapes=[pltpu.VMEM((s, d), F32), pltpu.VMEM((s, d), BF)],
        compiler_params=pltpu.CompilerParams(vmem_limit_bytes=60 << 20),
    )(n, we, wc, be.reshape(1, ff), bias, gain)


def ffn_bwd_kernel(extra, len_ref, cot_ref, dm_ref, gp_ref, xhat_ref, r_ref, we_ref, wc_ref, gain_ref,
                   dn_ref, da_ref, dt_ref, sums_ref, sume_ref):
    s, d = cot_ref.shape

    @pl.when(pl.program_id(0) == 0)
    def _():
        row = lax.broadcasted_iota(jnp.int32, (s, 1), 0)
        dy = jnp.where(row < len_ref[0, 0], cot_ref[...].astype(F32), 0.0)
        if extra:
            dy = dy + dm_ref[...].astype(F32)
        xhat = xhat_ref[...]
        du = norm_backward(dy, xhat, r_ref[:, :1], gain_ref[1:2, :])
        dt = du.astype(BF)
        dt_ref[...] = dt
        sums_ref[0:1, :] = jnp.sum(dt.astype(F32), axis=0, keepdims=True)
        sums_ref[1:2, :] = jnp.sum(dy, axis=0, keepdims=True)
        sums_ref[2:3, :] = jnp.sum(dy * xhat, axis=0, keepdims=True)
        sums_ref[3:8, :] = jnp.zeros((5, d), F32)
        dn_ref[...] = du

    dg = dot_nt(dt_ref[...], wc_ref[...])
    da = (dg * gp_ref[...].astype(F32)).astype(BF)
    da_ref[...] = da
    sume_ref[...] = jnp.sum(da.astype(F32), axis=0, keepdims=True)
    dn_ref[...] += dot_nt(da, we_ref[...])


def ffn_bwd(cot, dm, length, saved, we, wc, gain, chunk=768):
    gp, xhat, r = saved
    s, d = cot.shape
    ff = we.shape[1]
    extra = dm is not None
    sm = pl.BlockSpec(memory_space=pltpu.SMEM)
    columns = pl.BlockSpec((s, chunk), lambda c: (0, c))
    row = pl.BlockSpec((1, chunk), lambda c: (0, c))
    if not extra:
        dm = gain
    return pl.pallas_call(
        functools.partial(ffn_bwd_kernel, extra),
        out_shape=(jax.ShapeDtypeStruct((s, d), F32), jax.ShapeDtypeStruct((s, ff), BF), jax.ShapeDtypeStruct((s, d), BF),
                   jax.ShapeDtypeStruct((8, d), F32), jax.ShapeDtypeStruct((1, ff), F32)),
        grid=(ff // chunk,),
        in_specs=[sm, whole(s, d), whole(*dm.shape), columns, whole(s, d), whole(s, 128),
                  pl.BlockSpec((d, chunk), lambda c: (0, c)), pl.BlockSpec((chunk, d), lambda c: (c, 0)),
                  whole(*gain.shape)],
        out_specs=(whole(s, d), columns, whole(s, d), whole(8, d), row),
        compiler_params=pltpu.CompilerParams(vmem_limit_bytes=60 << 20),
    )(length.reshape(1, 1), cot, dm, gp, xhat, r, we, wc, gain)


MESH = pl.DeviceIdType.MESH
LAG = 2
RING = 8


def store_rows(total, out_ref):
    blocks, shards, rows, width = out_ref.shape
    halves = total.shape[1] // width
    groups = blocks // halves
    for k in range(shards):
        for j in range(groups):
            at = (k * groups + j) * rows
            for h in range(halves):
                out_ref[j * halves + h, k] = total[at : at + rows, h * width : (h + 1) * width]


def product(xs, dys):
    total = None
    for x, dy in zip(xs, dys):
        part = dot_tn(x[...].astype(BF), dy[...].astype(BF))
        total = part if total is None else total + part
    return total.astype(BF)


def wgrad_rows_kernel(n, *refs):
    store_rows(product(refs[:n], refs[n : 2 * n]), refs[2 * n])


def wgrad_rows(xs, dys, shards):
    sizes = [x.shape[0] for x in xs]
    n, k = xs[0].shape[1], dys[0].shape[1]
    width, rows = k // 2, k // shards
    groups = n // k
    return pl.pallas_call(
        functools.partial(wgrad_rows_kernel, len(xs)),
        out_shape=jax.ShapeDtypeStruct((2 * groups, shards, rows, width), BF),
        grid=(n // k,),
        in_specs=[pl.BlockSpec((s, k), lambda i: (0, i)) for s in sizes]
        + [pl.BlockSpec((s, k), lambda i: (0, 0)) for s in sizes],
        out_specs=pl.BlockSpec((2 * groups, shards // groups, rows, width), lambda i: (0, i, 0, 0)),
        compiler_params=pltpu.CompilerParams(vmem_limit_bytes=60 << 20),
    )(*xs, *dys)


def wgrad_cross_kernel(n, *refs):
    dqkv, dt, n1, mem, mixed = (refs[j * n : (j + 1) * n] for j in range(5))
    first_ref, second_ref = refs[5 * n :]
    i = pl.program_id(0)
    for at, xs, dys, out_ref in (
        (0, dqkv, n1, first_ref),
        (1, dqkv, mem, first_ref),
        (2, dqkv, mem, second_ref),
        (3, dt, mixed, second_ref),
    ):

        @pl.when(i == at)
        def _():
            store_rows(product(xs, dys), out_ref)


def wgrad_cross(dqkv, dt, n1, mem, mixed, shards):
    sizes = [x.shape[0] for x in dt]
    k = dt[0].shape[1]
    width, rows = k // 2, k // shards
    out = jax.ShapeDtypeStruct((4, shards, rows, width), BF)
    whole = [pl.BlockSpec((s, k), lambda i: (0, 0)) for s in sizes]
    return pl.pallas_call(
        functools.partial(wgrad_cross_kernel, len(sizes)),
        out_shape=(out, out),
        grid=(4,),
        in_specs=[pl.BlockSpec((s, k), lambda i: (0, jnp.minimum(i, 2))) for s in sizes] + whole * 4,
        out_specs=(
            pl.BlockSpec((4, shards // 2, rows, width), lambda i: (0, jnp.minimum(i, 1), 0, 0)),
            pl.BlockSpec((4, shards // 2, rows, width), lambda i: (0, jnp.maximum(i - 2, 0), 0, 0)),
        ),
        compiler_params=pltpu.CompilerParams(vmem_limit_bytes=60 << 20),
    )(*dqkv, *dt, *n1, *mem, *mixed)


def reduce_kernel(counts, *refs):
    (len_ref, dn_ref, qkv_hbm, o_hbm, lse_hbm, xhat_ref, r_ref, w_hbm, wo_ref, gain_ref) = refs[:10]
    (contract, cross_first, cross_second) = refs[15:18]
    ffn_refs = (refs[18:22], refs[22:26])
    (ssum_ref, fsum_ref, esum_ref, csum_ref, csent_ref) = refs[26:31]
    refs = (*refs[:30], *refs[31:])
    (dres_ref, in_ref, out_ref, expand_ref, contract_ref, cross_ref, vsum_ref, landed) = refs[30:38]
    (dqkv_ref, dt_ref, do_ref, dq_ref, sums_ref, made, own, r0, r1, r2, r3, vbuf, vrecv) = refs[38:51]
    (n0_buf, n1_buf, da0_buf, da1_buf) = refs[51:55]
    held = refs[55:64]
    (qkv_ref, o_ref, lse_ref, wqkv_ref, x0_ref, x_ref, dqkv0_ref, o0_ref, dt0_ref) = held
    send_sem, recv_sem, local_sem, vsend_sem, vrecv_sem, xsend_sem, xrecv_sem, fetch_sem, held_sem = refs[64:]
    copies = incoming((qkv_hbm, o_hbm, lse_hbm, w_hbm, *refs[10:15]), held, held_sem)
    for copy in copies[:3]:
        copy.start()
    d = dn_ref.shape[1]
    n_ffn, n_in, n_out, n_cross = 2 * counts[0], counts[1], counts[2], counts[3]
    blocks = n_ffn + n_in + n_out + n_cross
    rows, width = own.shape[-2:]
    second = lax.axis_index("section") == 1
    me = lax.axis_index("dp")
    c, y, zl, zh = me % 2, (me // 2) % 2, (me // 4) % 2, me // 8
    mates = (me + 1 - 2 * c, me + 2 - 4 * y, me + 4 - 8 * zl, me + 8 - 16 * zh)
    barrier = pltpu.get_barrier_semaphore()
    for mate in mates:
        pl.semaphore_signal(barrier, inc=1, device_id={"dp": mate}, device_id_type=MESH)
    across = 1 - lax.axis_index("section")
    pl.semaphore_signal(barrier, inc=1, device_id={"section": across}, device_id_type=MESH)

    def chosen(visit):
        for which, here in enumerate((jnp.logical_not(second), second)):

            @pl.when(here)
            def _():
                visit(ffn_refs[which])

    def fetch_norms(from_refs):
        return [
            pltpu.make_async_copy(from_refs[k], (n0_buf, n1_buf)[k], fetch_sem.at[2, k]) for k in range(2)
        ]

    def fetch_columns(from_refs, i):
        at = pl.ds(pl.multiple_of(i * d, 128), d)
        return [
            pltpu.make_async_copy(
                from_refs[2 + k].at[:, at], (da0_buf, da1_buf)[k].at[i % 2], fetch_sem.at[i % 2, k]
            )
            for k in range(2)
        ]

    def begin_fetch(from_refs):
        for copy in fetch_norms(from_refs) + fetch_columns(from_refs, 0) + fetch_columns(from_refs, 1):
            copy.start()

    chosen(begin_fetch)
    for copy in copies[3:]:
        copy.start()
    pl.semaphore_wait(barrier, 5)

    def over(j):
        return pltpu.make_async_remote_copy(
            src_ref=cross_first.at[j],
            dst_ref=landed.at[j],
            send_sem=xsend_sem.at[j],
            recv_sem=xrecv_sem.at[j],
            device_id={"section": across},
            device_id_type=MESH,
        )

    @pl.when(second)
    def _():
        for j in (*range(n_cross // 2, n_cross), *range(n_cross // 2)):
            over(j).start()

    order = ((0, 1, 2, 3), (0, 2, 3, 1))

    def remote(src, dst, stage, b, color):
        return pltpu.make_async_remote_copy(
            src_ref=src,
            dst_ref=dst,
            send_sem=send_sem.at[stage, b],
            recv_sem=recv_sem.at[stage, b],
            device_id={"dp": mates[order[color][stage]]},
            device_id_type=MESH,
        )

    turned = blocks // 7
    half = turned // 2
    steps = blocks - turned
    gap = 3
    early = counts[0] - half

    def slot(b, color):
        if color == 0:
            return (b - jnp.where(b >= early, half, 0)) % RING
        return RING + jnp.where(b < steps, b - early, b - steps)

    def first_copy(part, at, b, color):
        return remote(part.at[at, :, :, :, 1 - c], r0.at[slot(b, color)], 0, b, color)

    def local_copy(part, at, b):
        return pltpu.make_async_copy(part.at[at, :, :, :, c], own.at[b], local_sem.at[b])

    def copy_of(stage, b, color):
        if color == 0:
            src = (own.at[b, :, :, 1 - y], own.at[b, :, 1 - zl, y], own.at[b, 1 - zh, zl, y])
        else:
            src = (own.at[b, :, 1 - zl], own.at[b, 1 - zh, zl], own.at[b, zh, zl, 1 - y])
        return remote(src[stage - 1], (r1, r2, r3)[stage - 1].at[b], stage, b, color)

    def add(left, right):
        return (left.astype(F32) + right.astype(F32)).astype(BF)

    def column(at):
        return pl.ds(pl.multiple_of(at * width, 128), width)

    def put_columns(ref, at, value):
        ref[:, column(at)] = value

    def put_groups(ref, at, value):
        ref[pl.ds(pl.multiple_of((at // 2) * rows, 8), rows), column(at % 2)] = value

    plan = (
        (((contract, None),), counts[0], put_groups, contract_ref),
        (((made, None),), counts[0], put_columns, expand_ref),
        (((made, None),), n_in, put_columns, in_ref),
        (((made, None),), n_out, put_columns, out_ref),
        (((landed, jnp.logical_not(second)), (cross_second, second)), n_cross, put_groups, cross_ref),
    )

    def each(b, visit):
        low = 0
        for sources, count, put, target in plan:
            inside = (b >= low) & (b < low + count)
            at = b % counts[0] if sources[0][0] is made else b - low
            visit(inside, sources, at, put, target, b - low)
            low += count

    def settle(stage, b, color):
        if stage == 0:
            first_copy(contract, 0, b, color).wait()
            local_copy(contract, 0, b).wait()
            own[b] = add(own[b], r0[slot(b, color)])
            return
        copy_of(stage, b, color).wait()
        if stage == 1:
            if color == 0:
                own[b, :, :, y] = add(own[b, :, :, y], r1[b])
            else:
                own[b, :, zl] = add(own[b, :, zl], r1[b])
        elif stage == 2:
            if color == 0:
                own[b, :, zl, y] = add(own[b, :, zl, y], r2[b])
            else:
                own[b, zh, zl] = add(own[b, zh, zl], r2[b])
        else:
            total = own[b, zh, zl, y].astype(F32) + r3[b].astype(F32)

            def finish(inside, sources, at, put, target, place):
                @pl.when(inside)
                def _():
                    put(target, place, total)

            each(b, finish)

    def vcopy(j):
        return pltpu.make_async_remote_copy(
            src_ref=vbuf.at[j],
            dst_ref=vrecv.at[j],
            send_sem=vsend_sem.at[j],
            recv_sem=vrecv_sem.at[j],
            device_id={"dp": mates[j]},
            device_id_type=MESH,
        )

    def advance(stage, b, color):
        if stage == 0:

            def launch(inside, sources, at, put, target, place):
                for part, here in sources:

                    @pl.when(inside if here is None else inside & here)
                    def _():
                        if part is landed:
                            over(at).wait_recv()
                        first_copy(part, at, b, color).start()
                        local_copy(part, at, b).start()

            each(b, launch)
            return
        settle(stage - 1, b, color)
        if stage < 4:
            copy_of(stage, b, color).start()

    def step(it, _):
        for stage in range(5):
            at = it - LAG * stage

            @pl.when((at >= 0) & (at < steps))
            def _():
                advance(stage, at + jnp.where(at >= early, half, 0), 0)

            @pl.when((at >= 0) & (at < turned * gap) & (at % gap == 1))
            def _():
                j = at // gap
                advance(stage, jnp.where(j < half, early, steps) + j, 1)

        return 0

    def some(low, high):
        lax.fori_loop(low, high, step, 0)

    def keep(block, total):
        for h in range(2):
            made[block + h] = total[:, h * width : (h + 1) * width].reshape(made.shape[1:]).astype(BF)

    pairs, chunks = d // 128, counts[0] // 2

    def beside(p):
        @pl.when(p < chunks)
        def _():
            @pl.when(p == 0)
            def _():
                for copy in fetch_norms(ffn_refs[0]):
                    copy.wait()

            for copy in fetch_columns(ffn_refs[0], p):
                copy.wait()
            keep(
                2 * p,
                dot_tn(n0_buf[...].astype(BF), da0_buf[p % 2]) + dot_tn(n1_buf[...].astype(BF), da1_buf[p % 2]),
            )

            def next_fetch(from_refs):
                for copy in fetch_columns(from_refs, p + 2):
                    copy.start()

            @pl.when(p + 2 < chunks)
            def _():
                chosen(next_fetch)

        some(jnp.minimum(3 + 2 * p, 7 + p), jnp.minimum(5 + 2 * p, 8 + p))

    def ready(stage):
        for copy in (copies[:3], copies[3:], ())[stage]:
            copy.wait()

    some(0, 3)
    attn_bwd_body(
        True, beside, ready,
        len_ref, dn_ref, qkv_ref, o_ref, lse_ref, xhat_ref, r_ref, wqkv_ref, wo_ref, gain_ref,
        dres_ref, dqkv_ref, dt_ref, None, sums_ref, do_ref, dq_ref,
    )
    after = 7 + pairs
    vbuf[0, 0:4] = sums_ref[0:4, :] + ssum_ref[0:4, :]
    vbuf[0, 4:6] = fsum_ref[0:2, :]
    vbuf[0, 6:7] = sums_ref[4:5, :] + ssum_ref[4:5, :]
    vbuf[0, 7:8] = fsum_ref[2:3, :]
    count = esum_ref.shape[1] // d
    for j in range(count):
        vbuf[0, 8 + j : 9 + j] = esum_ref[:, j * d : (j + 1) * d]
    vbuf[0, 8 + count : 13 + count] = jnp.where(second, csum_ref[0:5, :], csent_ref[0:5, :])
    vbuf[0, 13 + count :] = jnp.zeros((vbuf.shape[1] - 13 - count, d), F32)
    def weight(i, _):
        at = pl.ds(pl.multiple_of(i * d, 128), d)
        keep(2 * i, dot_tn(x0_ref[...], dqkv0_ref[:, at]) + dot_tn(x_ref[...], dqkv_ref[:, at]))
        step(after + i, 0)
        return 0

    lax.fori_loop(0, n_in // 2, weight, 0)
    keep(n_in, dot_tn(o0_ref[...], dt0_ref[...]) + dot_tn(o_ref[...], dt_ref[...]))
    begin = after + n_in // 2
    vcopy(0).start()

    def rest(it, _):
        step(it, 0)
        for j in range(4):

            @pl.when(it == begin + LAG * (j + 1))
            def _():
                vcopy(j).wait()
                vbuf[j + 1] = vbuf[j] + vrecv[j]
                if j < 3:
                    vcopy(j + 1).start()

        return 0

    lax.fori_loop(begin, steps + 4 * LAG, rest, 0)
    vsum_ref[...] = vbuf[4]

    @pl.when(second)
    def _():
        for j in range(n_cross):
            over(j).wait_send()


def reduce_scatter(length, dn, saved, w_in, w_out, gain, x0, x1, dqkv0, o0, dt0, parts, encoder, decoder, sums):
    s, d = dn.shape
    rows, width = parts[0].shape[-2:]
    n_in, n_out = dqkv0.shape[1] // width, dt0.shape[1] // width
    counts = (parts[0].shape[0], n_in, n_out, parts[1].shape[0])
    blocks = 2 * counts[0] + sum(counts[1:])
    parts = [part.reshape(part.shape[0], 2, 2, 2, 2, rows, width) for part in parts]
    short = x0.shape[0]
    vec = (24, d)
    vm = pl.BlockSpec(memory_space=pltpu.VMEM)
    sm = pl.BlockSpec(memory_space=pltpu.SMEM)
    hbm = pl.BlockSpec(memory_space=pl.ANY)
    shapes = ((s, d), (rows, n_in * width), (rows, n_out * width), (rows, counts[0] * width),
              (counts[0] // 2 * rows, d), (counts[3] // 2 * rows, d), vec)
    return pl.pallas_call(
        functools.partial(reduce_kernel, counts),
        out_shape=(*(jax.ShapeDtypeStruct(shape, F32) for shape in shapes), jax.ShapeDtypeStruct(parts[1].shape, BF)),
        in_specs=[sm, vm, hbm, hbm, hbm, vm, vm, hbm, vm, vm] + [hbm] * 16 + [vm] * 5,
        out_specs=(*(vm,) * 7, hbm),
        scratch_shapes=[
            pltpu.VMEM((s, 3 * d), BF),
            pltpu.VMEM((s, d), BF),
            pltpu.VMEM((s, d), BF),
            pltpu.VMEM((128, s), F32),
            pltpu.VMEM((8, d), F32),
            pltpu.VMEM((counts[0], 2, 2, 2, 2, rows, width), BF),
            pltpu.VMEM((blocks, 2, 2, 2, rows, width), BF),
            pltpu.VMEM((RING + blocks // 7, 2, 2, 2, rows, width), BF),
            pltpu.VMEM((blocks, 2, 2, rows, width), BF),
            pltpu.VMEM((blocks, 2, rows, width), BF),
            pltpu.VMEM((blocks, rows, width), BF),
            pltpu.VMEM((5, *vec), F32),
            pltpu.VMEM((4, *vec), F32),
            pltpu.VMEM((short, d), F32),
            pltpu.VMEM((s, d), F32),
            pltpu.VMEM((2, short, d), BF),
            pltpu.VMEM((2, s, d), BF),
            pltpu.VMEM((s, 3 * d), BF),
            pltpu.VMEM((s, d), BF),
            pltpu.VMEM((s, d), F32),
            pltpu.VMEM((d, 3 * d), BF),
            pltpu.VMEM((short, d), BF),
            pltpu.VMEM((s, d), BF),
            pltpu.VMEM((short, 3 * d), BF),
            pltpu.VMEM((short, d), BF),
            pltpu.VMEM((short, d), BF),
            pltpu.SemaphoreType.DMA((4, blocks)),
            pltpu.SemaphoreType.DMA((4, blocks)),
            pltpu.SemaphoreType.DMA((blocks,)),
            pltpu.SemaphoreType.DMA((4,)),
            pltpu.SemaphoreType.DMA((4,)),
            pltpu.SemaphoreType.DMA((counts[3],)),
            pltpu.SemaphoreType.DMA((counts[3],)),
            pltpu.SemaphoreType.DMA((3, 2)),
            pltpu.SemaphoreType.DMA((9,)),
        ],
        compiler_params=pltpu.CompilerParams(collective_id=0, has_side_effects=True, vmem_limit_bytes=67043328),
    )(length.reshape(1, 1), dn, *saved, w_in, w_out, gain, x0, x1, dqkv0, o0, dt0, *parts, *encoder, *decoder, *sums)[:7]


def shards(
    inputs_long,
    inputs_short,
    cotangent_long,
    cotangent_short,
    lengths_long,
    lengths_short,
    self_in_weight,
    self_out_weight,
    expand_weight,
    contract_weight,
    expand_bias,
    layer_biases,
    layer_gains,
    cross_weight,
    cross_biases,
    cross_gain,
):
    decoder = lax.axis_index("section") == 1
    d = inputs_long.shape[-1]
    ff = expand_weight.shape[2]
    w_in, w_out, w_e, w_c = self_in_weight[0], self_out_weight[0], expand_weight[0], contract_weight[0]
    b_e, bias, gain = expand_bias[0], layer_biases[0], layer_gains[0]
    c_gain = cross_gain.reshape(1, d)

    xs = (inputs_short[0, 0], inputs_long[0, 0])
    cots = (cotangent_short[0, 0], cotangent_long[0, 0])
    source = (lengths_short[0, 0], lengths_long[0, 0])
    target = (lengths_short[1, 0], lengths_long[1, 0])
    sizes = tuple(x.shape[0] for x in xs)

    own = tuple(jnp.where(decoder, t, o) for t, o in zip(target, source))

    def attend(i):
        x = xs[i]
        return attn_fwd(x, None, x, w_in, w_out, bias, gain, own[i])

    def encode_ffn(i, n):
        s = sizes[i]

        def decode():
            return blank(((s, d), BF), ((s, ff), BF), ((s, ff), BF), ((s, d), F32), ((s, 128), F32))

        return lax.cond(decoder, decode, lambda: ffn_fwd(n, w_e, w_c, b_e, bias, gain))

    def send(value, steps):
        return lax.ppermute(value, "section", [(0, 1)] if steps > 0 else [(1, 0)])

    def cross(i, memory, n1):
        s = sizes[i]

        def encode():
            return blank(
                ((s, 3 * d), BF), ((s, d), BF), ((s, d), F32), ((s, d), F32), ((s, 128), F32), ((s, d), F32)
            )

        def decode():
            return attn_fwd(n1, memory, n1, cross_weight, None, cross_biases, c_gain, source[i])

        return lax.cond(decoder, decode, encode)

    def turn(i, out):
        s = sizes[i]

        def decode():
            y, g, gp, xhat, r = ffn_fwd(out[5], w_e, w_c, b_e, bias, gain)
            fb = ffn_bwd(cots[i], None, target[i], (gp, xhat, r), w_e, w_c, gain)
            ab = attn_bwd(fb[0], out[:5], cross_weight, None, c_gain, source[i], False)
            return (g, fb[1], fb[2], ab[1], ab[2]), ab[0], ab[3], y, (fb[3], fb[4], ab[4])

        def encode():
            out = blank(
                ((s, ff), BF),
                ((s, ff), BF),
                ((s, d), BF),
                ((s, 3 * d), BF),
                ((s, d), BF),
                ((s, d), F32),
                ((s, d), BF),
                ((s, d), BF),
                ((8, d), F32),
                ((1, ff), F32),
                ((8, d), F32),
            )
            return tuple(out[:5]), out[5], out[6], out[7], tuple(out[8:])

        return lax.cond(decoder, decode, encode)

    att0 = attend(0)
    ffn0 = encode_ffn(0, att0[5])
    mem0 = send(ffn0[0], 1)
    x_long, _ = lax.optimization_barrier((xs[1], ffn0[0]))
    xs = (xs[0], x_long)
    att1 = attend(1)
    n_long, mem0 = lax.optimization_barrier((att1[5], mem0))
    ffn1 = encode_ffn(1, n_long)
    mem1 = send(ffn1[0], 1)
    n_short, _ = lax.optimization_barrier((att0[5], ffn1[0]))
    out0 = cross(0, mem0, n_short)
    keep0, dn0, dm0, y0, sums0 = turn(0, out0)
    back0 = send(dm0, -1)
    n_long, _ = lax.optimization_barrier((att1[5], dm0))
    out1 = cross(1, mem1, n_long)
    n_long, back0 = lax.optimization_barrier((out1[5], back0))
    out1 = (*out1[:5], n_long)
    keep1, dn1, dm1, y1, sums1 = turn(1, out1)
    back1 = send(dm1, -1)
    dp = lax.axis_size("dp")
    staged = dp == 16 and d % (16 * dp) == 0 and d == 6 * 128 and ff == 4 * d

    def cross_grads():
        n1, mem = (att0[5], att1[5]), (mem0, mem1)
        dqkv, dt = ((keep0[j], keep1[j]) for j in (3, 4))
        mixed = (out0[1], out1[1])
        if staged:
            return wgrad_cross(dqkv, dt, n1, mem, mixed, dp)
        joint = jnp.concatenate(dqkv, 0)
        low = jnp.concatenate(n1, 0).astype(BF)
        mem = jnp.concatenate(mem, 0)
        rows = (
            dot_tn(joint[:, :d], low),
            dot_tn(joint[:, d : 2 * d], mem),
            dot_tn(joint[:, 2 * d :], mem),
            dot_tn(jnp.concatenate(dt, 0), jnp.concatenate(mixed, 0)),
        )
        return tuple(jnp.concatenate(rows[j : j + 2], 0).astype(BF) for j in (0, 2))

    def cross_blank():
        shape = (4, dp, d // dp, d // 2) if staged else (2 * d, d)
        return tuple(blank((shape, BF), (shape, BF)))

    cross_sums = sums0[2] + sums1[2]
    cross_first, cross_second = lax.cond(decoder, cross_grads, cross_blank)
    back0, _ = lax.optimization_barrier((back0, cross_first))
    dn0, *enc0 = lax.cond(
        decoder,
        lambda: (dn0, *blank(((sizes[0], ff), BF), ((sizes[0], d), BF), ((8, d), F32), ((1, ff), F32))),
        lambda: tuple(ffn_bwd(cots[0], back0, source[0], ffn0[2:], w_e, w_c, gain)),
    )
    self0 = attn_bwd(dn0, att0[:5], w_in, w_out, gain, own[0], True)
    cross_sent = send(cross_sums, -1)
    back1, _ = lax.optimization_barrier((back1, self0[0]))

    def plain(left, right):
        left, right = (jnp.concatenate([e.astype(BF) for e in side], 0) for side in (left, right))
        return dot_tn(left, right).astype(BF)

    def contract_grad(g, dt):
        return wgrad_rows(g, dt, dp) if staged else plain(g, dt)

    def decode_last():
        grad = contract_grad((keep0[0], keep1[0]), (keep0[2], keep1[2]))
        return dn1, *blank(((sizes[1], ff), BF)), grad, sums0[0] + sums1[0], sums0[1] + sums1[1]

    def encode_last():
        dn, da, dt, sums, sum_e = ffn_bwd(cots[1], back1, source[1], ffn1[2:], w_e, w_c, gain)
        return dn, da, contract_grad((ffn0[1], ffn1[1]), (enc0[1], dt)), enc0[2] + sums, enc0[3] + sum_e

    dn1, enc_da, g_contract, ffn_sums, sum_e = lax.cond(decoder, decode_last, encode_last)
    if staged:
        dx1, *big, rows = reduce_scatter(
            own[1], dn1, att1[:5], w_in, w_out, gain, xs[0], xs[1], self0[1], att0[1], self0[2],
            (g_contract, cross_first, cross_second),
            (att0[5], att1[5], enc0[0], enc_da),
            (out0[5], out1[5], keep0[1], keep1[1]),
            (self0[4], ffn_sums, sum_e, cross_sums, cross_sent),
        )
    else:
        self1 = attn_bwd(dn1, att1[:5], w_in, w_out, gain, own[1], True)
        dx1 = self1[0]
        self_sums = self0[4] + self1[4]
        cross_rows = jnp.where(decoder, cross_sums, cross_sent)
        rows = [self_sums[0:4], ffn_sums[0:2], self_sums[4:5], ffn_sums[2:3], sum_e.reshape(ff // d, d), cross_rows[0:5]]
        rows = lax.psum(jnp.concatenate(rows, 0), "dp")
        cross_mine = jnp.where(decoder, cross_second, send(cross_first, -1))
        pairs = (((att0[5], enc0[0]), (att1[5], enc_da)), ((out0[5], keep0[1]), (out1[5], keep1[1])))
        g_expand = lax.cond(decoder, lambda: plain(*zip(*pairs[1])), lambda: plain(*zip(*pairs[0])))
        in_grad = plain(xs, (self0[1], self1[1]))
        out_grad = plain((att0[1], att1[1]), (self0[2], self1[2]))
        big = [
            lax.psum_scatter(part, "dp", scatter_dimension=0, tiled=True).astype(F32)
            for part in (in_grad, out_grad, g_expand, g_contract, cross_mine)
        ]
    count = 8 + ff // d
    me = lax.axis_index("dp")
    piece = lax.dynamic_slice_in_dim(rows[:8], me * (d // dp), d // dp, 1)
    e_piece = lax.dynamic_slice_in_dim(rows[8:count].reshape(1, ff), me * (ff // dp), ff // dp, 1)
    outs = [jnp.where(decoder, y, e)[None, None] for y, e in ((y0, ffn0[0]), (y1, ffn1[0]))]
    return (
        outs[1],
        outs[0],
        dx1[None, None],
        self0[0][None, None],
        big[0][None],
        big[1][None],
        big[2][None],
        big[3][None],
        e_piece,
        piece[None, :6],
        piece[None, 6:8],
        big[4].T,
        rows[count : count + 4],
        rows[count + 4],
    )


def solution(mesh):
    in_specs = (
        P("section", "dp", None, None),
        P("section", "dp", None, None),
        P("section", "dp", None, None),
        P("section", "dp", None, None),
        P(None, "dp"),
        P(None, "dp"),
        P("section", None, None),
        P("section", None, None),
        P("section", None, None),
        P("section", None, None),
        P("section", None),
        P("section", None, None),
        P("section", None, None),
        P(),
        P(),
        P(),
    )
    out_specs = (
        P("section", "dp", None, None),
        P("section", "dp", None, None),
        P("section", "dp", None, None),
        P("section", "dp", None, None),
        P("section", "dp", None),
        P("section", "dp", None),
        P("section", "dp", None),
        P("section", "dp", None),
        P("section", "dp"),
        P("section", None, "dp"),
        P("section", None, "dp"),
        P(None, ("section", "dp")),
        P(),
        P(),
    )
    return jax.shard_map(shards, mesh=mesh, in_specs=in_specs, out_specs=out_specs, check_vma=False)
```
